32 devices in a mesh: dp: 32 (over z, y, x, core).
Axes of the slice: x: 2, y: 2, z: 4, core: 2. Of those that a mesh axis runs over, the one named last changes fastest.
Arguments:
- tokens: bfloat16 [64, 512, 1024], P('dp'), may hold values from -6 to 6
- lengths: int32 [64, 16], P('dp'), may hold values from 1 to 64, 512 in all within a row
- w_query: float32 [2, 1024, 1024], P(None, 'dp'), may hold values from -0.1875 to 0.1875
- w_key: float32 [2, 1024, 1024], P(None, 'dp'), may hold values from -0.1875 to 0.1875
- w_value: float32 [2, 1024, 1024], P(None, 'dp'), may hold values from -0.1875 to 0.1875
- w_out: float32 [2, 1024, 1024], P(None, 'dp'), may hold values from -0.75 to 0.75
- w_inner: float32 [2, 1024, 4096], P(None, 'dp'), may hold values from -0.1875 to 0.1875
- w_outer: float32 [2, 4096, 1024], P(None, 'dp'), may hold values from -0.09375 to 0.09375
- bias_query: float32 [2, 1024], replicated, may hold values from -3 to 3
- bias_value: float32 [2, 1024], replicated, may hold values from -3 to 3
- bias_out: float32 [2, 1024], replicated, may hold values from -3 to 3
- bias_inner: float32 [2, 4096], replicated, may hold values from -3 to 3
- bias_outer: float32 [2, 1024], replicated, may hold values from -3 to 3
- shift_attn: float32 [2, 1024], replicated, may hold values from -3 to 3
- shift_ffn: float32 [2, 1024], replicated, may hold values from -3 to 3
- gain_attn: float32 [2, 1024], replicated, may hold values from 0.1 to 1.9
- gain_ffn: float32 [2, 1024], replicated, may hold values from 0.1 to 1.9
- cotangent: bfloat16 [64, 512, 1024], P('dp'), may hold values from -6 to 6
Outputs:
- output: bfloat16 [64, 512, 1024], P('dp')
- grad_tokens: float32 [64, 512, 1024], P('dp')
- grad_bias_query: float32 [2, 1024], replicated
- grad_bias_value: float32 [2, 1024], replicated
- grad_bias_out: float32 [2, 1024], replicated
- grad_bias_inner: float32 [2, 4096], replicated
- grad_bias_outer: float32 [2, 1024], replicated
- grad_shift_attn: float32 [2, 1024], replicated
- grad_shift_ffn: float32 [2, 1024], replicated
The draws below stay inside these ranges and needn't reach their ends.
Inputs may be any that keep to these rules, and one draw needn't show every extreme that they name: In each row the 16 entries sum to 512: the first 15 are sentence lengths in slot order, the last counts padding slots at the row's end; the largest entry of each row is 64.
All inputs are finite; a program needn't handle non-finite values.
Results may differ from the reference program's by a relative error of at most 0.019.
Values may be sent and summed in bfloat16 or wider, within the bound.
A program may use at most 320 MiB of HBM per device.

```python
import math
import jax
import jax.numpy as jnp
import numpy as np
from jax import lax

D = 1024
HEADS = 16
HEAD_DIM = 64
FF = 4096
LAYERS = 2
SLOTS = 512
NSEG = 16
SENT_MAX = 64
ROWS = 64


def steps_of(key, extent, cuts, smallest, largest):
    loudness = 1.0
    for axis_at, blocks in cuts:
        draws = jax.random.uniform(jax.random.fold_in(jax.random.fold_in(key, 6), axis_at), (blocks,), jnp.float32, smallest / len(cuts), largest / len(cuts))
        loudness = loudness * jnp.repeat(jnp.exp(draws), extent[axis_at] // blocks).reshape((-1,) + (1,) * (len(extent) - 1 - axis_at))
    return loudness


def profile(number_of, total, most, lean):
    loads = [(1 << 20) // math.isqrt(standing ** lean) + 1 for standing in range(2, number_of + 1)]
    spare, holding = total - most - (number_of - 1), [1] * (number_of - 1)
    while spare > 0:
        movable = [i for i in range(number_of - 1) if holding[i] < most]
        whole, remaining = sum([loads[i] for i in movable]), spare
        for i in movable:
            addition = min(most - holding[i], max(1, remaining * loads[i] // whole), spare)
            holding[i] = holding[i] + addition
            spare = spare - addition
    return np.array([most] + holding)


def uneven_parts(stream_key, count, total, reach, slope):
    if count == 2:
        one = jax.random.randint(stream_key, (), max(1, total - reach), min(reach, total - 1) + 1)
        return jnp.stack([one, total - one])
    sizes = jnp.asarray(profile(count, total, reach, slope), jnp.int32)
    pairs = (count - 1) // 2
    giver, taker = sizes[1:1 + 2 * pairs:2], sizes[2:2 + 2 * pairs:2]
    margin = jnp.minimum(giver - 1, reach - taker)
    moved = jax.random.randint(jax.random.fold_in(stream_key, 1), (pairs,), 0, 1 << 20) % (margin + 1)
    sizes = sizes.at[1:1 + 2 * pairs:2].set(giver - moved).at[2:2 + 2 * pairs:2].set(taker + moved)
    return sizes[jax.random.permutation(jax.random.fold_in(stream_key, 2), count)]


def normal_values(own_key, dims, scale, reach, pieces=(), kind=jnp.bfloat16):
    values = jax.random.normal(own_key, dims, jnp.float32) * scale
    if len(pieces) > 0:
        values = steps_of(own_key, dims, pieces, -0.22, 0.18) * values
    return jnp.clip(values, min=-reach, max=reach).astype(kind)


def setup_inputs(seed: int = 0) -> dict:
    splits = jax.random.split(jax.random.key(seed), 19)
    return {
        "tokens": normal_values(splits[0], (ROWS, SLOTS, D), 1.0, 6.0, ((0, 32),)),
        "lengths": jax.vmap(lambda own: uneven_parts(own, NSEG, SLOTS, SENT_MAX, 1))(jax.random.split(splits[1], ROWS)).reshape((ROWS, NSEG)).astype(jnp.int32),
        "w_query": normal_values(splits[2], (LAYERS, D, D), D ** -0.5, 0.1875, ((1, 32),), jnp.float32),
        "w_key": normal_values(splits[3], (LAYERS, D, D), D ** -0.5, 0.1875, ((1, 32),), jnp.float32),
        "w_value": normal_values(splits[4], (LAYERS, D, D), D ** -0.5, 0.1875, ((1, 32),), jnp.float32),
        "w_out": normal_values(splits[5], (LAYERS, D, D), (D // 16) ** -0.5, 0.75, ((1, 32),), jnp.float32),
        "w_inner": normal_values(splits[6], (LAYERS, D, FF), D ** -0.5, 0.1875, ((1, 32),), jnp.float32),
        "w_outer": normal_values(splits[7], (LAYERS, FF, D), FF ** -0.5, 0.09375, ((1, 32),), jnp.float32),
        "bias_query": normal_values(splits[8], (LAYERS, D), 0.5, 3.0, (), jnp.float32),
        "bias_value": normal_values(splits[9], (LAYERS, D), 0.5, 3.0, (), jnp.float32),
        "bias_out": normal_values(splits[10], (LAYERS, D), 0.5, 3.0, (), jnp.float32),
        "bias_inner": normal_values(splits[11], (LAYERS, FF), 0.5, 3.0, (), jnp.float32),
        "bias_outer": normal_values(splits[12], (LAYERS, D), 0.5, 3.0, (), jnp.float32),
        "shift_attn": normal_values(splits[13], (LAYERS, D), 0.5, 3.0, (), jnp.float32),
        "shift_ffn": normal_values(splits[14], (LAYERS, D), 0.5, 3.0, (), jnp.float32),
        "gain_attn": jnp.clip(1.0 + 0.18 * jax.random.normal(splits[15], (LAYERS, D), jnp.float32), 0.1, 1.9),
        "gain_ffn": jnp.clip(1.0 + 0.18 * jax.random.normal(splits[16], (LAYERS, D), jnp.float32), 0.1, 1.9),
        "cotangent": normal_values(splits[17], (ROWS, SLOTS, D), 1.0, 6.0, ((0, 32),)),
    }


@jax.custom_vjp
def low(v):
    return lax.optimization_barrier(v.astype(jnp.bfloat16)).astype(jnp.float32)

@jax.custom_vjp
def low_back(v):
    return v

def low_keep(v):
    return (low(v), None)

def low_pass(kept, grad):
    return (grad,)

def back_keep(v):
    return (v, None)

def back_low(kept, grad):
    return (low(grad),)
low.defvjp(low_keep, low_pass)
low_back.defvjp(back_keep, back_low)
EPSILON = 1e-12
NEGATIVE = -1000000000.0

def product(left, right):
    return jnp.dot(left, right, precision=lax.Precision.HIGHEST, preferred_element_type=jnp.float32)

def layer_norm(residual, gain_row, shift_row):
    average = lax.optimization_barrier(jnp.mean(residual, axis=-1, keepdims=True))
    centered = residual - average
    variance = lax.optimization_barrier(jnp.mean(centered * centered, axis=-1, keepdims=True))
    return centered * lax.rsqrt(variance + EPSILON) * gain_row + shift_row

def sentence_numbers(lengths, slot_count):
    sentence_ends = jnp.cumsum(lengths, axis=-1).astype(jnp.int32)
    position = jnp.arange(slot_count, dtype=jnp.int32)
    return lax.optimization_barrier(jnp.sum((position[None, :, None] >= sentence_ends[:, None, :]).astype(jnp.int32), axis=-1)).astype(jnp.int32)

def allowed_pairs(numbers, count):
    same = numbers[:, :, None] == numbers[:, None, :]
    key_real = numbers[:, None, :] < count - 1
    position = jnp.arange(numbers.shape[1], dtype=jnp.int32)
    diagonal = (position[:, None] == position[None, :])[None]
    return same & key_real | diagonal

def attend_row(query_rows, key_rows, value_rows, allowed):
    score_scale = HEAD_DIM ** (-0.5)
    scores = jnp.einsum('qhd,khd->hqk', query_rows, key_rows, precision=lax.Precision.HIGHEST) * score_scale
    scores = jnp.where(allowed[None], scores, NEGATIVE)
    scores = low_back(scores)
    row_max = lax.optimization_barrier(jnp.max(scores, axis=-1, keepdims=True))
    exponents = jnp.exp(scores - row_max)
    probabilities = low(exponents / lax.optimization_barrier(jnp.sum(exponents, axis=-1, keepdims=True)))
    attended = jnp.einsum('hqk,khd->qhd', probabilities, value_rows, precision=lax.Precision.HIGHEST)
    return attended.reshape(attended.shape[0], HEADS * HEAD_DIM)

def layer_forward(hidden, allowed, matrices, parameters, gain_attn, gain_ffn):
    weight_query, weight_key, weight_value, weight_out, weight_inner, weight_outer = matrices
    bias_query, bias_value, bias_out, bias_inner, bias_outer, shift_attn, shift_ffn = parameters
    row_count = hidden.shape[0]
    flat_rows = hidden.reshape(row_count * SLOTS, D)
    active = low(flat_rows)
    query_rows = low_back(low(product(active, weight_query) + bias_query))
    key_rows = low_back(low(product(active, weight_key)))
    value_rows = low_back(low(product(active, weight_value) + bias_value))
    split = (row_count, SLOTS, HEADS, HEAD_DIM)
    checked_attend = jax.checkpoint(attend_row)
    attended = lax.map(lambda row_item: checked_attend(*row_item), (query_rows.reshape(split), key_rows.reshape(split), value_rows.reshape(split), allowed))
    mixed_rows = low_back(low(attended.reshape(row_count * SLOTS, D)))
    branch = low_back(product(mixed_rows, weight_out) + bias_out)
    normed = layer_norm(flat_rows + branch, gain_attn, shift_attn)
    inner_pre = low_back(product(low(normed), weight_inner) + bias_inner)
    activated = low(jax.nn.gelu(inner_pre, approximate=False))
    outer_out = low_back(product(activated, weight_outer) + bias_outer)
    result = layer_norm(normed + outer_out, gain_ffn, shift_ffn)
    return result.reshape(row_count, SLOTS, D)

def reference(tokens, lengths, w_query, w_key, w_value, w_out, w_inner, w_outer, bias_query, bias_value, bias_out, bias_inner, bias_outer, shift_attn, shift_ffn, gain_attn, gain_ffn, cotangent):
    numbers = sentence_numbers(lengths, SLOTS)
    allowed = allowed_pairs(numbers, NSEG)
    is_real = (numbers < NSEG - 1).astype(jnp.float32)
    layer_matrices = [tuple((low(matrix[layer_index]) for matrix in (w_query, w_key, w_value, w_out, w_inner, w_outer))) for layer_index in range(LAYERS)]

    def forward(hidden, trainable):
        for layer_index in range(LAYERS):
            hidden = layer_forward(hidden, allowed, layer_matrices[layer_index], tuple((parameter[layer_index] for parameter in trainable)), gain_attn[layer_index], gain_ffn[layer_index])
        return hidden
    trainable = (bias_query, bias_value, bias_out, bias_inner, bias_outer, shift_attn, shift_ffn)
    result, pullback = jax.vjp(forward, tokens.astype(jnp.float32), trainable)
    grad_tokens, bias_grads = pullback(cotangent.astype(jnp.float32) * is_real[:, :, None])
    return (result.astype(jnp.bfloat16), grad_tokens, bias_grads[0], bias_grads[1], bias_grads[2], bias_grads[3], bias_grads[4], bias_grads[5], bias_grads[6])
```

```python
import functools

import jax
import jax.numpy as jnp
from jax import lax
from jax.experimental import pallas as pl
from jax.experimental.pallas import tpu as pltpu
from jax.sharding import PartitionSpec as P

HEADS = 16
LAYERS = 2
EPSILON = 1e-12
NEGATIVE = -1e9
PADDING_ID = 1000
MESH = pl.DeviceIdType.MESH
HBM = pltpu.MemorySpace.HBM
VMEM = pltpu.VMEM
DMA = pltpu.SemaphoreType.DMA

WIDTH = 512
GROUPS = 24
AT_OUT, AT_INNER, AT_OUTER = 6, 8, 16
BLOCK = 128
WINDOW = 256
ROW_TILE = 128
ROOT_HALF = 0.7071067811865476
DENSITY = 0.3989422804014327
B_Q, B_K, B_V, B_OUT, B_OUTER, S_ATTN, S_FFN, G_ATTN, G_FFN = range(9)
D_Q, D_V, D_OUT, D_OUTER, D_ATTN, D_FFN, D_INNER = range(7)
SUM_ROWS = 16


def chip_dims(devices):
    bits = (devices // 2).bit_length() - 1
    first = -(-bits // 3)
    second = -(-(bits - first) // 2)
    return (1 << first, 1 << second, 1 << (bits - first - second))


ORDERS = (((0, 2, 1), (1, 0, 2)), ((0, 1, 2), (2, 0, 1)))
SLOTS = 8


class Gather:
    def __init__(self, dims, own, buf, ssem, rsem, total):
        self.dims, self.own, self.buf = dims, own, buf
        self.ssem, self.rsem, self.total = ssem, rsem, total
        self.me = lax.axis_index("dp")
        _, n1, n2 = dims
        self.core = lax.rem(self.me, 2)
        chip = self.me // 2
        self.at = (chip // (n1 * n2), lax.rem(chip // n2, n1), lax.rem(chip, n2))
        self.step = (n1 * n2 * 2, n2 * 2, 2)
        rows, cols = own.shape[-2:]
        if rows % 32 == 0:
            cut = rows * 3 // 4
            self.parts = (
                (pl.ds(0, cut), pl.ds(0, cols)),
                (pl.ds(cut, rows - cut), pl.ds(0, cols)),
            )
        else:
            cut = cols * 3 // 4
            self.parts = (
                (pl.ds(0, rows), pl.ds(0, cut)),
                (pl.ds(0, rows), pl.ds(cut, cols - cut)),
            )

    def peers(self, dim):
        if dim == 3:
            return [self.me + 1 - 2 * self.core]
        out = []
        for d in range(1, self.dims[dim]):
            to = lax.rem(self.at[dim] + d, self.dims[dim])
            out.append(self.me + (to - self.at[dim]) * self.step[dim])
        return out

    def copies(self, g, par, s, p):
        order = ORDERS[par][s] + (3,)
        full = order[:p]
        where = tuple(
            pl.ds(0, self.dims[d]) if d in full else self.at[d] for d in range(3)
        )
        sub = self.parts[s]
        dst = self.buf.at[(g,) + where + (self.core,) + sub]
        src = self.own.at[(g,) + sub] if p == 0 else dst
        slot = lax.rem(g, SLOTS)
        first = sum(self.dims[d] - 1 for d in order[:p])
        return [
            pltpu.make_async_remote_copy(
                src_ref=src,
                dst_ref=dst,
                send_sem=self.ssem.at[slot, s, first + i],
                recv_sem=self.rsem.at[slot, s, first + i],
                device_id=(to,),
                device_id_type=MESH,
            )
            for i, to in enumerate(self.peers(order[p]))
        ]

    def barrier(self):
        bar = pltpu.get_barrier_semaphore()
        everyone = [to for d in range(4) for to in self.peers(d)]
        for to in everyone:
            pl.semaphore_signal(bar, inc=1, device_id=(to,), device_id_type=MESH)
        pl.semaphore_wait(bar, len(everyone))

    def pump(self, pair_step, par):
        for p in (3, 2, 1, 0):
            pair = pair_step - p

            @pl.when((pair >= 0) & (pair < self.total // 2))
            def _():
                g = 2 * pair + par
                for s in range(2):
                    if p > 0:
                        for c in self.copies(g, par, s, p - 1):
                            c.wait()
                    for c in self.copies(g, par, s, p):
                        c.start()

    def arrive(self, pair, par):
        for s in range(2):
            for c in self.copies(2 * pair + par, par, s, 3):
                c.wait()


def gather_kernel(dims, total, own, buf, ssem, rsem, lsem):
    gather = Gather(dims, own, buf, ssem, rsem, total)
    here = pltpu.make_async_copy(
        own, buf.at[(pl.ds(0, total),) + gather.at + (gather.core,)], lsem
    )
    here.start()
    gather.barrier()
    here.wait()

    def body(step, _):
        for par in range(2):
            gather.pump(step, par)

            @pl.when(step >= 4)
            def _():
                gather.arrive(step - 4, par)

        return 0

    lax.fori_loop(0, total // 2 + 4, body, 0)


def gather_weights(own, devices):
    total, rows, cols = own.shape
    dims = chip_dims(devices)
    sems = sum(d - 1 for d in dims) + 1
    return pl.pallas_call(
        functools.partial(gather_kernel, dims, total),
        out_shape=jax.ShapeDtypeStruct((total,) + dims + (2, rows, cols), own.dtype),
        in_specs=[pl.BlockSpec(memory_space=HBM)],
        out_specs=pl.BlockSpec(memory_space=HBM),
        scratch_shapes=[DMA((SLOTS, 2, sems)), DMA((SLOTS, 2, sems)), DMA],
        compiler_params=pltpu.CompilerParams(collective_id=0, has_side_effects=True),
    )(own)


def matmul(left, right):
    return jnp.dot(left, right, preferred_element_type=jnp.float32)


def matmul_nt(left, right):
    return lax.dot_general(
        left, right, (((1,), (1,)), ((), ())), preferred_element_type=jnp.float32
    )


def matmul_tn(left, right):
    return lax.dot_general(
        left, right, (((0,), (0,)), ((), ())), preferred_element_type=jnp.float32
    )


def loop(count, body):
    lax.fori_loop(0, count, lambda i, c: (body(i), c)[1], 0)


def tile(i, size):
    return pl.ds(pl.multiple_of(i * size, size), size)


def window_starts(slots):
    return [
        min(max(b * BLOCK - (WINDOW - BLOCK) // 2, 0), slots - WINDOW)
        for b in range(slots // BLOCK)
    ]


def pair_stack(rows):
    lane = lax.broadcasted_iota(jnp.int32, rows.shape, 1)
    zero = jnp.zeros_like(rows)
    half = rows.shape[1] // 2
    return jnp.concatenate(
        [jnp.where(lane < half, rows, zero), jnp.where(lane < half, zero, rows)], axis=0
    )


def pair_join(stacked):
    rows = stacked.shape[0] // 2
    lane = lax.broadcasted_iota(jnp.int32, (rows, stacked.shape[1]), 1)
    return jnp.where(lane < stacked.shape[1] // 2, stacked[:rows], stacked[rows:])


def forward_kernel(
    dims,
    wbuf, tokens, id_row, id_col, vectors, inner_bias,
    out, saved_qkv, saved_p, saved_x, saved_s, saved_d,
    h, a, qkv, o, z, u, w, p_stage, d_stage, x_stage, s_stage,
    wsem, psem, dsem, xsem, ssem, qsem, tsem,
):
    rows, slots = dims
    count = h.shape[0]
    pairs = HEADS // 2
    total = LAYERS * GROUPS

    def wload(g):
        slot = lax.rem(g, 3)
        return pltpu.make_async_copy(wbuf.at[g], w.at[slot], wsem.at[slot])

    def weights(g):
        @pl.when(g + 2 < total)
        def _():
            wload(g + 2).start()

        wload(g).wait()
        return w[lax.rem(g, 3)]

    load = pltpu.make_async_copy(tokens, a, tsem)
    load.start()
    wload(0).start()
    wload(1).start()
    load.wait()

    def widen(i):
        h[tile(i, ROW_TILE), :] = a[tile(i, ROW_TILE), :].astype(jnp.float32)

    loop(count // ROW_TILE, widen)

    def normalize(l, which):
        bias, gain, shift = ((B_OUT, G_ATTN, S_ATTN), (B_OUTER, G_FFN, S_FFN))[which]
        store_x = pltpu.make_async_copy(x_stage, saved_x.at[l, which], xsem)
        store_s = pltpu.make_async_copy(s_stage, saved_s.at[l, which], ssem)
        if which == 1:
            store_x.wait()
            store_s.wait()
        else:

            @pl.when(l > 0)
            def _():
                store_x.wait()
                store_s.wait()

        def body(i):
            t = tile(i, ROW_TILE)
            r = h[t, :] + vectors[l, bias : bias + 1, :]
            centered = r - jnp.mean(r, axis=1, keepdims=True)
            var = jnp.mean(centered * centered, axis=1, keepdims=True)
            scale = lax.rsqrt(var + EPSILON)
            xhat = centered * scale
            x_stage[t, :] = xhat
            s_stage[t, :] = jnp.broadcast_to(scale, (ROW_TILE, 128))
            y = xhat * vectors[l, gain : gain + 1, :] + vectors[l, shift : shift + 1, :]
            h[t, :] = y
            a[t, :] = y.astype(jnp.bfloat16)

        loop(count // ROW_TILE, body)
        store_x.start()
        store_s.start()

    def layer(l):
        base = l * GROUPS

        @pl.when(l > 0)
        def _():
            for m in range(3):
                pltpu.make_async_copy(qkv.at[m], saved_qkv.at[l, m], qsem.at[m]).wait()

        def project(i):
            m = i // 2
            y = matmul(a[...], weights(base + i)) + vectors[l, pl.ds(m, 1), tile(i % 2, WIDTH)]
            y = y * jnp.where(m == 0, jnp.float32((h.shape[1] // HEADS) ** -0.5), jnp.float32(1))
            qkv[m, :, tile(i % 2, WIDTH)] = y.astype(jnp.bfloat16)

        loop(6, project)
        for m in range(3):
            pltpu.make_async_copy(qkv.at[m], saved_qkv.at[l, m], qsem.at[m]).start()

        def attend(i):
            r = i // pairs
            lanes = tile(lax.rem(i, pairs), 128)
            slot = lax.rem(i, 2)
            store_p = pltpu.make_async_copy(p_stage.at[slot], saved_p.at[l, i], psem.at[slot])

            @pl.when((i >= 2) | (l > 0))
            def _():
                store_p.wait()

            top = pl.multiple_of(r * slots, slots)
            for b, start in enumerate(window_starts(slots)):
                qm = pair_stack(qkv[0, pl.ds(top + b * BLOCK, BLOCK), lanes])
                km = qkv[1, pl.ds(top + start, WINDOW), lanes]
                vm = qkv[2, pl.ds(top + start, WINDOW), lanes]
                same = id_col[r, start : start + WINDOW, :] == id_row[r, :, b * BLOCK : (b + 1) * BLOCK]
                s = matmul_nt(km, qm)
                s = jnp.where(jnp.concatenate([same, same], axis=1), s, NEGATIVE)
                e = jnp.exp(s - jnp.max(s, axis=0, keepdims=True))
                p = e * (1.0 / jnp.sum(e, axis=0, keepdims=True))
                p = p.astype(jnp.bfloat16)
                p_stage[slot, b] = p
                o[pl.ds(top + b * BLOCK, BLOCK), lanes] = pair_join(matmul_tn(p, vm)).astype(jnp.bfloat16)
            store_p.start()

        loop(rows * pairs, attend)

        def attn_out(i):
            cols = tile(i, WIDTH)
            h[:, cols] += matmul(o[...], weights(base + AT_OUT + i))

        loop(2, attn_out)
        normalize(l, 0)

        def inner(i):
            cols = tile(i, WIDTH)
            u[...] = matmul(a[...], weights(base + AT_INNER + i)) + inner_bias[l, :, cols]
            slot = lax.rem(i, 2)
            store_d = pltpu.make_async_copy(d_stage.at[slot], saved_d.at[l, i], dsem.at[slot])

            @pl.when((i >= 2) | (l > 0))
            def _():
                store_d.wait()

            def activate(t):
                part = tile(t, ROW_TILE)
                x = u[part, :]
                cdf = 0.5 + 0.5 * lax.erf(x * ROOT_HALF)
                z[i // 2, part, tile(i % 2, WIDTH)] = (x * cdf).astype(jnp.bfloat16)
                slope = cdf + x * (DENSITY * jnp.exp(-0.5 * x * x))
                d_stage[slot, part, :] = slope.astype(jnp.bfloat16)

            loop(count // ROW_TILE, activate)
            store_d.start()

        loop(8, inner)

        def outer(i):
            cols = tile(i // 4, WIDTH)
            h[:, cols] += matmul(z[lax.rem(i, 4)], weights(base + AT_OUTER + i))

        loop(8, outer)
        normalize(l, 1)

    loop(LAYERS, layer)
    store = pltpu.make_async_copy(a, out, tsem)
    store.start()
    last = LAYERS - 1
    for m in range(3):
        pltpu.make_async_copy(qkv.at[m], saved_qkv.at[last, m], qsem.at[m]).wait()
    for i in range(2):
        pltpu.make_async_copy(p_stage.at[i], saved_p.at[last, i], psem.at[i]).wait()
        pltpu.make_async_copy(d_stage.at[i], saved_d.at[last, i], dsem.at[i]).wait()
    pltpu.make_async_copy(x_stage, saved_x.at[last, 1], xsem).wait()
    pltpu.make_async_copy(s_stage, saved_s.at[last, 1], ssem).wait()
    store.wait()


def forward(wbuf, tokens, id_row, id_col, vectors, inner_bias, rows, slots):
    count, width = tokens.shape
    hidden = inner_bias.shape[-1]
    bf, f32 = jnp.bfloat16, jnp.float32
    blocks = slots // BLOCK
    any_ = pl.BlockSpec(memory_space=HBM)
    vm = pl.BlockSpec(memory_space=VMEM)
    return pl.pallas_call(
        functools.partial(forward_kernel, (rows, slots)),
        out_shape=(
            jax.ShapeDtypeStruct((count, width), bf),
            jax.ShapeDtypeStruct((LAYERS, 3, count, width), bf),
            jax.ShapeDtypeStruct((LAYERS, rows * HEADS // 2, blocks, WINDOW, 2 * BLOCK), bf),
            jax.ShapeDtypeStruct((LAYERS, 2, count, width), f32),
            jax.ShapeDtypeStruct((LAYERS, 2, count, 128), f32),
            jax.ShapeDtypeStruct((LAYERS, hidden // WIDTH, count, WIDTH), bf),
        ),
        in_specs=[any_, any_, vm, vm, vm, vm],
        out_specs=(any_,) * 6,
        scratch_shapes=[
            VMEM((count, width), f32),
            VMEM((count, width), bf),
            VMEM((3, count, width), bf),
            VMEM((count, width), bf),
            VMEM((hidden // width, count, width), bf),
            VMEM((count, WIDTH), f32),
            VMEM((3, width, WIDTH), bf),
            VMEM((2, blocks, WINDOW, 2 * BLOCK), bf),
            VMEM((2, count, WIDTH), bf),
            VMEM((count, width), f32),
            VMEM((count, 128), f32),
            DMA((3,)), DMA((2,)), DMA((2,)), DMA, DMA, DMA((3,)), DMA,
        ],
        compiler_params=pltpu.CompilerParams(vmem_limit_bytes=56 << 20),
    )(wbuf, tokens, id_row, id_col, vectors, inner_bias)


def fold(x):
    rows, width = x.shape
    return jnp.sum(x.reshape(rows // 8, 8, width), axis=0)


def backward_kernel(
    dims,
    wbuf, cotangent, real, vectors, saved_qkv, saved_p, saved_x, saved_s, saved_d,
    grad, sums,
    g, db, du, dh, qkv, dqkv, x, sc, d, w, p, dk, dv, part,
    wsem, psem, dsem, xsem, ssem, qsem, gsem,
):
    rows, slots = dims
    count, width = g.shape
    pairs = HEADS // 2
    total = LAYERS * GROUPS
    items = rows * pairs

    def block_of(i):
        l = LAYERS - 1 - i // GROUPS
        j = lax.rem(i, GROUPS)
        quarter, within = j // 4, lax.rem(j, 4)
        ffn = jnp.where(within < 2, AT_OUTER + 4 * within + quarter, AT_INNER + 2 * quarter + within - 2)
        late = jnp.where(j < 18, AT_OUT + j - 16, j - 18)
        return l * GROUPS + jnp.where(j < 16, ffn, late)

    def wload(i):
        slot = lax.rem(i, 3)
        return pltpu.make_async_copy(wbuf.at[block_of(i)], w.at[slot], wsem.at[slot])

    def weights(i):
        @pl.when(i + 2 < total)
        def _():
            wload(i + 2).start()

        wload(i).wait()
        return lax.rem(i, 3)

    def xload(l, which):
        return (
            pltpu.make_async_copy(saved_x.at[l, which], x.at[which], xsem.at[which]),
            pltpu.make_async_copy(saved_s.at[l, which], sc.at[which], ssem.at[which]),
        )

    def dload(l, i):
        slot = lax.rem(i, 2)
        return pltpu.make_async_copy(saved_d.at[l, i], d.at[slot], dsem.at[slot])

    def pload(l, i):
        slot = lax.rem(i, 2)
        return pltpu.make_async_copy(saved_p.at[l, i], p.at[slot], psem.at[slot])

    def qload(l):
        return [pltpu.make_async_copy(saved_qkv.at[l, m], qkv.at[m], qsem.at[m]) for m in range(3)]

    top_layer = LAYERS - 1
    first = pltpu.make_async_copy(cotangent, db, gsem)
    first.start()
    for which in (1, 0):
        for c in xload(top_layer, which):
            c.start()
    wload(0).start()
    wload(1).start()
    dload(top_layer, 0).start()
    first.wait()

    def widen(i):
        t = tile(i, ROW_TILE)
        g[t, :] = db[t, :].astype(jnp.float32) * real[t, :]

    loop(count // ROW_TILE, widen)

    def normalize_back(l, which):
        gain = (G_ATTN, G_FFN)[which]
        row_shift = (D_ATTN, D_FFN)[which]
        row_bias = (D_OUT, D_OUTER)[which]
        for c in xload(l, which):
            c.wait()

        def body(i, carry):
            t = tile(i, ROW_TILE)
            up = g[t, :]
            xh = x[which, t, :]
            scaled = up * vectors[l, gain : gain + 1, :]
            m1 = jnp.mean(scaled, axis=1, keepdims=True)
            m2 = jnp.mean(scaled * xh, axis=1, keepdims=True)
            down = sc[which, t, :1] * (scaled - m1 - xh * m2)
            g[t, :] = down
            low = down.astype(jnp.bfloat16)
            db[t, :] = low
            return carry[0] + fold(up), carry[1] + fold(low.astype(jnp.float32))

        zero = jnp.zeros((8, width), jnp.float32)
        shift_sum, bias_sum = lax.fori_loop(0, count // ROW_TILE, body, (zero, zero))
        part[row_shift] = shift_sum
        part[row_bias] = bias_sum

        @pl.when(l > 0)
        def _():
            for c in xload(l - 1, which):
                c.start()

    def layer(step):
        l = top_layer - step
        base = step * GROUPS
        for c in qload(l):
            c.start()
        normalize_back(l, 1)

        def quarter(kc):
            at = base + 4 * kc
            slot = weights(at)
            for c in range(width // 256):
                n = slice(c * 256, (c + 1) * 256)
                dh[:, n] = matmul_nt(db[:, :WIDTH], w[slot, n, :])
            slot = weights(at + 1)
            for c in range(width // 256):
                n = slice(c * 256, (c + 1) * 256)
                dh[:, n] += matmul_nt(db[:, WIDTH:], w[slot, n, :])

            total_ = []
            for half in range(2):
                i = 2 * kc + half

                @pl.when(i + 1 < 8)
                def _():
                    dload(l, i + 1).start()

                dload(l, i).wait()

                def slope(t, carry):
                    tl = tile(t, ROW_TILE)
                    cols = pl.ds(half * WIDTH, WIDTH)
                    low = (dh[tl, cols] * d[half, tl, :].astype(jnp.float32)).astype(jnp.bfloat16)
                    du[tl, cols] = low
                    return carry + fold(low.astype(jnp.float32))

                total_.append(
                    lax.fori_loop(0, count // ROW_TILE, slope, jnp.zeros((8, WIDTH), jnp.float32))
                )
            part[D_INNER + kc] = jnp.concatenate(total_, axis=1)

            def into(half):
                slot = weights(at + 2 + half)
                for c in range(width // 256):
                    n = slice(c * 256, (c + 1) * 256)
                    g[:, n] += matmul_nt(du[:, tile(half, WIDTH)], w[slot, n, :])

            loop(2, into)

        loop(4, quarter)

        @pl.when(l > 0)
        def _():
            dload(l - 1, 0).start()

        pload(l, 0).start()
        normalize_back(l, 0)

        slot = weights(base + 16)
        for c in range(width // 256):
            n = slice(c * 256, (c + 1) * 256)
            dh[:, n] = matmul_nt(db[:, :WIDTH], w[slot, n, :])
        slot = weights(base + 17)
        for c in range(width // 256):
            n = slice(c * 256, (c + 1) * 256)
            du[:, n] = (dh[:, n] + matmul_nt(db[:, WIDTH:], w[slot, n, :])).astype(jnp.bfloat16)
        for c in qload(l):
            c.wait()

        def attend(i):
            r = i // pairs
            lanes = tile(lax.rem(i, pairs), 128)
            slot = lax.rem(i, 2)

            @pl.when(i + 1 < items)
            def _():
                pload(l, i + 1).start()

            pload(l, i).wait()
            dk[...] = jnp.zeros_like(dk)
            dv[...] = jnp.zeros_like(dv)
            top = pl.multiple_of(r * slots, slots)
            for b, start in enumerate(window_starts(slots)):
                mine = pl.ds(top + b * BLOCK, BLOCK)
                reach = pl.ds(top + start, WINDOW)
                qm = pair_stack(qkv[0, mine, lanes])
                om = pair_stack(du[mine, lanes])
                pb = p[slot, b]
                pf = pb.astype(jnp.float32)
                dp = matmul_nt(qkv[2, reach, lanes], om)
                weighted = pf * dp
                ds = weighted - pf * jnp.sum(weighted, axis=0, keepdims=True)
                ds = ds.astype(jnp.bfloat16)
                dk[start : start + WINDOW, :] += matmul(ds, qm)
                dv[start : start + WINDOW, :] += matmul(pb, om)
                dq = pair_join(matmul_tn(ds, qkv[1, reach, lanes]))
                dqkv[0, mine, lanes] = (dq * (width // HEADS) ** -0.5).astype(jnp.bfloat16)
            every = pl.ds(top, slots)
            dqkv[1, every, lanes] = dk[...].astype(jnp.bfloat16)
            dqkv[2, every, lanes] = dv[...].astype(jnp.bfloat16)

        loop(items, attend)

        for m, row in ((0, D_Q), (2, D_V)):

            def add(t, carry):
                return carry + fold(dqkv[m, tile(t, ROW_TILE), :].astype(jnp.float32))

            part[row] = lax.fori_loop(
                0, count // ROW_TILE, add, jnp.zeros((8, width), jnp.float32)
            )

        def project(i):
            slot = weights(base + 18 + i)
            for c in range(width // 256):
                n = slice(c * 256, (c + 1) * 256)
                g[:, n] += matmul_nt(dqkv[i // 2, :, tile(lax.rem(i, 2), WIDTH)], w[slot, n, :])

        loop(6, project)
        sums[l] = jnp.sum(part[...], axis=1)

    part[...] = jnp.zeros_like(part)
    loop(LAYERS, layer)
    last = pltpu.make_async_copy(g, grad, gsem)
    last.start()
    last.wait()


def backward(wbuf, cotangent, real, vectors, saved, rows, slots):
    count, width = cotangent.shape
    bf, f32 = jnp.bfloat16, jnp.float32
    blocks = slots // BLOCK
    any_ = pl.BlockSpec(memory_space=HBM)
    vm = pl.BlockSpec(memory_space=VMEM)
    return pl.pallas_call(
        functools.partial(backward_kernel, (rows, slots)),
        out_shape=(
            jax.ShapeDtypeStruct((count, width), f32),
            jax.ShapeDtypeStruct((LAYERS, SUM_ROWS, width), f32),
        ),
        in_specs=[any_, any_, vm, vm] + [any_] * 5,
        out_specs=(any_, vm),
        scratch_shapes=[
            VMEM((count, width), f32),
            VMEM((count, width), bf),
            VMEM((count, width), bf),
            VMEM((count, width), f32),
            VMEM((3, count, width), bf),
            VMEM((3, count, width), bf),
            VMEM((2, count, width), f32),
            VMEM((2, count, 128), f32),
            VMEM((2, count, WIDTH), bf),
            VMEM((3, width, WIDTH), bf),
            VMEM((2, blocks, WINDOW, 2 * BLOCK), bf),
            VMEM((slots, 128), f32),
            VMEM((slots, 128), f32),
            VMEM((SUM_ROWS, 8, width), f32),
            DMA((3,)), DMA((2,)), DMA((2,)), DMA((2,)), DMA((2,)), DMA((3,)), DMA,
        ],
        compiler_params=pltpu.CompilerParams(vmem_limit_bytes=58 << 20),
    )(wbuf, cotangent, real, vectors, *saved)


def reduce_kernel(devices, x, out, got, ssem, rsem):
    me = lax.axis_index("dp")
    steps = devices.bit_length() - 1
    mates = [me + (1 << i) - 2 * (1 << i) * lax.rem(me >> i, 2) for i in range(steps)]
    bar = pltpu.get_barrier_semaphore()
    for to in mates:
        pl.semaphore_signal(bar, inc=1, device_id=(to,), device_id_type=MESH)
    pl.semaphore_wait(bar, steps)
    out[0] = x[...]
    for i, to in enumerate(mates):
        copy = pltpu.make_async_remote_copy(
            src_ref=out.at[i],
            dst_ref=got.at[i],
            send_sem=ssem.at[i],
            recv_sem=rsem.at[i],
            device_id=(to,),
            device_id_type=MESH,
        )
        copy.start()
        copy.wait()
        out[i + 1] = out[i] + got[i]


def all_sum(x, devices):
    steps = devices.bit_length() - 1
    out = pl.pallas_call(
        functools.partial(reduce_kernel, devices),
        out_shape=jax.ShapeDtypeStruct((steps + 1,) + x.shape, x.dtype),
        in_specs=[pl.BlockSpec(memory_space=VMEM)],
        out_specs=pl.BlockSpec(memory_space=VMEM),
        scratch_shapes=[VMEM((steps,) + x.shape, x.dtype), DMA((steps,)), DMA((steps,))],
        compiler_params=pltpu.CompilerParams(collective_id=1, has_side_effects=True),
    )(x)
    return out[steps]


def pack(devices, w_query, w_key, w_value, w_out, w_inner, w_outer):
    layers, rows, width = w_query.shape
    hidden = w_inner.shape[2]

    def halves(m):
        return m.astype(jnp.bfloat16).reshape(layers, rows, -1, WIDTH).transpose(0, 2, 1, 3)

    inner = w_inner.astype(jnp.bfloat16).reshape(layers, rows, devices, hidden // width, rows)
    inner = inner.transpose(0, 3, 2, 1, 4)
    inner = inner.reshape(layers, hidden // WIDTH, WIDTH // rows, rows, rows)
    inner = inner.transpose(0, 1, 3, 2, 4).reshape(layers, hidden // WIDTH, rows, WIDTH)
    outer = w_outer.astype(jnp.bfloat16).reshape(layers, hidden // width, rows, width // WIDTH, WIDTH)
    outer = outer.transpose(0, 3, 1, 2, 4).reshape(layers, -1, rows, WIDTH)
    parts = [halves(m) for m in (w_query, w_key, w_value, w_out)] + [inner, outer]
    return jnp.concatenate(parts, axis=1).reshape(layers * GROUPS, rows, WIDTH)


def per_device(
    devices,
    tokens,
    lengths,
    w_query,
    w_key,
    w_value,
    w_out,
    w_inner,
    w_outer,
    bias_query,
    bias_value,
    bias_out,
    bias_inner,
    bias_outer,
    shift_attn,
    shift_ffn,
    gain_attn,
    gain_ffn,
    cotangent,
):
    rows, slots, width = tokens.shape
    hidden = bias_inner.shape[1]
    unit = w_query.shape[1]
    count = rows * slots
    segments = lengths.shape[1]
    ends = jnp.cumsum(lengths, axis=-1)
    position = jnp.arange(slots, dtype=jnp.int32)
    numbers = jnp.sum((position[None, :, None] >= ends[:, None, :]).astype(jnp.int32), axis=-1)
    is_real = numbers < segments - 1
    ids = jnp.where(is_real, numbers, PADDING_ID + position[None, :])
    id_row = ids[:, None, :]
    id_col = jnp.broadcast_to(ids[:, :, None], (rows, slots, 128))
    real = is_real.astype(jnp.float32).reshape(count, 1)
    vectors = jnp.stack(
        [bias_query, jnp.zeros_like(bias_query), bias_value, bias_out, bias_outer,
         shift_attn, shift_ffn, gain_attn, gain_ffn],
        axis=1,
    )
    inner_bias = (
        bias_inner.reshape(LAYERS, devices, hidden // width, unit)
        .transpose(0, 2, 1, 3)
        .reshape(LAYERS, 1, hidden)
    )
    own = pack(devices, w_query, w_key, w_value, w_out, w_inner, w_outer)
    wbuf = gather_weights(own, devices).reshape(LAYERS * GROUPS, width, WIDTH)
    out, *saved = forward(
        wbuf, tokens.reshape(count, width), id_row, id_col, vectors, inner_bias, rows, slots
    )
    grad, sums = backward(
        wbuf, cotangent.reshape(count, width), real, vectors, saved, rows, slots
    )
    sums = all_sum(sums, devices)
    grad_inner = sums[:, D_INNER : D_INNER + hidden // width].reshape(
        LAYERS, hidden // width, devices, unit
    )
    grad_inner = grad_inner.transpose(0, 2, 1, 3).reshape(LAYERS, hidden)
    return (
        out.reshape(rows, slots, width),
        grad.reshape(rows, slots, width),
        sums[:, D_Q],
        sums[:, D_V],
        sums[:, D_OUT],
        grad_inner,
        sums[:, D_OUTER],
        sums[:, D_ATTN],
        sums[:, D_FFN],
    )


def solution(mesh):
    rows, whole = P("dp", None, None), P()
    weight = P(None, "dp", None)
    placed = (rows, P("dp", None)) + (weight,) * 6 + (whole,) * 9 + (rows,)
    return jax.shard_map(
        functools.partial(per_device, mesh.shape["dp"]),
        mesh=mesh,
        in_specs=placed,
        out_specs=(rows, rows) + (whole,) * 7,
        check_vma=False,
    )
```

```python
import functools

import jax
import jax.numpy as jnp
from jax import lax
from jax.experimental import pallas as pl
from jax.experimental.pallas import tpu as pltpu
from jax.sharding import PartitionSpec as P

HEADS = 16
LAYERS = 2
EPSILON = 1e-12
NEGATIVE = -1e9
PADDING_ID = 1000
MESH = pl.DeviceIdType.MESH
HBM = pltpu.MemorySpace.HBM
VMEM = pltpu.VMEM
DMA = pltpu.SemaphoreType.DMA

WIDTH = 512
GROUPS = 24
AT_OUT, AT_INNER, AT_OUTER = 6, 8, 16
BLOCK = 128
WINDOW = 256
ROW_TILE = 128
ROOT_HALF = 0.7071067811865476
DENSITY = 0.3989422804014327
B_Q, B_K, B_V, B_OUT, B_OUTER, S_ATTN, S_FFN, G_ATTN, G_FFN = range(9)
D_Q, D_V, D_OUT, D_OUTER, D_ATTN, D_FFN, D_INNER = range(7)
SUM_ROWS = 16


def chip_dims(devices):
    bits = (devices // 2).bit_length() - 1
    first = -(-bits // 3)
    second = -(-(bits - first) // 2)
    return (1 << first, 1 << second, 1 << (bits - first - second))


ORDERS = (((0, 2, 1), (1, 0, 2)), ((0, 1, 2), (2, 0, 1)))
SLOTS = 8


class Gather:
    def __init__(self, dims, own, buf, ssem, rsem, total):
        self.dims, self.own, self.buf = dims, own, buf
        self.ssem, self.rsem, self.total = ssem, rsem, total
        self.me = lax.axis_index("dp")
        _, n1, n2 = dims
        self.core = lax.rem(self.me, 2)
        chip = self.me // 2
        self.at = (chip // (n1 * n2), lax.rem(chip // n2, n1), lax.rem(chip, n2))
        self.step = (n1 * n2 * 2, n2 * 2, 2)
        rows, cols = own.shape[-2:]
        if rows % 32 == 0:
            cut = rows * 3 // 4
            self.parts = (
                (pl.ds(0, cut), pl.ds(0, cols)),
                (pl.ds(cut, rows - cut), pl.ds(0, cols)),
            )
        else:
            cut = cols * 3 // 4
            self.parts = (
                (pl.ds(0, rows), pl.ds(0, cut)),
                (pl.ds(0, rows), pl.ds(cut, cols - cut)),
            )

    def peers(self, dim):
        if dim == 3:
            return [self.me + 1 - 2 * self.core]
        out = []
        for d in range(1, self.dims[dim]):
            to = lax.rem(self.at[dim] + d, self.dims[dim])
            out.append(self.me + (to - self.at[dim]) * self.step[dim])
        return out

    def copies(self, g, par, s, p):
        order = ORDERS[par][s] + (3,)
        full = order[:p]
        where = tuple(
            pl.ds(0, self.dims[d]) if d in full else self.at[d] for d in range(3)
        )
        sub = self.parts[s]
        dst = self.buf.at[(g,) + where + (self.core,) + sub]
        src = self.own.at[(g,) + sub] if p == 0 else dst
        slot = lax.rem(g, SLOTS)
        first = sum(self.dims[d] - 1 for d in order[:p])
        return [
            pltpu.make_async_remote_copy(
                src_ref=src,
                dst_ref=dst,
                send_sem=self.ssem.at[slot, s, first + i],
                recv_sem=self.rsem.at[slot, s, first + i],
                device_id=(to,),
                device_id_type=MESH,
            )
            for i, to in enumerate(self.peers(order[p]))
        ]

    def barrier(self):
        bar = pltpu.get_barrier_semaphore()
        everyone = [to for d in range(4) for to in self.peers(d)]
        for to in everyone:
            pl.semaphore_signal(bar, inc=1, device_id=(to,), device_id_type=MESH)
        pl.semaphore_wait(bar, len(everyone))

    def pump(self, pair_step, par):
        for p in (3, 2, 1, 0):
            pair = pair_step - p

            @pl.when((pair >= 0) & (pair < self.total // 2))
            def _():
                g = 2 * pair + par
                for s in range(2):
                    if p > 0:
                        for c in self.copies(g, par, s, p - 1):
                            c.wait()
                    for c in self.copies(g, par, s, p):
                        c.start()

        pair = pair_step - 4

        @pl.when((pair >= 0) & (pair < self.total // 2))
        def _():
            for s in range(2):
                for c in self.copies(2 * pair + par, par, s, 3):
                    c.wait()


def matmul(left, right):
    return jnp.dot(left, right, preferred_element_type=jnp.float32)


def matmul_nt(left, right):
    return lax.dot_general(
        left, right, (((1,), (1,)), ((), ())), preferred_element_type=jnp.float32
    )


def matmul_tn(left, right):
    return lax.dot_general(
        left, right, (((0,), (0,)), ((), ())), preferred_element_type=jnp.float32
    )


def loop(count, body):
    lax.fori_loop(0, count, lambda i, c: (body(i), c)[1], 0)


def tile(i, size):
    return pl.ds(pl.multiple_of(i * size, size), size)


def window_starts(slots):
    return [
        min(max(b * BLOCK - (WINDOW - BLOCK) // 2, 0), slots - WINDOW)
        for b in range(slots // BLOCK)
    ]


def pair_stack(rows):
    lane = lax.broadcasted_iota(jnp.int32, rows.shape, 1)
    zero = jnp.zeros_like(rows)
    half = rows.shape[1] // 2
    return jnp.concatenate(
        [jnp.where(lane < half, rows, zero), jnp.where(lane < half, zero, rows)], axis=0
    )


def pair_join(stacked):
    rows = stacked.shape[0] // 2
    lane = lax.broadcasted_iota(jnp.int32, (rows, stacked.shape[1]), 1)
    return jnp.where(lane < stacked.shape[1] // 2, stacked[:rows], stacked[rows:])


def forward_kernel(
    dims, devices_dims,
    own, tokens, id_row, id_col, vectors, inner_bias,
    wbuf, out, saved_qkv, saved_p, saved_x, saved_s, saved_d,
    h, a, qkv, o, z, u, w, p_stage, d_stage, x_stage, s_stage,
    wsem, psem, dsem, xsem, ssem, qsem, tsem, hsem, send_sem, recv_sem,
):
    rows, slots = dims
    count = h.shape[0]
    pairs = HEADS // 2
    total = LAYERS * GROUPS
    gather = Gather(devices_dims, own, wbuf, send_sem, recv_sem, total)

    def wload(g):
        slot = lax.rem(g, 2)
        return pltpu.make_async_copy(wbuf.at[g], w.at[slot], wsem.at[slot])

    def weights(g):
        @pl.when(g + 1 < total)
        def _():
            wload(g + 1).start()

        wload(g).wait()
        return w[lax.rem(g, 2)].reshape(h.shape[1], WIDTH)

    def pump(half):
        for par in range(2):

            @pl.when(lax.rem(half, 2) == par)
            def _():
                gather.pump(half // 2 + 4, par)

    load = pltpu.make_async_copy(tokens, a, tsem)
    load.start()
    here = pltpu.make_async_copy(
        own, wbuf.at[(pl.ds(0, total),) + gather.at + (gather.core,)], hsem
    )
    here.start()
    gather.barrier()
    here.wait()
    load.wait()

    def widen(i):
        h[tile(i, ROW_TILE), :] = a[tile(i, ROW_TILE), :].astype(jnp.float32)

    loop(count // ROW_TILE, widen)

    def start(i):
        for par in range(2):
            gather.pump(i, par)

    loop(4, start)
    pump(0)
    wload(0).start()

    def normalize(l, which):
        bias, gain, shift = ((B_OUT, G_ATTN, S_ATTN), (B_OUTER, G_FFN, S_FFN))[which]
        store_x = pltpu.make_async_copy(x_stage, saved_x.at[l, which], xsem)
        store_s = pltpu.make_async_copy(s_stage, saved_s.at[l, which], ssem)
        if which == 1:
            store_x.wait()
            store_s.wait()
        else:

            @pl.when(l > 0)
            def _():
                store_x.wait()
                store_s.wait()

        def body(i):
            t = tile(i, ROW_TILE)
            r = h[t, :] + vectors[l, bias : bias + 1, :]
            centered = r - jnp.mean(r, axis=1, keepdims=True)
            var = jnp.mean(centered * centered, axis=1, keepdims=True)
            scale = lax.rsqrt(var + EPSILON)
            xhat = centered * scale
            x_stage[t, :] = xhat
            s_stage[t, :] = jnp.broadcast_to(scale, (ROW_TILE, 128))
            y = xhat * vectors[l, gain : gain + 1, :] + vectors[l, shift : shift + 1, :]
            h[t, :] = y
            a[t, :] = y.astype(jnp.bfloat16)

        loop(count // ROW_TILE, body)
        store_x.start()
        store_s.start()

    def layer(l):
        base = l * GROUPS

        @pl.when(l > 0)
        def _():
            for m in range(3):
                pltpu.make_async_copy(qkv.at[m], saved_qkv.at[l, m], qsem.at[m]).wait()

        def project(i):
            pump(base + i + 1)
            m = i // 2
            y = matmul(a[...], weights(base + i)) + vectors[l, pl.ds(m, 1), tile(i % 2, WIDTH)]
            y = y * jnp.where(m == 0, jnp.float32((h.shape[1] // HEADS) ** -0.5), jnp.float32(1))
            qkv[m, :, tile(i % 2, WIDTH)] = y.astype(jnp.bfloat16)

        loop(6, project)
        for m in range(3):
            pltpu.make_async_copy(qkv.at[m], saved_qkv.at[l, m], qsem.at[m]).start()

        def attend(i):
            @pl.when(lax.rem(i, 2) == 0)
            def _():
                pump(base + 7 + i // 2)

            r = i // pairs
            lanes = tile(lax.rem(i, pairs), 128)
            slot = lax.rem(i, 2)
            store_p = pltpu.make_async_copy(p_stage.at[slot], saved_p.at[l, i], psem.at[slot])

            @pl.when((i >= 2) | (l > 0))
            def _():
                store_p.wait()

            top = pl.multiple_of(r * slots, slots)
            for b, start in enumerate(window_starts(slots)):
                qm = pair_stack(qkv[0, pl.ds(top + b * BLOCK, BLOCK), lanes])
                km = qkv[1, pl.ds(top + start, WINDOW), lanes]
                vm = qkv[2, pl.ds(top + start, WINDOW), lanes]
                same = id_col[r, start : start + WINDOW, :] == id_row[r, :, b * BLOCK : (b + 1) * BLOCK]
                s = matmul_nt(km, qm)
                s = jnp.where(jnp.concatenate([same, same], axis=1), s, NEGATIVE)
                e = jnp.exp(s - jnp.max(s, axis=0, keepdims=True))
                p = e * (1.0 / jnp.sum(e, axis=0, keepdims=True))
                p = p.astype(jnp.bfloat16)
                p_stage[slot, b] = p
                o[pl.ds(top + b * BLOCK, BLOCK), lanes] = pair_join(matmul_tn(p, vm)).astype(jnp.bfloat16)
            store_p.start()

        loop(rows * pairs, attend)

        def attn_out(i):
            pump(base + 15 + i)
            cols = tile(i, WIDTH)
            h[:, cols] += matmul(o[...], weights(base + AT_OUT + i))

        loop(2, attn_out)
        normalize(l, 0)

        def inner(i):
            @pl.when(i < 6)
            def _():
                pump(base + 17 + i)

            cols = tile(i, WIDTH)
            u[...] = matmul(a[...], weights(base + AT_INNER + i)) + inner_bias[l, :, cols]
            slot = lax.rem(i, 2)
            store_d = pltpu.make_async_copy(d_stage.at[slot], saved_d.at[l, i], dsem.at[slot])

            @pl.when((i >= 2) | (l > 0))
            def _():
                store_d.wait()

            def activate(t):
                part = tile(t, ROW_TILE)
                x = u[part, :]
                cdf = 0.5 + 0.5 * lax.erf(x * ROOT_HALF)
                z[i // 2, part, tile(i % 2, WIDTH)] = (x * cdf).astype(jnp.bfloat16)
                slope = cdf + x * (DENSITY * jnp.exp(-0.5 * x * x))
                d_stage[slot, part, :] = slope.astype(jnp.bfloat16)

            loop(count // ROW_TILE, activate)
            store_d.start()

        loop(8, inner)

        def outer(i):
            @pl.when(i < 2)
            def _():
                pump(base + 23 + i)

            cols = tile(i // 4, WIDTH)
            h[:, cols] += matmul(z[lax.rem(i, 4)], weights(base + AT_OUTER + i))

        loop(8, outer)
        normalize(l, 1)

    loop(LAYERS, layer)
    store = pltpu.make_async_copy(a, out, tsem)
    store.start()
    last = LAYERS - 1
    for m in range(3):
        pltpu.make_async_copy(qkv.at[m], saved_qkv.at[last, m], qsem.at[m]).wait()
    for i in range(2):
        pltpu.make_async_copy(p_stage.at[i], saved_p.at[last, i], psem.at[i]).wait()
        pltpu.make_async_copy(d_stage.at[i], saved_d.at[last, i], dsem.at[i]).wait()
    pltpu.make_async_copy(x_stage, saved_x.at[last, 1], xsem).wait()
    pltpu.make_async_copy(s_stage, saved_s.at[last, 1], ssem).wait()
    store.wait()


def forward(devices, own, tokens, id_row, id_col, vectors, inner_bias, rows, slots):
    count, width = tokens.shape
    hidden = inner_bias.shape[-1]
    bf, f32 = jnp.bfloat16, jnp.float32
    blocks = slots // BLOCK
    devices_dims = chip_dims(devices)
    held = devices_dims + (2,) + own.shape[1:]
    sems = sum(d - 1 for d in devices_dims) + 1
    any_ = pl.BlockSpec(memory_space=HBM)
    vm = pl.BlockSpec(memory_space=VMEM)
    return pl.pallas_call(
        functools.partial(forward_kernel, (rows, slots), devices_dims),
        out_shape=(
            jax.ShapeDtypeStruct((LAYERS * GROUPS,) + held, bf),
            jax.ShapeDtypeStruct((count, width), bf),
            jax.ShapeDtypeStruct((LAYERS, 3, count, width), bf),
            jax.ShapeDtypeStruct((LAYERS, rows * HEADS // 2, blocks, WINDOW, 2 * BLOCK), bf),
            jax.ShapeDtypeStruct((LAYERS, 2, count, width), f32),
            jax.ShapeDtypeStruct((LAYERS, 2, count, 128), f32),
            jax.ShapeDtypeStruct((LAYERS, hidden // WIDTH, count, WIDTH), bf),
        ),
        in_specs=[any_, any_, vm, vm, vm, vm],
        out_specs=(any_,) * 7,
        scratch_shapes=[
            VMEM((count, width), f32),
            VMEM((count, width), bf),
            VMEM((3, count, width), bf),
            VMEM((count, width), bf),
            VMEM((hidden // width, count, width), bf),
            VMEM((count, WIDTH), f32),
            VMEM((2,) + held, bf),
            VMEM((2, blocks, WINDOW, 2 * BLOCK), bf),
            VMEM((2, count, WIDTH), bf),
            VMEM((count, width), f32),
            VMEM((count, 128), f32),
            DMA((2,)), DMA((2,)), DMA((2,)), DMA, DMA, DMA((3,)), DMA, DMA,
            DMA((SLOTS, 2, sems)), DMA((SLOTS, 2, sems)),
        ],
        compiler_params=pltpu.CompilerParams(
            vmem_limit_bytes=56 << 20, collective_id=0, has_side_effects=True
        ),
    )(own, tokens, id_row, id_col, vectors, inner_bias)


def fold(x):
    rows, width = x.shape
    return jnp.sum(x.reshape(rows // 8, 8, width), axis=0)


def backward_kernel(
    dims,
    wbuf, cotangent, real, vectors, saved_qkv, saved_p, saved_x, saved_s, saved_d,
    grad, sums,
    g, db, du, dh, qkv, dqkv, x, sc, d, w, p, dk, dv, part,
    wsem, psem, dsem, xsem, ssem, qsem, gsem,
):
    rows, slots = dims
    count, width = g.shape
    pairs = HEADS // 2
    total = LAYERS * GROUPS
    items = rows * pairs

    def block_of(i):
        l = LAYERS - 1 - i // GROUPS
        j = lax.rem(i, GROUPS)
        quarter, within = j // 4, lax.rem(j, 4)
        ffn = jnp.where(within < 2, AT_OUTER + 4 * within + quarter, AT_INNER + 2 * quarter + within - 2)
        late = jnp.where(j < 18, AT_OUT + j - 16, j - 18)
        return l * GROUPS + jnp.where(j < 16, ffn, late)

    def wload(i):
        slot = lax.rem(i, 3)
        return pltpu.make_async_copy(wbuf.at[block_of(i)], w.at[slot], wsem.at[slot])

    def weights(i):
        @pl.when(i + 2 < total)
        def _():
            wload(i + 2).start()

        wload(i).wait()
        return lax.rem(i, 3)

    def xload(l, which):
        return (
            pltpu.make_async_copy(saved_x.at[l, which], x.at[which], xsem.at[which]),
            pltpu.make_async_copy(saved_s.at[l, which], sc.at[which], ssem.at[which]),
        )

    def dload(l, i):
        slot = lax.rem(i, 2)
        return pltpu.make_async_copy(saved_d.at[l, i], d.at[slot], dsem.at[slot])

    def pload(l, i):
        slot = lax.rem(i, 2)
        return pltpu.make_async_copy(saved_p.at[l, i], p.at[slot], psem.at[slot])

    def qload(l):
        return [pltpu.make_async_copy(saved_qkv.at[l, m], qkv.at[m], qsem.at[m]) for m in range(3)]

    top_layer = LAYERS - 1
    first = pltpu.make_async_copy(cotangent, db, gsem)
    first.start()
    for which in (1, 0):
        for c in xload(top_layer, which):
            c.start()
    wload(0).start()
    wload(1).start()
    dload(top_layer, 0).start()
    first.wait()

    def widen(i):
        t = tile(i, ROW_TILE)
        g[t, :] = db[t, :].astype(jnp.float32) * real[t, :]

    loop(count // ROW_TILE, widen)

    def normalize_back(l, which):
        gain = (G_ATTN, G_FFN)[which]
        row_shift = (D_ATTN, D_FFN)[which]
        row_bias = (D_OUT, D_OUTER)[which]
        for c in xload(l, which):
            c.wait()

        def body(i, carry):
            t = tile(i, ROW_TILE)
            up = g[t, :]
            xh = x[which, t, :]
            scaled = up * vectors[l, gain : gain + 1, :]
            m1 = jnp.mean(scaled, axis=1, keepdims=True)
            m2 = jnp.mean(scaled * xh, axis=1, keepdims=True)
            down = sc[which, t, :1] * (scaled - m1 - xh * m2)
            g[t, :] = down
            low = down.astype(jnp.bfloat16)
            db[t, :] = low
            return carry[0] + fold(up), carry[1] + fold(low.astype(jnp.float32))

        zero = jnp.zeros((8, width), jnp.float32)
        shift_sum, bias_sum = lax.fori_loop(0, count // ROW_TILE, body, (zero, zero))
        part[row_shift] = shift_sum
        part[row_bias] = bias_sum

        @pl.when(l > 0)
        def _():
            for c in xload(l - 1, which):
                c.start()

    def layer(step):
        l = top_layer - step
        base = step * GROUPS
        for c in qload(l):
            c.start()
        normalize_back(l, 1)

        def quarter(kc):
            at = base + 4 * kc
            slot = weights(at)
            for c in range(width // 256):
                n = slice(c * 256, (c + 1) * 256)
                dh[:, n] = matmul_nt(db[:, :WIDTH], w[slot, n, :])
            slot = weights(at + 1)
            for c in range(width // 256):
                n = slice(c * 256, (c + 1) * 256)
                dh[:, n] += matmul_nt(db[:, WIDTH:], w[slot, n, :])

            total_ = []
            for half in range(2):
                i = 2 * kc + half

                @pl.when(i + 1 < 8)
                def _():
                    dload(l, i + 1).start()

                dload(l, i).wait()

                def slope(t, carry):
                    tl = tile(t, ROW_TILE)
                    cols = pl.ds(half * WIDTH, WIDTH)
                    low = (dh[tl, cols] * d[half, tl, :].astype(jnp.float32)).astype(jnp.bfloat16)
                    du[tl, cols] = low
                    return carry + fold(low.astype(jnp.float32))

                total_.append(
                    lax.fori_loop(0, count // ROW_TILE, slope, jnp.zeros((8, WIDTH), jnp.float32))
                )
            part[D_INNER + kc] = jnp.concatenate(total_, axis=1)

            def into(half):
                slot = weights(at + 2 + half)
                for c in range(width // 256):
                    n = slice(c * 256, (c + 1) * 256)
                    g[:, n] += matmul_nt(du[:, tile(half, WIDTH)], w[slot, n, :])

            loop(2, into)

        loop(4, quarter)

        @pl.when(l > 0)
        def _():
            dload(l - 1, 0).start()

        pload(l, 0).start()
        normalize_back(l, 0)

        slot = weights(base + 16)
        for c in range(width // 256):
            n = slice(c * 256, (c + 1) * 256)
            dh[:, n] = matmul_nt(db[:, :WIDTH], w[slot, n, :])
        slot = weights(base + 17)
        for c in range(width // 256):
            n = slice(c * 256, (c + 1) * 256)
            du[:, n] = (dh[:, n] + matmul_nt(db[:, WIDTH:], w[slot, n, :])).astype(jnp.bfloat16)
        for c in qload(l):
            c.wait()

        def attend(i):
            r = i // pairs
            lanes = tile(lax.rem(i, pairs), 128)
            slot = lax.rem(i, 2)

            @pl.when(i + 1 < items)
            def _():
                pload(l, i + 1).start()

            pload(l, i).wait()
            dk[...] = jnp.zeros_like(dk)
            dv[...] = jnp.zeros_like(dv)
            top = pl.multiple_of(r * slots, slots)
            for b, start in enumerate(window_starts(slots)):
                mine = pl.ds(top + b * BLOCK, BLOCK)
                reach = pl.ds(top + start, WINDOW)
                qm = pair_stack(qkv[0, mine, lanes])
                om = pair_stack(du[mine, lanes])
                pb = p[slot, b]
                pf = pb.astype(jnp.float32)
                dp = matmul_nt(qkv[2, reach, lanes], om)
                weighted = pf * dp
                ds = weighted - pf * jnp.sum(weighted, axis=0, keepdims=True)
                ds = ds.astype(jnp.bfloat16)
                dk[start : start + WINDOW, :] += matmul(ds, qm)
                dv[start : start + WINDOW, :] += matmul(pb, om)
                dq = pair_join(matmul_tn(ds, qkv[1, reach, lanes]))
                dqkv[0, mine, lanes] = (dq * (width // HEADS) ** -0.5).astype(jnp.bfloat16)
            every = pl.ds(top, slots)
            dqkv[1, every, lanes] = dk[...].astype(jnp.bfloat16)
            dqkv[2, every, lanes] = dv[...].astype(jnp.bfloat16)

        loop(items, attend)

        for m, row in ((0, D_Q), (2, D_V)):

            def add(t, carry):
                return carry + fold(dqkv[m, tile(t, ROW_TILE), :].astype(jnp.float32))

            part[row] = lax.fori_loop(
                0, count // ROW_TILE, add, jnp.zeros((8, width), jnp.float32)
            )

        def project(i):
            slot = weights(base + 18 + i)
            for c in range(width // 256):
                n = slice(c * 256, (c + 1) * 256)
                g[:, n] += matmul_nt(dqkv[i // 2, :, tile(lax.rem(i, 2), WIDTH)], w[slot, n, :])

        loop(6, project)
        sums[l] = jnp.sum(part[...], axis=1)

    part[...] = jnp.zeros_like(part)
    loop(LAYERS, layer)
    last = pltpu.make_async_copy(g, grad, gsem)
    last.start()
    last.wait()


def backward(wbuf, cotangent, real, vectors, saved, rows, slots):
    count, width = cotangent.shape
    bf, f32 = jnp.bfloat16, jnp.float32
    blocks = slots // BLOCK
    any_ = pl.BlockSpec(memory_space=HBM)
    vm = pl.BlockSpec(memory_space=VMEM)
    return pl.pallas_call(
        functools.partial(backward_kernel, (rows, slots)),
        out_shape=(
            jax.ShapeDtypeStruct((count, width), f32),
            jax.ShapeDtypeStruct((LAYERS, SUM_ROWS, width), f32),
        ),
        in_specs=[any_, any_, vm, vm] + [any_] * 5,
        out_specs=(any_, vm),
        scratch_shapes=[
            VMEM((count, width), f32),
            VMEM((count, width), bf),
            VMEM((count, width), bf),
            VMEM((count, width), f32),
            VMEM((3, count, width), bf),
            VMEM((3, count, width), bf),
            VMEM((2, count, width), f32),
            VMEM((2, count, 128), f32),
            VMEM((2, count, WIDTH), bf),
            VMEM((3, width, WIDTH), bf),
            VMEM((2, blocks, WINDOW, 2 * BLOCK), bf),
            VMEM((slots, 128), f32),
            VMEM((slots, 128), f32),
            VMEM((SUM_ROWS, 8, width), f32),
            DMA((3,)), DMA((2,)), DMA((2,)), DMA((2,)), DMA((2,)), DMA((3,)), DMA,
        ],
        compiler_params=pltpu.CompilerParams(vmem_limit_bytes=58 << 20),
    )(wbuf, cotangent, real, vectors, *saved)


def reduce_kernel(devices, x, out, got, ssem, rsem):
    me = lax.axis_index("dp")
    steps = devices.bit_length() - 1
    mates = [me + (1 << i) - 2 * (1 << i) * lax.rem(me >> i, 2) for i in range(steps)]
    bar = pltpu.get_barrier_semaphore()
    for to in mates:
        pl.semaphore_signal(bar, inc=1, device_id=(to,), device_id_type=MESH)
    pl.semaphore_wait(bar, steps)
    out[0] = x[...]
    for i, to in enumerate(mates):
        copy = pltpu.make_async_remote_copy(
            src_ref=out.at[i],
            dst_ref=got.at[i],
            send_sem=ssem.at[i],
            recv_sem=rsem.at[i],
            device_id=(to,),
            device_id_type=MESH,
        )
        copy.start()
        copy.wait()
        out[i + 1] = out[i] + got[i]


def all_sum(x, devices):
    steps = devices.bit_length() - 1
    out = pl.pallas_call(
        functools.partial(reduce_kernel, devices),
        out_shape=jax.ShapeDtypeStruct((steps + 1,) + x.shape, x.dtype),
        in_specs=[pl.BlockSpec(memory_space=VMEM)],
        out_specs=pl.BlockSpec(memory_space=VMEM),
        scratch_shapes=[VMEM((steps,) + x.shape, x.dtype), DMA((steps,)), DMA((steps,))],
        compiler_params=pltpu.CompilerParams(collective_id=1, has_side_effects=True),
    )(x)
    return out[steps]


def pack(devices, w_query, w_key, w_value, w_out, w_inner, w_outer):
    layers, rows, width = w_query.shape
    hidden = w_inner.shape[2]

    def halves(m):
        return m.astype(jnp.bfloat16).reshape(layers, rows, -1, WIDTH).transpose(0, 2, 1, 3)

    inner = w_inner.astype(jnp.bfloat16).reshape(layers, rows, devices, hidden // width, rows)
    inner = inner.transpose(0, 3, 2, 1, 4)
    inner = inner.reshape(layers, hidden // WIDTH, WIDTH // rows, rows, rows)
    inner = inner.transpose(0, 1, 3, 2, 4).reshape(layers, hidden // WIDTH, rows, WIDTH)
    outer = w_outer.astype(jnp.bfloat16).reshape(layers, hidden // width, rows, width // WIDTH, WIDTH)
    outer = outer.transpose(0, 3, 1, 2, 4).reshape(layers, -1, rows, WIDTH)
    parts = [halves(m) for m in (w_query, w_key, w_value, w_out)] + [inner, outer]
    return jnp.concatenate(parts, axis=1).reshape(layers * GROUPS, rows, WIDTH)


def per_device(
    devices,
    tokens,
    lengths,
    w_query,
    w_key,
    w_value,
    w_out,
    w_inner,
    w_outer,
    bias_query,
    bias_value,
    bias_out,
    bias_inner,
    bias_outer,
    shift_attn,
    shift_ffn,
    gain_attn,
    gain_ffn,
    cotangent,
):
    rows, slots, width = tokens.shape
    hidden = bias_inner.shape[1]
    unit = w_query.shape[1]
    count = rows * slots
    segments = lengths.shape[1]
    ends = jnp.cumsum(lengths, axis=-1)
    position = jnp.arange(slots, dtype=jnp.int32)
    numbers = jnp.sum((position[None, :, None] >= ends[:, None, :]).astype(jnp.int32), axis=-1)
    is_real = numbers < segments - 1
    ids = jnp.where(is_real, numbers, PADDING_ID + position[None, :])
    id_row = ids[:, None, :]
    id_col = jnp.broadcast_to(ids[:, :, None], (rows, slots, 128))
    real = is_real.astype(jnp.float32).reshape(count, 1)
    vectors = jnp.stack(
        [bias_query, jnp.zeros_like(bias_query), bias_value, bias_out, bias_outer,
         shift_attn, shift_ffn, gain_attn, gain_ffn],
        axis=1,
    )
    inner_bias = (
        bias_inner.reshape(LAYERS, devices, hidden // width, unit)
        .transpose(0, 2, 1, 3)
        .reshape(LAYERS, 1, hidden)
    )
    own = pack(devices, w_query, w_key, w_value, w_out, w_inner, w_outer)
    wbuf, out, *saved = forward(
        devices, own, tokens.reshape(count, width), id_row, id_col, vectors, inner_bias, rows, slots
    )
    wbuf = wbuf.reshape(LAYERS * GROUPS, width, WIDTH)
    grad, sums = backward(
        wbuf, cotangent.reshape(count, width), real, vectors, saved, rows, slots
    )
    sums = all_sum(sums, devices)
    grad_inner = sums[:, D_INNER : D_INNER + hidden // width].reshape(
        LAYERS, hidden // width, devices, unit
    )
    grad_inner = grad_inner.transpose(0, 2, 1, 3).reshape(LAYERS, hidden)
    return (
        out.reshape(rows, slots, width),
        grad.reshape(rows, slots, width),
        sums[:, D_Q],
        sums[:, D_V],
        sums[:, D_OUT],
        grad_inner,
        sums[:, D_OUTER],
        sums[:, D_ATTN],
        sums[:, D_FFN],
    )


def solution(mesh):
    rows, whole = P("dp", None, None), P()
    weight = P(None, "dp", None)
    placed = (rows, P("dp", None)) + (weight,) * 6 + (whole,) * 9 + (rows,)
    return jax.shard_map(
        functools.partial(per_device, mesh.shape["dp"]),
        mesh=mesh,
        in_specs=placed,
        out_specs=(rows, rows) + (whole,) * 7,
        check_vma=False,
    )
```

```python
import functools

import jax
import jax.numpy as jnp
from jax import lax
from jax.experimental import pallas as pl
from jax.experimental.pallas import tpu as pltpu
from jax.sharding import PartitionSpec as P

HEADS = 16
LAYERS = 2
EPSILON = 1e-12
NEGATIVE = -1e9
PADDING_ID = 1000
MESH = pl.DeviceIdType.MESH
HBM = pltpu.MemorySpace.HBM
VMEM = pltpu.VMEM
DMA = pltpu.SemaphoreType.DMA

WIDTH = 512
GROUPS = 24
AT_OUT, AT_INNER, AT_OUTER = 6, 8, 16
BLOCK = 128
WINDOW = 256
ROW_TILE = 128
ROOT_HALF = 0.7071067811865476
DENSITY = 0.3989422804014327
B_Q, B_V, B_OUT, B_OUTER, S_ATTN, S_FFN, G_ATTN, G_FFN = range(8)
D_OUT, D_OUTER, D_ATTN, D_FFN, D_INNER = range(5)
EARLY = 8


def chip_dims(devices):
    bits = (devices // 2).bit_length() - 1
    first = -(-bits // 3)
    second = -(-(bits - first) // 2)
    return (1 << first, 1 << second, 1 << (bits - first - second))


ORDERS = (((0, 2, 1), (1, 0, 2)), ((0, 1, 2), (2, 0, 1)))
SLOTS = 8


class Gather:
    def __init__(self, dims, own, buf, ssem, rsem, total):
        self.dims, self.own, self.buf = dims, own, buf
        self.ssem, self.rsem, self.total = ssem, rsem, total
        self.me = lax.axis_index("dp")
        _, n1, n2 = dims
        self.core = lax.rem(self.me, 2)
        chip = self.me // 2
        self.at = (chip // (n1 * n2), lax.rem(chip // n2, n1), lax.rem(chip, n2))
        self.step = (n1 * n2 * 2, n2 * 2, 2)
        rows, cols = own.shape[-2:]
        if rows % 32 == 0:
            cut = rows * 3 // 4
            self.parts = (
                (pl.ds(0, cut), pl.ds(0, cols)),
                (pl.ds(cut, rows - cut), pl.ds(0, cols)),
            )
        else:
            cut = cols * 3 // 4
            self.parts = (
                (pl.ds(0, rows), pl.ds(0, cut)),
                (pl.ds(0, rows), pl.ds(cut, cols - cut)),
            )

    def peers(self, dim):
        if dim == 3:
            return [self.me + 1 - 2 * self.core]
        out = []
        for d in range(1, self.dims[dim]):
            to = lax.rem(self.at[dim] + d, self.dims[dim])
            out.append(self.me + (to - self.at[dim]) * self.step[dim])
        return out

    def copies(self, g, par, s, p):
        order = ORDERS[par][s] + (3,)
        full = order[:p]
        where = tuple(
            pl.ds(0, self.dims[d]) if d in full else self.at[d] for d in range(3)
        )
        sub = self.parts[s]
        dst = self.buf.at[(g,) + where + (self.core,) + sub]
        src = self.own.at[(g,) + sub] if p == 0 else dst
        slot = lax.rem(g, SLOTS)
        first = sum(self.dims[d] - 1 for d in order[:p])
        return [
            pltpu.make_async_remote_copy(
                src_ref=src,
                dst_ref=dst,
                send_sem=self.ssem.at[slot, s, first + i],
                recv_sem=self.rsem.at[slot, s, first + i],
                device_id=(to,),
                device_id_type=MESH,
            )
            for i, to in enumerate(self.peers(order[p]))
        ]

    def barrier(self):
        bar = pltpu.get_barrier_semaphore()
        everyone = [to for d in range(4) for to in self.peers(d)]
        for to in everyone:
            pl.semaphore_signal(bar, inc=1, device_id=(to,), device_id_type=MESH)
        pl.semaphore_wait(bar, len(everyone))

    def pump(self, pair_step, par):
        for p in (3, 2, 1, 0):
            pair = pair_step - p

            @pl.when((pair >= 0) & (pair < self.total // 2))
            def _():
                g = 2 * pair + par
                for s in range(2):
                    if p > 0:
                        for c in self.copies(g, par, s, p - 1):
                            c.wait()
                    for c in self.copies(g, par, s, p):
                        c.start()

        pair = pair_step - 4

        @pl.when((pair >= 0) & (pair < self.total // 2))
        def _():
            for s in range(2):
                for c in self.copies(2 * pair + par, par, s, 3):
                    c.wait()


def matmul(left, right):
    return jnp.dot(left, right, preferred_element_type=jnp.float32)


def matmul_nt(left, right):
    return lax.dot_general(
        left, right, (((1,), (1,)), ((), ())), preferred_element_type=jnp.float32
    )


def matmul_tn(left, right):
    return lax.dot_general(
        left, right, (((0,), (0,)), ((), ())), preferred_element_type=jnp.float32
    )


def loop(count, body):
    lax.fori_loop(0, count, lambda i, c: (body(i), c)[1], 0)


def tile(i, size):
    return pl.ds(pl.multiple_of(i * size, size), size)


def window_starts(slots):
    return [
        min(max(b * BLOCK - (WINDOW - BLOCK) // 2, 0), slots - WINDOW)
        for b in range(slots // BLOCK)
    ]


def pair_stack(rows):
    lane = lax.broadcasted_iota(jnp.int32, rows.shape, 1)
    zero = jnp.zeros_like(rows)
    half = rows.shape[1] // 2
    return jnp.concatenate(
        [jnp.where(lane < half, rows, zero), jnp.where(lane < half, zero, rows)], axis=0
    )


def pair_join(stacked):
    rows = stacked.shape[0] // 2
    lane = lax.broadcasted_iota(jnp.int32, (rows, stacked.shape[1]), 1)
    return jnp.where(lane < stacked.shape[1] // 2, stacked[:rows], stacked[rows:])


def permute_hidden(load, store, unit, hidden):
    devices = hidden // (4 * unit)
    for b in range(hidden // 128):
        block = None
        for piece in range(128 // unit):
            quarter, device = divmod(b * (128 // unit) + piece, devices)
            source = (4 * device + quarter) * unit
            x = load(source // 128)
            shift = (piece * unit - source) % 128
            if shift:
                x = pltpu.roll(x, shift, axis=1)
            if block is None:
                block = x
            else:
                lane = lax.broadcasted_iota(jnp.int32, x.shape, 1)
                block = jnp.where(lane >= piece * unit, x, block)
        store(b, block)


def store_block(own, first, b, x):
    per = WIDTH // 128
    own[first + b // per, :, b % per * 128 : (b % per + 1) * 128] = x.astype(own.dtype)


def slot_ids(lengths, r, position):
    segments = lengths.shape[1]
    number = jnp.zeros_like(position)
    end = jnp.int32(0)
    for j in range(segments):
        end = end + lengths[r, j]
        number = number + (position >= end).astype(jnp.int32)
    return jnp.where(number < segments - 1, number, PADDING_ID + position)


def forward_kernel(
    dims, devices_dims,
    lengths, w_query, w_key, w_value, w_out, w_inner, w_outer, tokens, *rest,
):
    vectors, rest = rest[:8], rest[8:]
    (
        inner_raw, wbuf, out, saved_qkv, saved_p, saved_x, saved_s, saved_d,
        h, a, qkv, o, z, u, w, p_stage, d_stage, x_stage, s_stage, own, id_row, id_col, inner_bias,
        wsem, psem, dsem, xsem, ssem, qsem, tsem, hsem, send_sem, recv_sem,
    ) = rest
    rows, slots = dims
    count = h.shape[0]
    pairs = HEADS // 2
    total = LAYERS * GROUPS
    gather = Gather(devices_dims, own, wbuf, send_sem, recv_sem, total)

    def wload(g):
        slot = lax.rem(g, 2)
        return pltpu.make_async_copy(wbuf.at[g], w.at[slot], wsem.at[slot])

    def weights(g):
        @pl.when(g + 1 < total)
        def _():
            wload(g + 1).start()

        wload(g).wait()
        return w[lax.rem(g, 2)].reshape(h.shape[1], WIDTH)

    def pump(half):
        for par in range(2):

            @pl.when(lax.rem(half, 2) == par)
            def _():
                gather.pump(half // 2 + 4, par)

    load = pltpu.make_async_copy(tokens, a, tsem)
    load.start()
    unit = own.shape[1]
    for l in range(LAYERS):
        at = l * GROUPS
        for m, matrix in enumerate((w_query, w_key, w_value, w_out)):
            for c in range(2):
                own[at + 2 * m + c] = matrix[l, :, c * WIDTH : (c + 1) * WIDTH].astype(jnp.bfloat16)
        for c in range(2):
            for kc in range(4):
                piece = w_outer[l, kc * unit : (kc + 1) * unit, c * WIDTH : (c + 1) * WIDTH]
                own[at + AT_OUTER + 4 * c + kc] = piece.astype(jnp.bfloat16)
        permute_hidden(
            lambda b: w_inner[l, :, b * 128 : (b + 1) * 128],
            lambda b, x: store_block(own, at + AT_INNER, b, x),
            unit,
            w_inner.shape[2],
        )
    here = pltpu.make_async_copy(
        own, wbuf.at[(pl.ds(0, total),) + gather.at + (gather.core,)], hsem
    )
    here.start()
    gather.barrier()
    here.wait()

    def start(i):
        for par in range(2):
            gather.pump(i, par)

    start(0)

    def keep_bias(b, x):
        inner_bias[:, b * 128 : (b + 1) * 128] = x

    permute_hidden(
        lambda b: inner_raw[:, b * 128 : (b + 1) * 128], keep_bias, unit, w_inner.shape[2]
    )
    for r in range(rows):
        id_row[r] = slot_ids(lengths, r, lax.broadcasted_iota(jnp.int32, (8, slots), 1))
        id_col[r] = slot_ids(lengths, r, lax.broadcasted_iota(jnp.int32, (slots, 128), 0))
    load.wait()

    def widen(i):
        h[tile(i, ROW_TILE), :] = a[tile(i, ROW_TILE), :].astype(jnp.float32)

    loop(count // ROW_TILE, widen)

    for i in (1, 2, 3):
        start(i)
    pump(0)
    wload(0).start()

    def normalize(l, which):
        bias, gain, shift = ((B_OUT, G_ATTN, S_ATTN), (B_OUTER, G_FFN, S_FFN))[which]
        store_x = pltpu.make_async_copy(x_stage, saved_x.at[l, which], xsem)
        store_s = pltpu.make_async_copy(s_stage, saved_s.at[l, which], ssem)
        if which == 1:
            store_x.wait()
            store_s.wait()
        else:

            @pl.when(l > 0)
            def _():
                store_x.wait()
                store_s.wait()

        def body(i):
            t = tile(i, ROW_TILE)
            r = h[t, :] + vectors[bias][pl.ds(l, 1), :]
            centered = r - jnp.mean(r, axis=1, keepdims=True)
            var = jnp.mean(centered * centered, axis=1, keepdims=True)
            scale = lax.rsqrt(var + EPSILON)
            xhat = centered * scale
            x_stage[t, :] = xhat
            s_stage[t, :] = jnp.broadcast_to(scale, (ROW_TILE, 128))
            y = xhat * vectors[gain][pl.ds(l, 1), :] + vectors[shift][pl.ds(l, 1), :]
            h[t, :] = y
            a[t, :] = y.astype(jnp.bfloat16)

        loop(count // ROW_TILE, body)
        store_x.start()
        store_s.start()

    def layer(l):
        base = l * GROUPS

        @pl.when(l > 0)
        def _():
            for m in range(3):
                pltpu.make_async_copy(qkv.at[m], saved_qkv.at[l, m], qsem.at[m]).wait()

        def project(i):
            pump(base + i + 1)
            m = i // 2
            cols = tile(i % 2, WIDTH)
            bias_q = vectors[B_Q][pl.ds(l, 1), cols]
            bias_v = vectors[B_V][pl.ds(l, 1), cols]
            bias = jnp.where(m == 0, bias_q, jnp.where(m == 1, jnp.zeros_like(bias_v), bias_v))
            y = matmul(a[...], weights(base + i)) + bias
            y = y * jnp.where(m == 0, jnp.float32((h.shape[1] // HEADS) ** -0.5), jnp.float32(1))
            qkv[m, :, cols] = y.astype(jnp.bfloat16)

        loop(6, project)
        for m in range(3):
            pltpu.make_async_copy(qkv.at[m], saved_qkv.at[l, m], qsem.at[m]).start()

        def attend(i):
            @pl.when(lax.rem(i, 2) == 0)
            def _():
                pump(base + 7 + i // 2)

            r = i // pairs
            lanes = tile(lax.rem(i, pairs), 128)
            slot = lax.rem(i, 2)
            store_p = pltpu.make_async_copy(p_stage.at[slot], saved_p.at[l, i], psem.at[slot])

            @pl.when((i >= 2) | (l > 0))
            def _():
                store_p.wait()

            top = pl.multiple_of(r * slots, slots)
            for b, start in enumerate(window_starts(slots)):
                qm = pair_stack(qkv[0, pl.ds(top + b * BLOCK, BLOCK), lanes])
                km = qkv[1, pl.ds(top + start, WINDOW), lanes]
                vm = qkv[2, pl.ds(top + start, WINDOW), lanes]
                same = id_col[r, start : start + WINDOW, :] == id_row[r, :1, b * BLOCK : (b + 1) * BLOCK]
                s = matmul_nt(km, qm)
                s = jnp.where(jnp.concatenate([same, same], axis=1), s, NEGATIVE)
                e = jnp.exp(s - jnp.max(s, axis=0, keepdims=True))
                p = e * (1.0 / jnp.sum(e, axis=0, keepdims=True))
                p = p.astype(jnp.bfloat16)
                p_stage[slot, b] = p
                o[pl.ds(top + b * BLOCK, BLOCK), lanes] = pair_join(matmul_tn(p, vm)).astype(jnp.bfloat16)
            store_p.start()

        loop(rows * pairs, attend)

        def attn_out(i):
            pump(base + 15 + i)
            cols = tile(i, WIDTH)
            h[:, cols] += matmul(o[...], weights(base + AT_OUT + i))

        loop(2, attn_out)
        normalize(l, 0)

        def inner(i):
            @pl.when(i < 6)
            def _():
                pump(base + 17 + i)

            cols = tile(i, WIDTH)
            u[...] = matmul(a[...], weights(base + AT_INNER + i)) + inner_bias[pl.ds(l, 1), cols]
            slot = lax.rem(i, 2)
            store_d = pltpu.make_async_copy(d_stage.at[slot], saved_d.at[l, i], dsem.at[slot])

            @pl.when((i >= 2) | (l > 0))
            def _():
                store_d.wait()

            def activate(t):
                part = tile(t, ROW_TILE)
                x = u[part, :]
                cdf = 0.5 + 0.5 * lax.erf(x * ROOT_HALF)
                z[i // 2, part, tile(i % 2, WIDTH)] = (x * cdf).astype(jnp.bfloat16)
                slope = cdf + x * (DENSITY * jnp.exp(-0.5 * x * x))
                d_stage[slot, part, :] = slope.astype(jnp.bfloat16)

            loop(count // ROW_TILE, activate)
            store_d.start()

        loop(8, inner)

        def outer(i):
            @pl.when(i < 2)
            def _():
                pump(base + 23 + i)

            cols = tile(i // 4, WIDTH)
            h[:, cols] += matmul(z[lax.rem(i, 4)], weights(base + AT_OUTER + i))

        loop(8, outer)
        normalize(l, 1)

    loop(LAYERS, layer)
    store = pltpu.make_async_copy(a, out, tsem)
    store.start()
    last = LAYERS - 1
    for m in range(3):
        pltpu.make_async_copy(qkv.at[m], saved_qkv.at[last, m], qsem.at[m]).wait()
    for i in range(2):
        pltpu.make_async_copy(p_stage.at[i], saved_p.at[last, i], psem.at[i]).wait()
        pltpu.make_async_copy(d_stage.at[i], saved_d.at[last, i], dsem.at[i]).wait()
    pltpu.make_async_copy(x_stage, saved_x.at[last, 1], xsem).wait()
    pltpu.make_async_copy(s_stage, saved_s.at[last, 1], ssem).wait()
    store.wait()


def forward(devices, lengths, matrices, tokens, vectors, inner_bias, rows, slots):
    count, width = tokens.shape
    hidden = inner_bias.shape[-1]
    unit = matrices[0].shape[1]
    bf, f32 = jnp.bfloat16, jnp.float32
    blocks = slots // BLOCK
    devices_dims = chip_dims(devices)
    held = devices_dims + (2, unit, WIDTH)
    sems = sum(d - 1 for d in devices_dims) + 1
    any_ = pl.BlockSpec(memory_space=HBM)
    vm = pl.BlockSpec(memory_space=VMEM)
    return pl.pallas_call(
        functools.partial(forward_kernel, (rows, slots), devices_dims),
        out_shape=(
            jax.ShapeDtypeStruct((LAYERS * GROUPS,) + held, bf),
            jax.ShapeDtypeStruct((count, width), bf),
            jax.ShapeDtypeStruct((LAYERS, 3, count, width), bf),
            jax.ShapeDtypeStruct((LAYERS, rows * HEADS // 2, blocks, WINDOW, 2 * BLOCK), bf),
            jax.ShapeDtypeStruct((LAYERS, 2, count, width), f32),
            jax.ShapeDtypeStruct((LAYERS, 2, count, 128), f32),
            jax.ShapeDtypeStruct((LAYERS, hidden // WIDTH, count, WIDTH), bf),
        ),
        in_specs=[pl.BlockSpec(memory_space=pltpu.SMEM)] + [vm] * 6 + [any_] + [vm] * 9,
        out_specs=(any_,) * 7,
        scratch_shapes=[
            VMEM((count, width), f32),
            VMEM((count, width), bf),
            VMEM((3, count, width), bf),
            VMEM((count, width), bf),
            VMEM((hidden // width, count, width), bf),
            VMEM((count, WIDTH), f32),
            VMEM((2,) + held, bf),
            VMEM((2, blocks, WINDOW, 2 * BLOCK), bf),
            VMEM((2, count, WIDTH), bf),
            VMEM((count, width), f32),
            VMEM((count, 128), f32),
            VMEM((LAYERS * GROUPS, unit, WIDTH), bf),
            VMEM((rows, 8, slots), jnp.int32),
            VMEM((rows, slots, 128), jnp.int32),
            VMEM((LAYERS, hidden), f32),
            DMA((2,)), DMA((2,)), DMA((2,)), DMA, DMA, DMA((3,)), DMA, DMA,
            DMA((SLOTS, 2, sems)), DMA((SLOTS, 2, sems)),
        ],
        compiler_params=pltpu.CompilerParams(
            vmem_limit_bytes=58 << 20, collective_id=0, has_side_effects=True
        ),
    )(lengths, *matrices, tokens, *vectors, inner_bias)


class Exchange:
    def __init__(self, mates, held, got, ssem, rsem):
        self.mates, self.held, self.got = mates, held, got
        self.ssem, self.rsem = ssem, rsem

    def copy(self, k):
        return pltpu.make_async_remote_copy(
            src_ref=self.held.at[k],
            dst_ref=self.got.at[k],
            send_sem=self.ssem.at[k],
            recv_sem=self.rsem.at[k],
            device_id=(self.mates[k],),
            device_id_type=MESH,
        )

    def step(self, k):
        if k > 0:
            self.copy(k - 1).wait()
            self.held[k] = self.held[k - 1] + self.got[k - 1]
        if k < len(self.mates):
            self.copy(k).start()


def fold(x):
    rows, width = x.shape
    return jnp.sum(x.reshape(rows // 8, 8, width), axis=0)


def backward_kernel(
    dims, devices,
    lengths, wbuf, cotangent, gain_attn, gain_ffn, saved_qkv, saved_p, saved_x, saved_s, saved_d,
    grad, sums, late_sums,
    g, db, du, dh, qkv, dqkv, x, sc, d, w, p, dk, dv, part, late,
    held, got, late_held, late_got,
    wsem, psem, dsem, xsem, ssem, qsem, gsem, send_sem, recv_sem, late_send, late_recv,
):
    rows, slots = dims
    count, width = g.shape
    pairs = HEADS // 2
    total = LAYERS * GROUPS
    items = rows * pairs

    def block_of(i):
        l = LAYERS - 1 - i // GROUPS
        j = lax.rem(i, GROUPS)
        quarter, within = j // 4, lax.rem(j, 4)
        ffn = jnp.where(within < 2, AT_OUTER + 4 * within + quarter, AT_INNER + 2 * quarter + within - 2)
        late = jnp.where(j < 18, AT_OUT + j - 16, j - 18)
        return l * GROUPS + jnp.where(j < 16, ffn, late)

    def wload(i):
        slot = lax.rem(i, 3)
        return pltpu.make_async_copy(wbuf.at[block_of(i)], w.at[slot], wsem.at[slot])

    def weights(i):
        @pl.when(i + 2 < total)
        def _():
            wload(i + 2).start()

        wload(i).wait()
        return lax.rem(i, 3)

    def xload(l, which):
        return (
            pltpu.make_async_copy(saved_x.at[l, which], x.at[which], xsem.at[which]),
            pltpu.make_async_copy(saved_s.at[l, which], sc.at[which], ssem.at[which]),
        )

    def dload(l, i):
        slot = lax.rem(i, 2)
        return pltpu.make_async_copy(saved_d.at[l, i], d.at[slot], dsem.at[slot])

    def pload(l, i):
        slot = lax.rem(i, 2)
        return pltpu.make_async_copy(saved_p.at[l, i], p.at[slot], psem.at[slot])

    def qload(l):
        return [pltpu.make_async_copy(saved_qkv.at[l, m], qkv.at[m], qsem.at[m]) for m in range(3)]

    top_layer = LAYERS - 1
    first = pltpu.make_async_copy(cotangent, db, gsem)
    first.start()
    for which in (1, 0):
        for c in xload(top_layer, which):
            c.start()
    wload(0).start()
    wload(1).start()
    dload(top_layer, 0).start()
    me = lax.axis_index("dp")
    steps = devices.bit_length() - 1
    mates = [me + (1 << k) - 2 * (1 << k) * lax.rem(me // (1 << k), 2) for k in range(steps)]
    barrier = pltpu.get_barrier_semaphore()
    for to in mates:
        pl.semaphore_signal(barrier, inc=1, device_id=(to,), device_id_type=MESH)
    first.wait()
    for r in range(rows):
        real = slots - lengths[r, lengths.shape[1] - 1]

        def widen(i):
            t = pl.ds(pl.multiple_of(r * slots + i * ROW_TILE, ROW_TILE), ROW_TILE)
            slot = i * ROW_TILE + lax.broadcasted_iota(jnp.int32, (ROW_TILE, width), 0)
            g[t, :] = jnp.where(slot < real, db[t, :].astype(jnp.float32), 0.0)

        loop(slots // ROW_TILE, widen)
    pl.semaphore_wait(barrier, steps)

    def normalize_back(l, which):
        gain = (gain_attn, gain_ffn)[which]
        row_shift = (D_ATTN, D_FFN)[which]
        row_bias = (D_OUT, D_OUTER)[which]
        for c in xload(l, which):
            c.wait()

        def body(i, carry):
            t = tile(i, ROW_TILE)
            up = g[t, :]
            xh = x[which, t, :]
            scaled = up * gain[pl.ds(l, 1), :]
            m1 = jnp.mean(scaled, axis=1, keepdims=True)
            m2 = jnp.mean(scaled * xh, axis=1, keepdims=True)
            down = sc[which, t, :1] * (scaled - m1 - xh * m2)
            g[t, :] = down
            low = down.astype(jnp.bfloat16)
            db[t, :] = low
            return carry[0] + fold(up), carry[1] + fold(low.astype(jnp.float32))

        zero = jnp.zeros((8, width), jnp.float32)
        shift_sum, bias_sum = lax.fori_loop(0, count // ROW_TILE, body, (zero, zero))
        part[row_shift] = shift_sum
        part[row_bias] = bias_sum

        @pl.when(l > 0)
        def _():
            for c in xload(l - 1, which):
                c.start()

    def layer(step):
        l = top_layer - step
        base = step * GROUPS
        for c in qload(l):
            c.start()
        normalize_back(l, 1)

        def quarter(kc):
            at = base + 4 * kc
            slot = weights(at)
            for c in range(width // 256):
                n = slice(c * 256, (c + 1) * 256)
                dh[:, n] = matmul_nt(db[:, :WIDTH], w[slot, n, :])
            slot = weights(at + 1)
            for c in range(width // 256):
                n = slice(c * 256, (c + 1) * 256)
                dh[:, n] += matmul_nt(db[:, WIDTH:], w[slot, n, :])

            total_ = []
            for half in range(2):
                i = 2 * kc + half

                @pl.when(i + 1 < 8)
                def _():
                    dload(l, i + 1).start()

                dload(l, i).wait()

                def slope(t, carry):
                    tl = tile(t, ROW_TILE)
                    cols = pl.ds(half * WIDTH, WIDTH)
                    low = (dh[tl, cols] * d[half, tl, :].astype(jnp.float32)).astype(jnp.bfloat16)
                    du[tl, cols] = low
                    return carry + fold(low.astype(jnp.float32))

                total_.append(
                    lax.fori_loop(0, count // ROW_TILE, slope, jnp.zeros((8, WIDTH), jnp.float32))
                )
            part[D_INNER + kc] = jnp.concatenate(total_, axis=1)

            def into(half):
                slot = weights(at + 2 + half)
                for c in range(width // 256):
                    n = slice(c * 256, (c + 1) * 256)
                    g[:, n] += matmul_nt(du[:, tile(half, WIDTH)], w[slot, n, :])

            loop(2, into)

        loop(4, quarter)

        @pl.when(l > 0)
        def _():
            dload(l - 1, 0).start()

        pload(l, 0).start()
        normalize_back(l, 0)

        slot = weights(base + 16)
        for c in range(width // 256):
            n = slice(c * 256, (c + 1) * 256)
            dh[:, n] = matmul_nt(db[:, :WIDTH], w[slot, n, :])
        slot = weights(base + 17)
        for c in range(width // 256):
            n = slice(c * 256, (c + 1) * 256)
            du[:, n] = (dh[:, n] + matmul_nt(db[:, WIDTH:], w[slot, n, :])).astype(jnp.bfloat16)
        for c in qload(l):
            c.wait()

        early = Exchange(mates, held.at[l], got.at[l], send_sem.at[l], recv_sem.at[l])
        held[l, 0] = jnp.sum(part[...], axis=1)
        early.step(0)
        apart = (items - 1) // steps

        def attend(i):
            for k in range(1, steps + 1):

                @pl.when(i == k * apart)
                def _():
                    early.step(k)

            r = i // pairs
            lanes = tile(lax.rem(i, pairs), 128)
            slot = lax.rem(i, 2)

            @pl.when(i + 1 < items)
            def _():
                pload(l, i + 1).start()

            pload(l, i).wait()
            dk[...] = jnp.zeros_like(dk)
            dv[...] = jnp.zeros_like(dv)
            top = pl.multiple_of(r * slots, slots)
            for b, start in enumerate(window_starts(slots)):
                mine = pl.ds(top + b * BLOCK, BLOCK)
                reach = pl.ds(top + start, WINDOW)
                qm = pair_stack(qkv[0, mine, lanes])
                om = pair_stack(du[mine, lanes])
                pb = p[slot, b]
                pf = pb.astype(jnp.float32)
                dp = matmul_nt(qkv[2, reach, lanes], om)
                weighted = pf * dp
                ds = weighted - pf * jnp.sum(weighted, axis=0, keepdims=True)
                ds = ds.astype(jnp.bfloat16)
                dk[start : start + WINDOW, :] += matmul(ds, qm)
                dv[start : start + WINDOW, :] += matmul(pb, om)
                dq = pair_join(matmul_tn(ds, qkv[1, reach, lanes]))
                dqkv[0, mine, lanes] = (dq * (width // HEADS) ** -0.5).astype(jnp.bfloat16)
            every = pl.ds(top, slots)
            dqkv[1, every, lanes] = dk[...].astype(jnp.bfloat16)
            dqkv[2, every, lanes] = dv[...].astype(jnp.bfloat16)

        loop(items, attend)

        sums[l] = held[l, steps]
        for m, row in ((0, 0), (2, 1)):

            def add(t, carry):
                return carry + fold(dqkv[m, tile(t, ROW_TILE), :].astype(jnp.float32))

            late[2 * l + row] = lax.fori_loop(
                0, count // ROW_TILE, add, jnp.zeros((8, width), jnp.float32)
            )

        @pl.when(l == 0)
        def _():
            late_held[0] = jnp.sum(late[...], axis=1)
            last_sums.step(0)

        def project(i):
            for k in range(1, min(steps, 5) + 1):

                @pl.when((l == 0) & (i == k))
                def _():
                    last_sums.step(k)

            slot = weights(base + 18 + i)
            for c in range(width // 256):
                n = slice(c * 256, (c + 1) * 256)
                g[:, n] += matmul_nt(dqkv[i // 2, :, tile(lax.rem(i, 2), WIDTH)], w[slot, n, :])

        loop(6, project)

    last_sums = Exchange(mates, late_held, late_got, late_send, late_recv)
    late[...] = jnp.zeros_like(late)
    loop(LAYERS, layer)
    last = pltpu.make_async_copy(g, grad, gsem)
    last.start()
    for k in range(min(steps, 5) + 1, steps + 1):
        last_sums.step(k)
    late_sums[...] = late_held[steps]
    last.wait()


def backward(devices, lengths, wbuf, cotangent, gain_attn, gain_ffn, saved, rows, slots):
    count, width = cotangent.shape
    bf, f32 = jnp.bfloat16, jnp.float32
    blocks = slots // BLOCK
    steps = devices.bit_length() - 1
    any_ = pl.BlockSpec(memory_space=HBM)
    vm = pl.BlockSpec(memory_space=VMEM)
    return pl.pallas_call(
        functools.partial(backward_kernel, (rows, slots), devices),
        out_shape=(
            jax.ShapeDtypeStruct((count, width), f32),
            jax.ShapeDtypeStruct((LAYERS, EARLY, width), f32),
            jax.ShapeDtypeStruct((8, width), f32),
        ),
        in_specs=[pl.BlockSpec(memory_space=pltpu.SMEM), any_, any_, vm, vm] + [any_] * 5,
        out_specs=(any_, vm, vm),
        scratch_shapes=[
            VMEM((count, width), f32),
            VMEM((count, width), bf),
            VMEM((count, width), bf),
            VMEM((count, width), f32),
            VMEM((3, count, width), bf),
            VMEM((3, count, width), bf),
            VMEM((2, count, width), f32),
            VMEM((2, count, 128), f32),
            VMEM((2, count, WIDTH), bf),
            VMEM((3, width, WIDTH), bf),
            VMEM((2, blocks, WINDOW, 2 * BLOCK), bf),
            VMEM((slots, 128), f32),
            VMEM((slots, 128), f32),
            VMEM((EARLY, 8, width), f32),
            VMEM((8, 8, width), f32),
            VMEM((LAYERS, steps + 1, EARLY, width), f32),
            VMEM((LAYERS, steps, EARLY, width), f32),
            VMEM((steps + 1, 8, width), f32),
            VMEM((steps, 8, width), f32),
            DMA((3,)), DMA((2,)), DMA((2,)), DMA((2,)), DMA((2,)), DMA((3,)), DMA,
            DMA((LAYERS, steps)), DMA((LAYERS, steps)), DMA((steps,)), DMA((steps,)),
        ],
        compiler_params=pltpu.CompilerParams(
            vmem_limit_bytes=58 << 20, collective_id=1, has_side_effects=True
        ),
    )(lengths, wbuf, cotangent, gain_attn, gain_ffn, *saved)


def per_device(
    devices,
    tokens,
    lengths,
    w_query,
    w_key,
    w_value,
    w_out,
    w_inner,
    w_outer,
    bias_query,
    bias_value,
    bias_out,
    bias_inner,
    bias_outer,
    shift_attn,
    shift_ffn,
    gain_attn,
    gain_ffn,
    cotangent,
):
    rows, slots, width = tokens.shape
    hidden = bias_inner.shape[1]
    unit = w_query.shape[1]
    count = rows * slots
    vectors = (
        bias_query, bias_value, bias_out, bias_outer, shift_attn, shift_ffn, gain_attn, gain_ffn,
    )
    matrices = (w_query, w_key, w_value, w_out, w_inner, w_outer)
    wbuf, out, *saved = forward(
        devices, lengths, matrices, tokens.reshape(count, width), vectors, bias_inner, rows, slots
    )
    wbuf = wbuf.reshape(LAYERS * GROUPS, width, WIDTH)
    grad, sums, late = backward(
        devices, lengths, wbuf, cotangent.reshape(count, width), gain_attn, gain_ffn, saved, rows, slots
    )
    late = late.reshape(4, 2, width)[:LAYERS]
    grad_inner = sums[:, D_INNER:].reshape(LAYERS, hidden // width, devices, unit)
    grad_inner = grad_inner.transpose(0, 2, 1, 3).reshape(LAYERS, hidden)
    return (
        out.reshape(rows, slots, width),
        grad.reshape(rows, slots, width),
        late[:, 0],
        late[:, 1],
        sums[:, D_OUT],
        grad_inner,
        sums[:, D_OUTER],
        sums[:, D_ATTN],
        sums[:, D_FFN],
    )


def solution(mesh):
    rows, whole = P("dp", None, None), P()
    weight = P(None, "dp", None)
    placed = (rows, P("dp", None)) + (weight,) * 6 + (whole,) * 9 + (rows,)
    return jax.shard_map(
        functools.partial(per_device, mesh.shape["dp"]),
        mesh=mesh,
        in_specs=placed,
        out_specs=(rows, rows) + (whole,) * 7,
        check_vma=False,
    )
```

```python
import functools

import jax
import jax.numpy as jnp
from jax import lax
from jax.experimental import pallas as pl
from jax.experimental.pallas import tpu as pltpu
from jax.sharding import PartitionSpec as P

HEADS = 16
LAYERS = 2
EPSILON = 1e-12
NEGATIVE = -1e9
PADDING_ID = 1000
MESH = pl.DeviceIdType.MESH
HBM = pltpu.MemorySpace.HBM
VMEM = pltpu.VMEM
DMA = pltpu.SemaphoreType.DMA

WIDTH = 512
GROUPS = 24
AT_OUT, AT_INNER, AT_OUTER = 6, 8, 16
BLOCK = 128
WINDOW = 256
ROW_TILE = 128
ROOT_HALF = 0.7071067811865476
DENSITY = 0.3989422804014327
B_Q, B_V, B_OUT, B_OUTER, S_ATTN, S_FFN, G_ATTN, G_FFN = range(8)
D_OUT, D_OUTER, D_ATTN, D_FFN, D_INNER = range(5)
EARLY = 8


def chip_dims(devices):
    bits = (devices // 2).bit_length() - 1
    first = -(-bits // 3)
    second = -(-(bits - first) // 2)
    return (1 << first, 1 << second, 1 << (bits - first - second))


RELAY = 4
ORDERS = (((0, 4, 2, 1, 3), (1, 0, 4, 2, 3)), ((0, 4, 1, 2, 3), (2, 0, 4, 1, 3)))
SLOTS = 8


class Gather:
    def __init__(self, dims, own, buf, ssem, rsem, total):
        self.dims, self.own, self.buf = dims, own, buf
        self.ssem, self.rsem, self.total = ssem, rsem, total
        self.me = lax.axis_index("dp")
        _, n1, n2 = dims
        self.core = lax.rem(self.me, 2)
        chip = self.me // 2
        self.at = (chip // (n1 * n2), lax.rem(chip // n2, n1), lax.rem(chip, n2))
        self.step = (n1 * n2 * 2, n2 * 2, 2)
        self.relay = dims[0] == 4
        self.orders = ORDERS
        if not self.relay:
            self.orders = tuple(
                tuple(tuple(d for d in order if d != RELAY) for order in pair) for pair in ORDERS
            )
        self.phases = len(self.orders[0][0])
        rows, cols = own.shape[-2:]
        if rows % 16 == 0:
            half = rows // 2
            self.parts = tuple((pl.ds(c * half, half), pl.ds(0, cols)) for c in range(2))
        else:
            half = cols // 2
            self.parts = tuple((pl.ds(0, rows), pl.ds(c * half, half)) for c in range(2))

    def peers(self, dim):
        if dim == 3:
            return [self.me + 1 - 2 * self.core]
        out = []
        for d in range(1, self.dims[dim]):
            to = lax.rem(self.at[dim] + d, self.dims[dim])
            out.append(self.me + (to - self.at[dim]) * self.step[dim])
        return out

    def moves(self, g, par, s, p):
        order = self.orders[par][s]
        dim, full = order[p], order[:p]
        n0, n1, n2 = self.dims
        first = (0, n0, n0 + n1 - 1, n0 + n1 + n2 - 2, n0 - 1)[dim]
        where = [pl.ds(0, self.dims[d]) if d in full else self.at[d] for d in range(3)]
        slot = lax.rem(g, SLOTS)
        z = self.at[0]
        if dim == RELAY:
            middle = (z == 1) | (z == 2)
            where[0] = jnp.where(z < 2, 3, 0)
            targets = [self.me + (3 - where[0] - z) * self.step[0]]
            guards = [(middle, jnp.logical_not(middle))]
        else:
            targets = self.peers(dim)
            guards = [(None, None)] * len(targets)
            if dim == 0 and self.relay:
                guards = [
                    (jnp.abs(lax.rem(z + d, 4) - z) != 3, jnp.abs(lax.rem(z + 4 - d, 4) - z) != 3)
                    if d != 2
                    else (None, None)
                    for d in (1, 2, 3)
                ]
        sub = self.parts[s]
        dst = self.buf.at[(g,) + tuple(where) + (self.core,) + sub]
        src = self.own.at[(g,) + sub] if p == 0 else dst
        return [
            (
                pltpu.make_async_remote_copy(
                    src_ref=src,
                    dst_ref=dst,
                    send_sem=self.ssem.at[slot, s, first + i],
                    recv_sem=self.rsem.at[slot, s, first + i],
                    device_id=(to,),
                    device_id_type=MESH,
                ),
                *guard,
            )
            for i, (to, guard) in enumerate(zip(targets, guards))
        ]

    def greet(self):
        bar = pltpu.get_barrier_semaphore()
        for d in range(4):
            for to in self.peers(d):
                pl.semaphore_signal(bar, inc=1, device_id=(to,), device_id_type=MESH)

    def meet(self):
        pl.semaphore_wait(pltpu.get_barrier_semaphore(), sum(self.dims) - 3 + 1)

    def pump(self, pair_step, par):
        for p in range(self.phases, -1, -1):
            pair = pair_step - p

            @pl.when((pair >= 0) & (pair < self.total // 2))
            def _():
                g = 2 * pair + par
                for s in range(2):
                    if p > 0:
                        for copy, sends, receives in self.moves(g, par, s, p - 1):
                            if sends is None:
                                copy.wait()
                            else:
                                pl.when(sends)(copy.wait_send)
                                pl.when(receives)(copy.wait_recv)
                    if p < self.phases:
                        for copy, sends, _ in self.moves(g, par, s, p):
                            if sends is None:
                                copy.start()
                            else:
                                pl.when(sends)(copy.start)


def matmul(left, right):
    return jnp.dot(left, right, preferred_element_type=jnp.float32)


def matmul_nt(left, right):
    return lax.dot_general(
        left, right, (((1,), (1,)), ((), ())), preferred_element_type=jnp.float32
    )


def matmul_tn(left, right):
    return lax.dot_general(
        left, right, (((0,), (0,)), ((), ())), preferred_element_type=jnp.float32
    )


def loop(count, body):
    lax.fori_loop(0, count, lambda i, c: (body(i), c)[1], 0)


def tile(i, size):
    return pl.ds(pl.multiple_of(i * size, size), size)


def window_starts(slots):
    return [
        min(max(b * BLOCK - (WINDOW - BLOCK) // 2, 0), slots - WINDOW)
        for b in range(slots // BLOCK)
    ]


def pair_stack(rows):
    lane = lax.broadcasted_iota(jnp.int32, rows.shape, 1)
    zero = jnp.zeros_like(rows)
    half = rows.shape[1] // 2
    return jnp.concatenate(
        [jnp.where(lane < half, rows, zero), jnp.where(lane < half, zero, rows)], axis=0
    )


def pair_join(stacked):
    rows = stacked.shape[0] // 2
    lane = lax.broadcasted_iota(jnp.int32, (rows, stacked.shape[1]), 1)
    return jnp.where(lane < stacked.shape[1] // 2, stacked[:rows], stacked[rows:])


def permute_hidden(load, store, unit, hidden):
    devices = hidden // (4 * unit)
    for b in range(hidden // 128):
        block = None
        for piece in range(128 // unit):
            quarter, device = divmod(b * (128 // unit) + piece, devices)
            source = (4 * device + quarter) * unit
            x = load(source // 128)
            shift = (piece * unit - source) % 128
            if shift:
                x = pltpu.roll(x, shift, axis=1)
            if block is None:
                block = x
            else:
                lane = lax.broadcasted_iota(jnp.int32, x.shape, 1)
                block = jnp.where(lane >= piece * unit, x, block)
        store(b, block)


def store_block(own, first, b, x):
    per = WIDTH // 128
    own[first + b // per, :, b % per * 128 : (b % per + 1) * 128] = x.astype(own.dtype)


def slot_ids(lengths, r, position):
    segments = lengths.shape[1]
    number = jnp.zeros_like(position)
    end = jnp.int32(0)
    for j in range(segments):
        end = end + lengths[r, j]
        number = number + (position >= end).astype(jnp.int32)
    return jnp.where(number < segments - 1, number, PADDING_ID + position)


def forward_kernel(
    dims, devices_dims,
    lengths, w_query, w_key, w_value, w_out, w_inner, w_outer, tokens, *rest,
):
    vectors, rest = rest[:8], rest[8:]
    (
        inner_raw, wbuf, out, saved_qkv, saved_p, saved_x, saved_s, saved_d,
        h, a, qkv, o, z, u, w, p_stage, d_stage, x_stage, s_stage, own, id_row, id_col, inner_bias,
        wsem, psem, dsem, xsem, ssem, qsem, tsem, hsem, send_sem, recv_sem,
    ) = rest
    rows, slots = dims
    count = h.shape[0]
    pairs = HEADS // 2
    total = LAYERS * GROUPS
    gather = Gather(devices_dims, own, wbuf, send_sem, recv_sem, total)

    def wload(g):
        slot = lax.rem(g, 2)
        return pltpu.make_async_copy(wbuf.at[g], w.at[slot], wsem.at[slot])

    def weights(g):
        @pl.when(g + 1 < total)
        def _():
            wload(g + 1).start()

        wload(g).wait()
        return w[lax.rem(g, 2)].reshape(h.shape[1], WIDTH)

    def pump(half):
        for par in range(2):

            @pl.when(lax.rem(half, 2) == par)
            def _():
                gather.pump(half // 2 + gather.phases, par)

    gather.greet()
    load = pltpu.make_async_copy(tokens, a, tsem)
    load.start()
    unit = own.shape[1]

    def cast(l, m):
        matrix = (w_query, w_key, w_value, w_out)[m]
        for c in range(2):
            own[l * GROUPS + 2 * m + c] = matrix[l, :, tile(c, WIDTH)].astype(jnp.bfloat16)

    def start(i):
        for par in range(2):
            gather.pump(i, par)

    cast(0, 0)
    gather.meet()
    start(0)
    for l in range(LAYERS):
        at = l * GROUPS
        for m in range(4):
            if (l, m) != (0, 0):
                cast(l, m)
        for c in range(2):
            for kc in range(4):
                piece = w_outer[l, kc * unit : (kc + 1) * unit, c * WIDTH : (c + 1) * WIDTH]
                own[at + AT_OUTER + 4 * c + kc] = piece.astype(jnp.bfloat16)
        permute_hidden(
            lambda b: w_inner[l, :, b * 128 : (b + 1) * 128],
            lambda b, x: store_block(own, at + AT_INNER, b, x),
            unit,
            w_inner.shape[2],
        )
    here = pltpu.make_async_copy(
        own, wbuf.at[(pl.ds(0, total),) + gather.at + (gather.core,)], hsem
    )
    here.start()
    here.wait()
    start(1)

    def keep_bias(b, x):
        inner_bias[:, b * 128 : (b + 1) * 128] = x

    permute_hidden(
        lambda b: inner_raw[:, b * 128 : (b + 1) * 128], keep_bias, unit, w_inner.shape[2]
    )
    for r in range(rows):
        id_row[r] = slot_ids(lengths, r, lax.broadcasted_iota(jnp.int32, (8, slots), 1))
        id_col[r] = slot_ids(lengths, r, lax.broadcasted_iota(jnp.int32, (slots, 128), 0))
    load.wait()

    def widen(i):
        h[tile(i, ROW_TILE), :] = a[tile(i, ROW_TILE), :].astype(jnp.float32)

    loop(count // ROW_TILE, widen)

    for i in range(2, gather.phases):
        start(i)
    pump(0)
    wload(0).start()

    def normalize(l, which):
        bias, gain, shift = ((B_OUT, G_ATTN, S_ATTN), (B_OUTER, G_FFN, S_FFN))[which]
        store_x = pltpu.make_async_copy(x_stage, saved_x.at[l, which], xsem)
        store_s = pltpu.make_async_copy(s_stage, saved_s.at[l, which], ssem)
        if which == 1:
            store_x.wait()
            store_s.wait()
        else:

            @pl.when(l > 0)
            def _():
                store_x.wait()
                store_s.wait()

        def body(i):
            t = tile(i, ROW_TILE)
            r = h[t, :] + vectors[bias][pl.ds(l, 1), :]
            centered = r - jnp.mean(r, axis=1, keepdims=True)
            var = jnp.mean(centered * centered, axis=1, keepdims=True)
            scale = lax.rsqrt(var + EPSILON)
            xhat = centered * scale
            x_stage[t, :] = xhat
            s_stage[t, :] = jnp.broadcast_to(scale, (ROW_TILE, 128))
            y = xhat * vectors[gain][pl.ds(l, 1), :] + vectors[shift][pl.ds(l, 1), :]
            h[t, :] = y
            a[t, :] = y.astype(jnp.bfloat16)

        loop(count // ROW_TILE, body)
        store_x.start()
        store_s.start()

    def layer(l):
        base = l * GROUPS

        @pl.when(l > 0)
        def _():
            for m in range(3):
                pltpu.make_async_copy(qkv.at[m], saved_qkv.at[l, m], qsem.at[m]).wait()

        def project(i):
            pump(base + i + 1)
            m = i // 2
            cols = tile(i % 2, WIDTH)
            bias_q = vectors[B_Q][pl.ds(l, 1), cols]
            bias_v = vectors[B_V][pl.ds(l, 1), cols]
            bias = jnp.where(m == 0, bias_q, jnp.where(m == 1, jnp.zeros_like(bias_v), bias_v))
            y = matmul(a[...], weights(base + i)) + bias
            y = y * jnp.where(m == 0, jnp.float32((h.shape[1] // HEADS) ** -0.5), jnp.float32(1))
            qkv[m, :, cols] = y.astype(jnp.bfloat16)

        loop(6, project)
        for m in range(3):
            pltpu.make_async_copy(qkv.at[m], saved_qkv.at[l, m], qsem.at[m]).start()

        def attend(i):
            @pl.when(lax.rem(i, 3) == 0)
            def _():
                pump(base + 7 + i // 3)

            r = i // pairs
            lanes = tile(lax.rem(i, pairs), 128)
            slot = lax.rem(i, 2)
            store_p = pltpu.make_async_copy(p_stage.at[slot], saved_p.at[l, i], psem.at[slot])

            @pl.when((i >= 2) | (l > 0))
            def _():
                store_p.wait()

            top = pl.multiple_of(r * slots, slots)
            for b, start in enumerate(window_starts(slots)):
                qm = pair_stack(qkv[0, pl.ds(top + b * BLOCK, BLOCK), lanes])
                km = qkv[1, pl.ds(top + start, WINDOW), lanes]
                vm = qkv[2, pl.ds(top + start, WINDOW), lanes]
                same = id_col[r, start : start + WINDOW, :] == id_row[r, :1, b * BLOCK : (b + 1) * BLOCK]
                s = matmul_nt(km, qm)
                s = jnp.where(jnp.concatenate([same, same], axis=1), s, NEGATIVE)
                e = jnp.exp(s - jnp.max(s, axis=0, keepdims=True))
                p = e * (1.0 / jnp.sum(e, axis=0, keepdims=True))
                p = p.astype(jnp.bfloat16)
                p_stage[slot, b] = p
                o[pl.ds(top + b * BLOCK, BLOCK), lanes] = pair_join(matmul_tn(p, vm)).astype(jnp.bfloat16)
            store_p.start()

        loop(rows * pairs, attend)

        def attn_out(i):
            pump(base + 13 + i)
            cols = tile(i, WIDTH)
            h[:, cols] += matmul(o[...], weights(base + AT_OUT + i))

        loop(2, attn_out)
        normalize(l, 0)

        def inner(i):
            @pl.when(lax.rem(i, 4) < 3)
            def _():
                pump(base + 15 + i - i // 4)

            cols = tile(i, WIDTH)
            u[...] = matmul(a[...], weights(base + AT_INNER + i)) + inner_bias[pl.ds(l, 1), cols]
            slot = lax.rem(i, 2)
            store_d = pltpu.make_async_copy(d_stage.at[slot], saved_d.at[l, i], dsem.at[slot])

            @pl.when((i >= 2) | (l > 0))
            def _():
                store_d.wait()

            def activate(t):
                part = tile(t, ROW_TILE)
                x = u[part, :]
                cdf = 0.5 + 0.5 * lax.erf(x * ROOT_HALF)
                z[i // 2, part, tile(i % 2, WIDTH)] = (x * cdf).astype(jnp.bfloat16)
                slope = cdf + x * (DENSITY * jnp.exp(-0.5 * x * x))
                d_stage[slot, part, :] = slope.astype(jnp.bfloat16)

            loop(count // ROW_TILE, activate)
            store_d.start()

        loop(8, inner)

        def outer(i):
            @pl.when((lax.rem(i, 2) == 0) & (i > 0))
            def _():
                pump(base + 20 + i // 2)

            @pl.when(i == 7)
            def _():
                pump(base + 24)

            cols = tile(i // 4, WIDTH)
            h[:, cols] += matmul(z[lax.rem(i, 4)], weights(base + AT_OUTER + i))

        loop(8, outer)
        normalize(l, 1)

    loop(LAYERS, layer)
    store = pltpu.make_async_copy(a, out, tsem)
    store.start()
    last = LAYERS - 1
    for m in range(3):
        pltpu.make_async_copy(qkv.at[m], saved_qkv.at[last, m], qsem.at[m]).wait()
    for i in range(2):
        pltpu.make_async_copy(p_stage.at[i], saved_p.at[last, i], psem.at[i]).wait()
        pltpu.make_async_copy(d_stage.at[i], saved_d.at[last, i], dsem.at[i]).wait()
    pltpu.make_async_copy(x_stage, saved_x.at[last, 1], xsem).wait()
    pltpu.make_async_copy(s_stage, saved_s.at[last, 1], ssem).wait()
    store.wait()


def forward(devices, lengths, matrices, tokens, vectors, inner_bias, rows, slots):
    count, width = tokens.shape
    hidden = inner_bias.shape[-1]
    unit = matrices[0].shape[1]
    bf, f32 = jnp.bfloat16, jnp.float32
    blocks = slots // BLOCK
    devices_dims = chip_dims(devices)
    held = devices_dims + (2, unit, WIDTH)
    sems = sum(devices_dims) - 1
    any_ = pl.BlockSpec(memory_space=HBM)
    vm = pl.BlockSpec(memory_space=VMEM)
    return pl.pallas_call(
        functools.partial(forward_kernel, (rows, slots), devices_dims),
        out_shape=(
            jax.ShapeDtypeStruct((LAYERS * GROUPS,) + held, bf),
            jax.ShapeDtypeStruct((count, width), bf),
            jax.ShapeDtypeStruct((LAYERS, 3, count, width), bf),
            jax.ShapeDtypeStruct((LAYERS, rows * HEADS // 2, blocks, WINDOW, 2 * BLOCK), bf),
            jax.ShapeDtypeStruct((LAYERS, 2, count, width), f32),
            jax.ShapeDtypeStruct((LAYERS, 2, count, 128), f32),
            jax.ShapeDtypeStruct((LAYERS, hidden // WIDTH, count, WIDTH), bf),
        ),
        in_specs=[pl.BlockSpec(memory_space=pltpu.SMEM)] + [vm] * 6 + [any_] + [vm] * 9,
        out_specs=(any_,) * 7,
        scratch_shapes=[
            VMEM((count, width), f32),
            VMEM((count, width), bf),
            VMEM((3, count, width), bf),
            VMEM((count, width), bf),
            VMEM((hidden // width, count, width), bf),
            VMEM((count, WIDTH), f32),
            VMEM((2,) + held, bf),
            VMEM((2, blocks, WINDOW, 2 * BLOCK), bf),
            VMEM((2, count, WIDTH), bf),
            VMEM((count, width), f32),
            VMEM((count, 128), f32),
            VMEM((LAYERS * GROUPS, unit, WIDTH), bf),
            VMEM((rows, 8, slots), jnp.int32),
            VMEM((rows, slots, 128), jnp.int32),
            VMEM((LAYERS, hidden), f32),
            DMA((2,)), DMA((2,)), DMA((2,)), DMA, DMA, DMA((3,)), DMA, DMA,
            DMA((SLOTS, 2, sems)), DMA((SLOTS, 2, sems)),
        ],
        compiler_params=pltpu.CompilerParams(
            vmem_limit_bytes=58 << 20, collective_id=0, has_side_effects=True
        ),
    )(lengths, *matrices, tokens, *vectors, inner_bias)


class Exchange:
    def __init__(self, mates, held, got, ssem, rsem):
        self.mates, self.held, self.got = mates, held, got
        self.ssem, self.rsem = ssem, rsem

    def copy(self, k):
        return pltpu.make_async_remote_copy(
            src_ref=self.held.at[k],
            dst_ref=self.got.at[k],
            send_sem=self.ssem.at[k],
            recv_sem=self.rsem.at[k],
            device_id=(self.mates[k],),
            device_id_type=MESH,
        )

    def step(self, k):
        if k > 0:
            self.copy(k - 1).wait()
            self.held[k] = self.held[k - 1] + self.got[k - 1]
        if k < len(self.mates):
            self.copy(k).start()


def fold(x):
    rows, width = x.shape
    return jnp.sum(x.reshape(rows // 8, 8, width), axis=0)


def backward_kernel(
    dims, devices,
    lengths, wbuf, cotangent, gain_attn, gain_ffn, saved_qkv, saved_p, saved_x, saved_s, saved_d,
    grad, sums, late_sums,
    g, db, du, dh, qkv, dqkv, x, sc, d, w, p, dk, dv, part, late,
    held, got, late_held, late_got,
    wsem, psem, dsem, xsem, ssem, qsem, gsem, send_sem, recv_sem, late_send, late_recv,
):
    rows, slots = dims
    count, width = g.shape
    pairs = HEADS // 2
    total = LAYERS * GROUPS
    items = rows * pairs

    def block_of(i):
        l = LAYERS - 1 - i // GROUPS
        j = lax.rem(i, GROUPS)
        quarter, within = j // 4, lax.rem(j, 4)
        ffn = jnp.where(within < 2, AT_OUTER + 4 * within + quarter, AT_INNER + 2 * quarter + within - 2)
        late = jnp.where(j < 18, AT_OUT + j - 16, j - 18)
        return l * GROUPS + jnp.where(j < 16, ffn, late)

    def wload(i):
        slot = lax.rem(i, 3)
        return pltpu.make_async_copy(wbuf.at[block_of(i)], w.at[slot], wsem.at[slot])

    def weights(i):
        @pl.when(i + 2 < total)
        def _():
            wload(i + 2).start()

        wload(i).wait()
        return lax.rem(i, 3)

    def xload(l, which):
        return (
            pltpu.make_async_copy(saved_x.at[l, which], x.at[which], xsem.at[which]),
            pltpu.make_async_copy(saved_s.at[l, which], sc.at[which], ssem.at[which]),
        )

    def dload(l, i):
        slot = lax.rem(i, 2)
        return pltpu.make_async_copy(saved_d.at[l, i], d.at[slot], dsem.at[slot])

    def pload(l, i):
        slot = lax.rem(i, 2)
        return pltpu.make_async_copy(saved_p.at[l, i], p.at[slot], psem.at[slot])

    def qload(l):
        return [pltpu.make_async_copy(saved_qkv.at[l, m], qkv.at[m], qsem.at[m]) for m in range(3)]

    top_layer = LAYERS - 1
    first = pltpu.make_async_copy(cotangent, db, gsem)
    first.start()
    for which in (1, 0):
        for c in xload(top_layer, which):
            c.start()
    wload(0).start()
    wload(1).start()
    dload(top_layer, 0).start()
    me = lax.axis_index("dp")
    steps = devices.bit_length() - 1
    mates = [me + (1 << k) - 2 * (1 << k) * lax.rem(me // (1 << k), 2) for k in range(steps)]
    barrier = pltpu.get_barrier_semaphore()
    for to in mates:
        pl.semaphore_signal(barrier, inc=1, device_id=(to,), device_id_type=MESH)
    first.wait()
    for r in range(rows):
        real = slots - lengths[r, lengths.shape[1] - 1]

        def widen(i):
            t = pl.ds(pl.multiple_of(r * slots + i * ROW_TILE, ROW_TILE), ROW_TILE)
            slot = i * ROW_TILE + lax.broadcasted_iota(jnp.int32, (ROW_TILE, width), 0)
            g[t, :] = jnp.where(slot < real, db[t, :].astype(jnp.float32), 0.0)

        loop(slots // ROW_TILE, widen)
    pl.semaphore_wait(barrier, steps)

    def normalize_back(l, which):
        gain = (gain_attn, gain_ffn)[which]
        row_shift = (D_ATTN, D_FFN)[which]
        row_bias = (D_OUT, D_OUTER)[which]
        for c in xload(l, which):
            c.wait()

        def body(i, carry):
            t = tile(i, ROW_TILE)
            up = g[t, :]
            xh = x[which, t, :]
            scaled = up * gain[pl.ds(l, 1), :]
            m1 = jnp.mean(scaled, axis=1, keepdims=True)
            m2 = jnp.mean(scaled * xh, axis=1, keepdims=True)
            down = sc[which, t, :1] * (scaled - m1 - xh * m2)
            g[t, :] = down
            low = down.astype(jnp.bfloat16)
            db[t, :] = low
            return carry[0] + fold(up), carry[1] + fold(low.astype(jnp.float32))

        zero = jnp.zeros((8, width), jnp.float32)
        shift_sum, bias_sum = lax.fori_loop(0, count // ROW_TILE, body, (zero, zero))
        part[row_shift] = shift_sum
        part[row_bias] = bias_sum

        @pl.when(l > 0)
        def _():
            for c in xload(l - 1, which):
                c.start()

    def layer(step):
        l = top_layer - step
        base = step * GROUPS
        for c in qload(l):
            c.start()
        normalize_back(l, 1)

        def quarter(kc):
            at = base + 4 * kc
            slot = weights(at)
            for c in range(width // 256):
                n = slice(c * 256, (c + 1) * 256)
                dh[:, n] = matmul_nt(db[:, :WIDTH], w[slot, n, :])
            slot = weights(at + 1)
            for c in range(width // 256):
                n = slice(c * 256, (c + 1) * 256)
                dh[:, n] += matmul_nt(db[:, WIDTH:], w[slot, n, :])

            total_ = []
            for half in range(2):
                i = 2 * kc + half

                @pl.when(i + 1 < 8)
                def _():
                    dload(l, i + 1).start()

                dload(l, i).wait()

                def slope(t, carry):
                    tl = tile(t, ROW_TILE)
                    cols = pl.ds(half * WIDTH, WIDTH)
                    low = (dh[tl, cols] * d[half, tl, :].astype(jnp.float32)).astype(jnp.bfloat16)
                    du[tl, cols] = low
                    return carry + fold(low.astype(jnp.float32))

                total_.append(
                    lax.fori_loop(0, count // ROW_TILE, slope, jnp.zeros((8, WIDTH), jnp.float32))
                )
            part[D_INNER + kc] = jnp.concatenate(total_, axis=1)

            def into(half):
                slot = weights(at + 2 + half)
                for c in range(width // 256):
                    n = slice(c * 256, (c + 1) * 256)
                    g[:, n] += matmul_nt(du[:, tile(half, WIDTH)], w[slot, n, :])

            loop(2, into)

        loop(4, quarter)

        @pl.when(l > 0)
        def _():
            dload(l - 1, 0).start()

        pload(l, 0).start()
        normalize_back(l, 0)

        slot = weights(base + 16)
        for c in range(width // 256):
            n = slice(c * 256, (c + 1) * 256)
            dh[:, n] = matmul_nt(db[:, :WIDTH], w[slot, n, :])
        slot = weights(base + 17)
        for c in range(width // 256):
            n = slice(c * 256, (c + 1) * 256)
            du[:, n] = (dh[:, n] + matmul_nt(db[:, WIDTH:], w[slot, n, :])).astype(jnp.bfloat16)
        for c in qload(l):
            c.wait()

        early = Exchange(mates, held.at[l], got.at[l], send_sem.at[l], recv_sem.at[l])
        held[l, 0] = jnp.sum(part[...], axis=1)
        early.step(0)
        apart = (items - 1) // steps

        def attend(i):
            for k in range(1, steps + 1):

                @pl.when(i == k * apart)
                def _():
                    early.step(k)

            r = i // pairs
            lanes = tile(lax.rem(i, pairs), 128)
            slot = lax.rem(i, 2)

            @pl.when(i + 1 < items)
            def _():
                pload(l, i + 1).start()

            pload(l, i).wait()
            dk[...] = jnp.zeros_like(dk)
            dv[...] = jnp.zeros_like(dv)
            top = pl.multiple_of(r * slots, slots)
            for b, start in enumerate(window_starts(slots)):
                mine = pl.ds(top + b * BLOCK, BLOCK)
                reach = pl.ds(top + start, WINDOW)
                qm = pair_stack(qkv[0, mine, lanes])
                om = pair_stack(du[mine, lanes])
                pb = p[slot, b]
                pf = pb.astype(jnp.float32)
                dp = matmul_nt(qkv[2, reach, lanes], om)
                weighted = pf * dp
                ds = weighted - pf * jnp.sum(weighted, axis=0, keepdims=True)
                ds = ds.astype(jnp.bfloat16)
                dk[start : start + WINDOW, :] += matmul(ds, qm)
                dv[start : start + WINDOW, :] += matmul(pb, om)
                dq = pair_join(matmul_tn(ds, qkv[1, reach, lanes]))
                dqkv[0, mine, lanes] = (dq * (width // HEADS) ** -0.5).astype(jnp.bfloat16)
            every = pl.ds(top, slots)
            dqkv[1, every, lanes] = dk[...].astype(jnp.bfloat16)
            dqkv[2, every, lanes] = dv[...].astype(jnp.bfloat16)

        loop(items, attend)

        sums[l] = held[l, steps]
        for m, row in ((0, 0), (2, 1)):

            def add(t, carry):
                return carry + fold(dqkv[m, tile(t, ROW_TILE), :].astype(jnp.float32))

            late[2 * l + row] = lax.fori_loop(
                0, count // ROW_TILE, add, jnp.zeros((8, width), jnp.float32)
            )

        @pl.when(l == 0)
        def _():
            late_held[0] = jnp.sum(late[...], axis=1)
            last_sums.step(0)

        def project(i):
            for k in range(1, min(steps, 5) + 1):

                @pl.when((l == 0) & (i == k))
                def _():
                    last_sums.step(k)

            slot = weights(base + 18 + i)
            for c in range(width // 256):
                n = slice(c * 256, (c + 1) * 256)
                g[:, n] += matmul_nt(dqkv[i // 2, :, tile(lax.rem(i, 2), WIDTH)], w[slot, n, :])

        loop(6, project)

    last_sums = Exchange(mates, late_held, late_got, late_send, late_recv)
    late[...] = jnp.zeros_like(late)
    loop(LAYERS, layer)
    last = pltpu.make_async_copy(g, grad, gsem)
    last.start()
    for k in range(min(steps, 5) + 1, steps + 1):
        last_sums.step(k)
    late_sums[...] = late_held[steps]
    last.wait()


def backward(devices, lengths, wbuf, cotangent, gain_attn, gain_ffn, saved, rows, slots):
    count, width = cotangent.shape
    bf, f32 = jnp.bfloat16, jnp.float32
    blocks = slots // BLOCK
    steps = devices.bit_length() - 1
    any_ = pl.BlockSpec(memory_space=HBM)
    vm = pl.BlockSpec(memory_space=VMEM)
    return pl.pallas_call(
        functools.partial(backward_kernel, (rows, slots), devices),
        out_shape=(
            jax.ShapeDtypeStruct((count, width), f32),
            jax.ShapeDtypeStruct((LAYERS, EARLY, width), f32),
            jax.ShapeDtypeStruct((8, width), f32),
        ),
        in_specs=[pl.BlockSpec(memory_space=pltpu.SMEM), any_, any_, vm, vm] + [any_] * 5,
        out_specs=(any_, vm, vm),
        scratch_shapes=[
            VMEM((count, width), f32),
            VMEM((count, width), bf),
            VMEM((count, width), bf),
            VMEM((count, width), f32),
            VMEM((3, count, width), bf),
            VMEM((3, count, width), bf),
            VMEM((2, count, width), f32),
            VMEM((2, count, 128), f32),
            VMEM((2, count, WIDTH), bf),
            VMEM((3, width, WIDTH), bf),
            VMEM((2, blocks, WINDOW, 2 * BLOCK), bf),
            VMEM((slots, 128), f32),
            VMEM((slots, 128), f32),
            VMEM((EARLY, 8, width), f32),
            VMEM((8, 8, width), f32),
            VMEM((LAYERS, steps + 1, EARLY, width), f32),
            VMEM((LAYERS, steps, EARLY, width), f32),
            VMEM((steps + 1, 8, width), f32),
            VMEM((steps, 8, width), f32),
            DMA((3,)), DMA((2,)), DMA((2,)), DMA((2,)), DMA((2,)), DMA((3,)), DMA,
            DMA((LAYERS, steps)), DMA((LAYERS, steps)), DMA((steps,)), DMA((steps,)),
        ],
        compiler_params=pltpu.CompilerParams(
            vmem_limit_bytes=58 << 20, collective_id=1, has_side_effects=True
        ),
    )(lengths, wbuf, cotangent, gain_attn, gain_ffn, *saved)


def finish_kernel(unit, sums, late, query, value, out, inner, outer, attn, ffn):
    width = sums.shape[2]
    devices = width // unit
    for l in range(LAYERS):
        here = slice(l, l + 1)
        for row, ref in ((D_OUT, out), (D_OUTER, outer), (D_ATTN, attn), (D_FFN, ffn)):
            ref[here, :] = sums[l, row : row + 1, :]
        query[here, :] = late[2 * l : 2 * l + 1, :]
        value[here, :] = late[2 * l + 1 : 2 * l + 2, :]
        for b in range(inner.shape[1] // 128):
            block = None
            for piece in range(128 // unit):
                device, quarter = divmod(b * (128 // unit) + piece, inner.shape[1] // width)
                source = device * unit
                row = D_INNER + quarter
                first = source // 128 * 128
                x = sums[l, row : row + 1, first : first + 128]
                shift = (piece * unit - source) % 128
                if shift:
                    x = pltpu.roll(x, shift, axis=1)
                if block is None:
                    block = x
                else:
                    lane = lax.broadcasted_iota(jnp.int32, x.shape, 1)
                    block = jnp.where(lane >= piece * unit, x, block)
            inner[here, b * 128 : (b + 1) * 128] = block


def finish(unit, hidden, sums, late):
    width = sums.shape[2]
    vm = pl.BlockSpec(memory_space=VMEM)
    sizes = (width, width, width, hidden, width, width, width)
    return pl.pallas_call(
        functools.partial(finish_kernel, unit),
        out_shape=tuple(jax.ShapeDtypeStruct((LAYERS, n), jnp.float32) for n in sizes),
        in_specs=[vm, vm],
        out_specs=(vm,) * 7,
    )(sums, late)


def per_device(
    devices,
    tokens,
    lengths,
    w_query,
    w_key,
    w_value,
    w_out,
    w_inner,
    w_outer,
    bias_query,
    bias_value,
    bias_out,
    bias_inner,
    bias_outer,
    shift_attn,
    shift_ffn,
    gain_attn,
    gain_ffn,
    cotangent,
):
    rows, slots, width = tokens.shape
    hidden = bias_inner.shape[1]
    unit = w_query.shape[1]
    count = rows * slots
    vectors = (
        bias_query, bias_value, bias_out, bias_outer, shift_attn, shift_ffn, gain_attn, gain_ffn,
    )
    matrices = (w_query, w_key, w_value, w_out, w_inner, w_outer)
    wbuf, out, *saved = forward(
        devices, lengths, matrices, tokens.reshape(count, width), vectors, bias_inner, rows, slots
    )
    wbuf = wbuf.reshape(LAYERS * GROUPS, width, WIDTH)
    grad, sums, late = backward(
        devices, lengths, wbuf, cotangent.reshape(count, width), gain_attn, gain_ffn, saved, rows, slots
    )
    return (
        out.reshape(rows, slots, width),
        grad.reshape(rows, slots, width),
        *finish(unit, hidden, sums, late),
    )


def solution(mesh):
    rows, whole = P("dp", None, None), P()
    weight = P(None, "dp", None)
    placed = (rows, P("dp", None)) + (weight,) * 6 + (whole,) * 9 + (rows,)
    return jax.shard_map(
        functools.partial(per_device, mesh.shape["dp"]),
        mesh=mesh,
        in_specs=placed,
        out_specs=(rows, rows) + (whole,) * 7,
        check_vma=False,
    )
```

```python
import functools

import jax
import jax.numpy as jnp
from jax import lax
from jax.experimental import pallas as pl
from jax.experimental.pallas import tpu as pltpu
from jax.sharding import PartitionSpec as P

HEADS = 16
LAYERS = 2
EPSILON = 1e-12
NEGATIVE = -1e9
PADDING_ID = 1000
MESH = pl.DeviceIdType.MESH
HBM = pltpu.MemorySpace.HBM
VMEM = pltpu.VMEM
DMA = pltpu.SemaphoreType.DMA

WIDTH = 512
GROUPS = 24
AT_OUT, AT_INNER, AT_OUTER = 6, 8, 16
BLOCK = 128
WINDOW = 256
ROW_TILE = 128
ROOT_HALF = 0.7071067811865476
DENSITY = 0.3989422804014327
B_Q, B_V, B_OUT, B_OUTER, S_ATTN, S_FFN, G_ATTN, G_FFN = range(8)
D_OUT, D_OUTER, D_ATTN, D_FFN, D_INNER = range(5)
EARLY = 8


def chip_dims(devices):
    bits = (devices // 2).bit_length() - 1
    first = -(-bits // 3)
    second = -(-(bits - first) // 2)
    return (1 << first, 1 << second, 1 << (bits - first - second))


RELAY = 4
ORDERS = (((0, 4, 2, 1, 3), (1, 0, 4, 2, 3)), ((0, 4, 1, 2, 3), (2, 0, 4, 1, 3)))
SLOTS = 8


class Gather:
    def __init__(self, dims, own, buf, ssem, rsem, total):
        self.dims, self.own, self.buf = dims, own, buf
        self.ssem, self.rsem, self.total = ssem, rsem, total
        self.me = lax.axis_index("dp")
        _, n1, n2 = dims
        self.core = lax.rem(self.me, 2)
        chip = self.me // 2
        self.at = (chip // (n1 * n2), lax.rem(chip // n2, n1), lax.rem(chip, n2))
        self.step = (n1 * n2 * 2, n2 * 2, 2)
        self.relay = dims[0] == 4
        self.orders = ORDERS
        if not self.relay:
            self.orders = tuple(
                tuple(tuple(d for d in order if d != RELAY) for order in pair) for pair in ORDERS
            )
        self.phases = len(self.orders[0][0])
        rows, cols = own.shape[-2:]
        if rows % 16 == 0:
            half = rows // 2
            self.parts = tuple((pl.ds(c * half, half), pl.ds(0, cols)) for c in range(2))
        else:
            half = cols // 2
            self.parts = tuple((pl.ds(0, rows), pl.ds(c * half, half)) for c in range(2))

    def peers(self, dim):
        if dim == 3:
            return [self.me + 1 - 2 * self.core]
        out = []
        for d in range(1, self.dims[dim]):
            to = lax.rem(self.at[dim] + d, self.dims[dim])
            out.append(self.me + (to - self.at[dim]) * self.step[dim])
        return out

    def moves(self, g, par, s, p):
        order = self.orders[par][s]
        dim, full = order[p], order[:p]
        n0, n1, n2 = self.dims
        first = (0, n0, n0 + n1 - 1, n0 + n1 + n2 - 2, n0 - 1)[dim]
        where = [pl.ds(0, self.dims[d]) if d in full else self.at[d] for d in range(3)]
        slot = lax.rem(g, SLOTS)
        z = self.at[0]
        if dim == RELAY:
            middle = (z == 1) | (z == 2)
            where[0] = jnp.where(z < 2, 3, 0)
            targets = [self.me + (3 - where[0] - z) * self.step[0]]
            guards = [(middle, jnp.logical_not(middle))]
        else:
            targets = self.peers(dim)
            guards = [(None, None)] * len(targets)
            if dim == 0 and self.relay:
                guards = [
                    (jnp.abs(lax.rem(z + d, 4) - z) != 3, jnp.abs(lax.rem(z + 4 - d, 4) - z) != 3)
                    if d != 2
                    else (None, None)
                    for d in (1, 2, 3)
                ]
        sub = self.parts[s]
        dst = self.buf.at[(g,) + tuple(where) + (self.core,) + sub]
        src = self.own.at[(g,) + sub] if p == 0 else dst
        return [
            (
                pltpu.make_async_remote_copy(
                    src_ref=src,
                    dst_ref=dst,
                    send_sem=self.ssem.at[slot, s, first + i],
                    recv_sem=self.rsem.at[slot, s, first + i],
                    device_id=(to,),
                    device_id_type=MESH,
                ),
                *guard,
            )
            for i, (to, guard) in enumerate(zip(targets, guards))
        ]

    def greet(self):
        bar = pltpu.get_barrier_semaphore()
        for d in range(4):
            for to in self.peers(d):
                pl.semaphore_signal(bar, inc=1, device_id=(to,), device_id_type=MESH)

    def meet(self):
        pl.semaphore_wait(pltpu.get_barrier_semaphore(), sum(self.dims) - 3 + 1)

    def pump(self, pair_step, par):
        for p in range(self.phases, -1, -1):
            pair = pair_step - p

            @pl.when((pair >= 0) & (pair < self.total // 2))
            def _():
                g = 2 * pair + par
                for s in range(2):
                    if p > 0:
                        for copy, sends, receives in self.moves(g, par, s, p - 1):
                            if sends is None:
                                copy.wait()
                            else:
                                pl.when(sends)(copy.wait_send)
                                pl.when(receives)(copy.wait_recv)
                    if p < self.phases:
                        for copy, sends, _ in self.moves(g, par, s, p):
                            if sends is None:
                                copy.start()
                            else:
                                pl.when(sends)(copy.start)


def matmul(left, right):
    return jnp.dot(left, right, preferred_element_type=jnp.float32)


def matmul_nt(left, right):
    return lax.dot_general(
        left, right, (((1,), (1,)), ((), ())), preferred_element_type=jnp.float32
    )


def matmul_tn(left, right):
    return lax.dot_general(
        left, right, (((0,), (0,)), ((), ())), preferred_element_type=jnp.float32
    )


def loop(count, body):
    lax.fori_loop(0, count, lambda i, c: (body(i), c)[1], 0)


def tile(i, size):
    return pl.ds(pl.multiple_of(i * size, size), size)


def window_starts(slots):
    return [
        min(max(b * BLOCK - (WINDOW - BLOCK) // 2, 0), slots - WINDOW)
        for b in range(slots // BLOCK)
    ]


def pair_stack(rows):
    lane = lax.broadcasted_iota(jnp.int32, rows.shape, 1)
    zero = jnp.zeros_like(rows)
    half = rows.shape[1] // 2
    return jnp.concatenate(
        [jnp.where(lane < half, rows, zero), jnp.where(lane < half, zero, rows)], axis=0
    )


def pair_join(stacked):
    rows = stacked.shape[0] // 2
    lane = lax.broadcasted_iota(jnp.int32, (rows, stacked.shape[1]), 1)
    return jnp.where(lane < stacked.shape[1] // 2, stacked[:rows], stacked[rows:])


def permute_hidden(load, store, unit, hidden):
    devices = hidden // (4 * unit)
    for b in range(hidden // 128):
        block = None
        for piece in range(128 // unit):
            quarter, device = divmod(b * (128 // unit) + piece, devices)
            source = (4 * device + quarter) * unit
            x = load(source // 128)
            shift = (piece * unit - source) % 128
            if shift:
                x = pltpu.roll(x, shift, axis=1)
            if block is None:
                block = x
            else:
                lane = lax.broadcasted_iota(jnp.int32, x.shape, 1)
                block = jnp.where(lane >= piece * unit, x, block)
        store(b, block)


def store_block(own, first, b, x):
    per = WIDTH // 128
    own[first + b // per, :, b % per * 128 : (b % per + 1) * 128] = x.astype(own.dtype)


def slot_ids(lengths, r, position):
    segments = lengths.shape[1]
    number = jnp.zeros_like(position)
    end = jnp.int32(0)
    for j in range(segments):
        end = end + lengths[r, j]
        number = number + (position >= end).astype(jnp.int32)
    return jnp.where(number < segments - 1, number, PADDING_ID + position)


def forward_kernel(
    dims, devices_dims,
    lengths, w_query, w_key, w_value, w_out, w_inner, w_outer, tokens, *rest,
):
    vectors, rest = rest[:8], rest[8:]
    (
        inner_raw, wbuf, out, saved_qkv, saved_p, saved_x, saved_s, saved_d,
        h, a, qkv, o, z, u, w, p_stage, d_stage, x_stage, s_stage, own, id_row, id_col, inner_bias,
        wsem, psem, dsem, xsem, ssem, qsem, tsem, hsem, send_sem, recv_sem,
    ) = rest
    rows, slots = dims
    count = h.shape[0]
    pairs = HEADS // 2
    total = LAYERS * GROUPS
    gather = Gather(devices_dims, own, wbuf, send_sem, recv_sem, total)

    def wload(g):
        slot = lax.rem(g, 2)
        return pltpu.make_async_copy(wbuf.at[g], w.at[slot], wsem.at[slot])

    def weights(g):
        @pl.when(g + 1 < total)
        def _():
            wload(g + 1).start()

        wload(g).wait()
        return w[lax.rem(g, 2)].reshape(h.shape[1], WIDTH)

    def pump(half):
        for par in range(2):

            @pl.when(lax.rem(half, 2) == par)
            def _():
                gather.pump(half // 2 + gather.phases, par)

    gather.greet()
    load = pltpu.make_async_copy(tokens, a, tsem)
    load.start()
    unit = own.shape[1]

    def cast(l, m):
        matrix = (w_query, w_key, w_value, w_out)[m]
        for c in range(2):
            own[l * GROUPS + 2 * m + c] = matrix[l, :, tile(c, WIDTH)].astype(jnp.bfloat16)

    def start(i):
        for par in range(2):
            gather.pump(i, par)

    cast(0, 0)
    gather.meet()
    start(0)
    for l in range(LAYERS):
        at = l * GROUPS
        for m in range(4):
            if (l, m) != (0, 0):
                cast(l, m)
        for c in range(2):
            for kc in range(4):
                piece = w_outer[l, kc * unit : (kc + 1) * unit, c * WIDTH : (c + 1) * WIDTH]
                own[at + AT_OUTER + 4 * c + kc] = piece.astype(jnp.bfloat16)
        permute_hidden(
            lambda b: w_inner[l, :, b * 128 : (b + 1) * 128],
            lambda b, x: store_block(own, at + AT_INNER, b, x),
            unit,
            w_inner.shape[2],
        )
    here = pltpu.make_async_copy(
        own, wbuf.at[(pl.ds(0, total),) + gather.at + (gather.core,)], hsem
    )
    here.start()
    here.wait()
    start(1)

    def keep_bias(b, x):
        inner_bias[:, b * 128 : (b + 1) * 128] = x

    permute_hidden(
        lambda b: inner_raw[:, b * 128 : (b + 1) * 128], keep_bias, unit, w_inner.shape[2]
    )
    for r in range(rows):
        id_row[r] = slot_ids(lengths, r, lax.broadcasted_iota(jnp.int32, (8, slots), 1))
        id_col[r] = slot_ids(lengths, r, lax.broadcasted_iota(jnp.int32, (slots, 128), 0))
    load.wait()

    def widen(i):
        h[tile(i, ROW_TILE), :] = a[tile(i, ROW_TILE), :].astype(jnp.float32)

    loop(count // ROW_TILE, widen)

    for i in range(2, gather.phases):
        start(i)
    pump(0)
    wload(0).start()

    def normalize(l, which):
        bias, gain, shift = ((B_OUT, G_ATTN, S_ATTN), (B_OUTER, G_FFN, S_FFN))[which]
        store_x = pltpu.make_async_copy(x_stage, saved_x.at[l, which], xsem)
        store_s = pltpu.make_async_copy(s_stage, saved_s.at[l, which], ssem)
        if which == 1:
            store_x.wait()
            store_s.wait()
        else:

            @pl.when(l > 0)
            def _():
                store_x.wait()
                store_s.wait()

        def body(i):
            t = tile(i, ROW_TILE)
            r = h[t, :] + vectors[bias][pl.ds(l, 1), :]
            centered = r - jnp.mean(r, axis=1, keepdims=True)
            var = jnp.mean(centered * centered, axis=1, keepdims=True)
            scale = lax.rsqrt(var + EPSILON)
            xhat = centered * scale
            x_stage[t, :] = xhat
            s_stage[t, :] = jnp.broadcast_to(scale, (ROW_TILE, 128))
            y = xhat * vectors[gain][pl.ds(l, 1), :] + vectors[shift][pl.ds(l, 1), :]
            h[t, :] = y
            a[t, :] = y.astype(jnp.bfloat16)

        loop(count // ROW_TILE, body)
        store_x.start()
        store_s.start()

    def layer(l):
        base = l * GROUPS

        @pl.when(l > 0)
        def _():
            for m in range(3):
                pltpu.make_async_copy(qkv.at[m], saved_qkv.at[l, m], qsem.at[m]).wait()

        def project(i):
            pump(base + i + 1)
            m = i // 2
            cols = tile(i % 2, WIDTH)
            bias_q = vectors[B_Q][pl.ds(l, 1), cols]
            bias_v = vectors[B_V][pl.ds(l, 1), cols]
            bias = jnp.where(m == 0, bias_q, jnp.where(m == 1, jnp.zeros_like(bias_v), bias_v))
            y = matmul(a[...], weights(base + i)) + bias
            y = y * jnp.where(m == 0, jnp.float32((h.shape[1] // HEADS) ** -0.5), jnp.float32(1))
            qkv[m, :, cols] = y.astype(jnp.bfloat16)

        loop(6, project)
        for m in range(3):
            pltpu.make_async_copy(qkv.at[m], saved_qkv.at[l, m], qsem.at[m]).start()

        def attend(i):
            @pl.when(lax.rem(i, 3) == 0)
            def _():
                pump(base + 7 + i // 3)

            r = i // pairs
            lanes = tile(lax.rem(i, pairs), 128)
            slot = lax.rem(i, 2)
            store_p = pltpu.make_async_copy(p_stage.at[slot], saved_p.at[l, i], psem.at[slot])

            @pl.when((i >= 2) | (l > 0))
            def _():
                store_p.wait()

            top = pl.multiple_of(r * slots, slots)
            starts = window_starts(slots)
            scores = [
                matmul_nt(
                    qkv[1, pl.ds(top + start, WINDOW), lanes],
                    pair_stack(qkv[0, pl.ds(top + b * BLOCK, BLOCK), lanes]),
                )
                for b, start in enumerate(starts)
            ]
            for b, start in enumerate(starts):
                vm = qkv[2, pl.ds(top + start, WINDOW), lanes]
                same = id_col[r, start : start + WINDOW, :] == id_row[r, :1, b * BLOCK : (b + 1) * BLOCK]
                s = jnp.where(jnp.concatenate([same, same], axis=1), scores[b], NEGATIVE)
                e = jnp.exp(s - jnp.max(s, axis=0, keepdims=True))
                p = e * (1.0 / jnp.sum(e, axis=0, keepdims=True))
                p = p.astype(jnp.bfloat16)
                p_stage[slot, b] = p
                o[pl.ds(top + b * BLOCK, BLOCK), lanes] = pair_join(matmul_tn(p, vm)).astype(jnp.bfloat16)
            store_p.start()

        loop(rows * pairs, attend)

        def attn_out(i):
            pump(base + 13 + i)
            cols = tile(i, WIDTH)
            h[:, cols] += matmul(o[...], weights(base + AT_OUT + i))

        loop(2, attn_out)
        normalize(l, 0)

        def inner(i):
            @pl.when(lax.rem(i, 4) < 3)
            def _():
                pump(base + 15 + i - i // 4)

            cols = tile(i, WIDTH)
            u[...] = matmul(a[...], weights(base + AT_INNER + i)) + inner_bias[pl.ds(l, 1), cols]
            slot = lax.rem(i, 2)
            store_d = pltpu.make_async_copy(d_stage.at[slot], saved_d.at[l, i], dsem.at[slot])

            @pl.when((i >= 2) | (l > 0))
            def _():
                store_d.wait()

            def activate(t):
                part = tile(t, ROW_TILE)
                x = u[part, :]
                cdf = 0.5 + 0.5 * lax.erf(x * ROOT_HALF)
                z[i // 2, part, tile(i % 2, WIDTH)] = (x * cdf).astype(jnp.bfloat16)
                slope = cdf + x * (DENSITY * jnp.exp(-0.5 * x * x))
                d_stage[slot, part, :] = slope.astype(jnp.bfloat16)

            loop(count // ROW_TILE, activate)
            store_d.start()

        loop(8, inner)

        def outer(i):
            @pl.when((lax.rem(i, 2) == 0) & (i > 0))
            def _():
                pump(base + 20 + i // 2)

            @pl.when(i == 7)
            def _():
                pump(base + 24)

            cols = tile(i // 4, WIDTH)
            h[:, cols] += matmul(z[lax.rem(i, 4)], weights(base + AT_OUTER + i))

        loop(8, outer)
        normalize(l, 1)

    loop(LAYERS, layer)
    store = pltpu.make_async_copy(a, out, tsem)
    store.start()
    last = LAYERS - 1
    for m in range(3):
        pltpu.make_async_copy(qkv.at[m], saved_qkv.at[last, m], qsem.at[m]).wait()
    for i in range(2):
        pltpu.make_async_copy(p_stage.at[i], saved_p.at[last, i], psem.at[i]).wait()
        pltpu.make_async_copy(d_stage.at[i], saved_d.at[last, i], dsem.at[i]).wait()
    pltpu.make_async_copy(x_stage, saved_x.at[last, 1], xsem).wait()
    pltpu.make_async_copy(s_stage, saved_s.at[last, 1], ssem).wait()
    store.wait()


def forward(devices, lengths, matrices, tokens, vectors, inner_bias, rows, slots):
    count, width = tokens.shape
    hidden = inner_bias.shape[-1]
    unit = matrices[0].shape[1]
    bf, f32 = jnp.bfloat16, jnp.float32
    blocks = slots // BLOCK
    devices_dims = chip_dims(devices)
    held = devices_dims + (2, unit, WIDTH)
    sems = sum(devices_dims) - 1
    any_ = pl.BlockSpec(memory_space=HBM)
    vm = pl.BlockSpec(memory_space=VMEM)
    return pl.pallas_call(
        functools.partial(forward_kernel, (rows, slots), devices_dims),
        out_shape=(
            jax.ShapeDtypeStruct((LAYERS * GROUPS,) + held, bf),
            jax.ShapeDtypeStruct((count, width), bf),
            jax.ShapeDtypeStruct((LAYERS, 3, count, width), bf),
            jax.ShapeDtypeStruct((LAYERS, rows * HEADS // 2, blocks, WINDOW, 2 * BLOCK), bf),
            jax.ShapeDtypeStruct((LAYERS, 2, count, width), f32),
            jax.ShapeDtypeStruct((LAYERS, 2, count, 128), f32),
            jax.ShapeDtypeStruct((LAYERS, hidden // WIDTH, count, WIDTH), bf),
        ),
        in_specs=[pl.BlockSpec(memory_space=pltpu.SMEM)] + [vm] * 6 + [any_] + [vm] * 9,
        out_specs=(any_,) * 7,
        scratch_shapes=[
            VMEM((count, width), f32),
            VMEM((count, width), bf),
            VMEM((3, count, width), bf),
            VMEM((count, width), bf),
            VMEM((hidden // width, count, width), bf),
            VMEM((count, WIDTH), f32),
            VMEM((2,) + held, bf),
            VMEM((2, blocks, WINDOW, 2 * BLOCK), bf),
            VMEM((2, count, WIDTH), bf),
            VMEM((count, width), f32),
            VMEM((count, 128), f32),
            VMEM((LAYERS * GROUPS, unit, WIDTH), bf),
            VMEM((rows, 8, slots), jnp.int32),
            VMEM((rows, slots, 128), jnp.int32),
            VMEM((LAYERS, hidden), f32),
            DMA((2,)), DMA((2,)), DMA((2,)), DMA, DMA, DMA((3,)), DMA, DMA,
            DMA((SLOTS, 2, sems)), DMA((SLOTS, 2, sems)),
        ],
        compiler_params=pltpu.CompilerParams(
            vmem_limit_bytes=58 << 20, collective_id=0, has_side_effects=True
        ),
    )(lengths, *matrices, tokens, *vectors, inner_bias)


def digits(devices):
    out, stride = [], 1
    while stride < devices:
        size = 2 if stride == 1 else min(4, devices // stride)
        out.append((stride, size))
        stride *= size
    return out


class Exchange:
    def __init__(self, me, places, held, got, ssem, rsem):
        self.me, self.places = me, places
        self.held, self.got, self.ssem, self.rsem = held, got, ssem, rsem

    def copies(self, k):
        stride, size = self.places[k]
        digit = lax.rem(self.me // stride, size)
        out = []
        for d in range(1, size):
            to = self.me + (lax.rem(digit + d, size) - digit) * stride
            out.append(
                pltpu.make_async_remote_copy(
                    src_ref=self.held.at[k],
                    dst_ref=self.got.at[k, digit],
                    send_sem=self.ssem.at[k, d],
                    recv_sem=self.rsem.at[k, d],
                    device_id=(to,),
                    device_id_type=MESH,
                )
            )
        return out, digit, size

    def step(self, k):
        if k > 0:
            copies, digit, size = self.copies(k - 1)
            for c in copies:
                c.wait()
            self.got[k - 1, digit] = self.held[k - 1]
            total = self.got[k - 1, 0]
            for j in range(1, size):
                total = total + self.got[k - 1, j]
            self.held[k] = total
        if k < len(self.places):
            for c in self.copies(k)[0]:
                c.start()


def fold(x):
    rows, width = x.shape
    return jnp.sum(x.reshape(rows // 8, 8, width), axis=0)


def backward_kernel(
    dims, places,
    lengths, wbuf, cotangent, gain_attn, gain_ffn, saved_qkv, saved_p, saved_x, saved_s, saved_d,
    grad, sums, late_sums,
    g, db, du, qkv, dqkv, x, sc, d, w, p, dk, dv, part, late,
    held, got, late_held, late_got,
    wsem, psem, dsem, xsem, ssem, qsem, csem, gsem, send_sem, recv_sem, late_send, late_recv,
):
    rows, slots = dims
    count, width = g.shape
    pairs = HEADS // 2
    per_layer = GROUPS // 2
    total = LAYERS * per_layer
    items = rows * pairs
    steps = len(places)
    chunk = 256
    chunks = [slice(c * chunk, (c + 1) * chunk) for c in range(width // chunk)]

    def wload(i):
        l = LAYERS - 1 - i // per_layer
        j = lax.rem(i, per_layer)
        outer = (j < 8) & (lax.rem(j, 2) == 0)
        ffn = jnp.where(outer, AT_OUTER + j // 2, AT_INNER + j // 2 * 2)
        block = l * GROUPS + jnp.where(j < 8, ffn, jnp.where(j == 8, AT_OUT, 2 * (j - 9)))
        slot = lax.rem(i, 3)
        apart = jnp.where(outer, 4, 1)
        return [
            pltpu.make_async_copy(wbuf.at[block + c * apart], w.at[slot, c], wsem.at[slot, c])
            for c in range(2)
        ]

    def weights(i):
        @pl.when(i + 2 < total)
        def _():
            for c in wload(i + 2):
                c.start()

        for c in wload(i):
            c.wait()
        return lax.rem(i, 3)

    def product(left, slot, n):
        return matmul_nt(left[:, :WIDTH], w[slot, 0, n, :]) + matmul_nt(left[:, WIDTH:], w[slot, 1, n, :])

    def xload(l, which):
        return (
            pltpu.make_async_copy(saved_x.at[l, which], x.at[which], xsem.at[which]),
            pltpu.make_async_copy(saved_s.at[l, which], sc.at[which], ssem.at[which]),
        )

    def dload(l, quarter):
        slot = lax.rem(quarter, 2)
        return pltpu.make_async_copy(saved_d.at[l, pl.ds(2 * quarter, 2)], d.at[slot], dsem.at[slot])

    def pload(l, i):
        slot = lax.rem(i, 3)
        return pltpu.make_async_copy(saved_p.at[l, i], p.at[slot], psem.at[slot])

    def qload(l):
        return [pltpu.make_async_copy(saved_qkv.at[l, m], qkv.at[m], qsem.at[m]) for m in range(3)]

    top_layer = LAYERS - 1
    first = pltpu.make_async_copy(cotangent, db, csem)
    first.start()
    for c in xload(top_layer, 1):
        c.start()
    for i in range(2):
        for c in wload(i):
            c.start()
    dload(top_layer, 0).start()
    for c in xload(top_layer, 0):
        c.start()
    me = lax.axis_index("dp")
    if steps:
        barrier = pltpu.get_barrier_semaphore()
        for stride, size in places:
            digit = lax.rem(me // stride, size)
            for k in range(1, size):
                to = me + (lax.rem(digit + k, size) - digit) * stride
                pl.semaphore_signal(barrier, inc=1, device_id=(to,), device_id_type=MESH)
    first.wait()
    for r in range(rows):
        real = slots - lengths[r, lengths.shape[1] - 1]

        def widen(i):
            t = pl.ds(pl.multiple_of(r * slots + i * ROW_TILE, ROW_TILE), ROW_TILE)
            slot = i * ROW_TILE + lax.broadcasted_iota(jnp.int32, (ROW_TILE, width), 0)
            g[t, :] = jnp.where(slot < real, db[t, :].astype(jnp.float32), 0.0)

        loop(slots // ROW_TILE, widen)
    if steps:
        pl.semaphore_wait(barrier, sum(size - 1 for _, size in places))

    def normalize_back(l, which):
        gain = (gain_attn, gain_ffn)[which]
        row_shift = (D_ATTN, D_FFN)[which]
        row_bias = (D_OUT, D_OUTER)[which]
        for c in xload(l, which):
            c.wait()

        def body(i, carry):
            t = tile(i, ROW_TILE)
            up = g[t, :]
            xh = x[which, t, :]
            scaled = up * gain[pl.ds(l, 1), :]
            m1 = jnp.mean(scaled, axis=1, keepdims=True)
            m2 = jnp.mean(scaled * xh, axis=1, keepdims=True)
            down = sc[which, t, :1] * (scaled - m1 - xh * m2)
            g[t, :] = down
            low = down.astype(jnp.bfloat16)
            db[t, :] = low
            return carry[0] + fold(up), carry[1] + fold(low.astype(jnp.float32))

        zero = jnp.zeros((8, width), jnp.float32)
        shift_sum, bias_sum = lax.fori_loop(0, count // ROW_TILE, body, (zero, zero))
        part[row_shift] = shift_sum
        part[row_bias] = bias_sum

        @pl.when(l > 0)
        def _():
            for c in xload(l - 1, which):
                c.start()

    last_sums = Exchange(me, places, late_held, late_got, late_send, late_recv)

    def layer(step):
        l = top_layer - step
        base = step * per_layer
        normalize_back(l, 1)

        def quarter(kc):
            @pl.when(kc + 1 < 4)
            def _():
                dload(l, kc + 1).start()

            @pl.when(kc == 1)
            def _():
                for c in qload(l):
                    c.start()

            slot = weights(base + 2 * kc)
            dload(l, kc).wait()
            for c, n in enumerate(chunks):
                within = slice(c * chunk % WIDTH, c * chunk % WIDTH + chunk)
                slope = d[lax.rem(kc, 2), c * chunk // WIDTH, :, within].astype(jnp.float32)
                low = (product(db, slot, n) * slope).astype(jnp.bfloat16)
                du[:, n] = low
                part[D_INNER + kc, :, n] = fold(low.astype(jnp.float32))
            slot = weights(base + 2 * kc + 1)
            for n in chunks:
                g[:, n] += product(du, slot, n)

        loop(4, quarter)

        @pl.when(l > 0)
        def _():
            dload(l - 1, 0).start()

        pload(l, 0).start()
        pload(l, 1).start()
        normalize_back(l, 0)
        slot = weights(base + 8)
        for n in chunks:
            du[:, n] = product(db, slot, n).astype(jnp.bfloat16)
        for c in qload(l):
            c.wait()
        early = Exchange(me, places, held.at[l], got.at[l], send_sem.at[l], recv_sem.at[l])
        held[l, 0] = jnp.sum(part[...], axis=1)
        early.step(0)

        def attend(i):
            for k in range(1, steps + 1):

                @pl.when(i == 3 * k)
                def _():
                    early.step(k)

            r = i // pairs
            lanes = tile(lax.rem(i, pairs), 128)
            slot = lax.rem(i, 3)

            @pl.when(i + 2 < items)
            def _():
                pload(l, i + 2).start()

            pload(l, i).wait()
            dk[...] = jnp.zeros_like(dk)
            dv[...] = jnp.zeros_like(dv)
            top = pl.multiple_of(r * slots, slots)
            starts = window_starts(slots)
            mine = [pl.ds(top + b * BLOCK, BLOCK) for b in range(len(starts))]
            reach = [pl.ds(top + start, WINDOW) for start in starts]
            stacked = [pair_stack(du[rows_, lanes]) for rows_ in mine]
            dps = [matmul_nt(qkv[2, keys, lanes], om) for keys, om in zip(reach, stacked)]
            for b, start in enumerate(starts):
                qm = pair_stack(qkv[0, mine[b], lanes])
                pb = p[slot, b]
                pf = pb.astype(jnp.float32)
                weighted = pf * dps[b]
                ds = weighted - pf * jnp.sum(weighted, axis=0, keepdims=True)
                ds = ds.astype(jnp.bfloat16)
                dk[start : start + WINDOW, :] += matmul(ds, qm)
                dv[start : start + WINDOW, :] += matmul(pb, stacked[b])
                dq = pair_join(matmul_tn(ds, qkv[1, reach[b], lanes]))
                dqkv[0, mine[b], lanes] = (dq * (width // HEADS) ** -0.5).astype(jnp.bfloat16)
            every = pl.ds(top, slots)
            dqkv[1, every, lanes] = dk[...].astype(jnp.bfloat16)
            dqkv[2, every, lanes] = dv[...].astype(jnp.bfloat16)

        loop(items, attend)
        sums[l] = held[l, steps]
        for m, row in ((0, 0), (2, 1)):

            def add(t, carry):
                return carry + fold(dqkv[m, tile(t, ROW_TILE), :].astype(jnp.float32))

            late[2 * l + row] = lax.fori_loop(
                0, count // ROW_TILE, add, jnp.zeros((8, width), jnp.float32)
            )

        @pl.when(l == 0)
        def _():
            late_held[0] = jnp.sum(late[...], axis=1)
            last_sums.step(0)

        for m in range(3):
            slot = weights(base + 9 + m)
            for c, n in enumerate(chunks):
                g[:, n] += product(dqkv.at[m], slot, n)
                if m == 2:

                    @pl.when(l == 0)
                    def _():
                        pltpu.make_async_copy(g.at[:, n], grad.at[:, n], gsem.at[c]).start()

            if m + 1 < steps:

                @pl.when(l == 0)
                def _():
                    last_sums.step(m + 1)

    late[...] = jnp.zeros_like(late)
    loop(LAYERS, layer)
    for k in range(min(steps, 3), steps + 1):
        if k > 0:
            last_sums.step(k)
    late_sums[...] = late_held[steps]
    for c, n in enumerate(chunks):
        pltpu.make_async_copy(g.at[:, n], grad.at[:, n], gsem.at[c]).wait()


def backward(devices, lengths, wbuf, cotangent, gain_attn, gain_ffn, saved, rows, slots):
    count, width = cotangent.shape
    bf, f32 = jnp.bfloat16, jnp.float32
    blocks = slots // BLOCK
    places = digits(devices)
    steps = max(len(places), 1)
    any_ = pl.BlockSpec(memory_space=HBM)
    vm = pl.BlockSpec(memory_space=VMEM)
    return pl.pallas_call(
        functools.partial(backward_kernel, (rows, slots), places),
        out_shape=(
            jax.ShapeDtypeStruct((count, width), f32),
            jax.ShapeDtypeStruct((LAYERS, EARLY, width), f32),
            jax.ShapeDtypeStruct((8, width), f32),
        ),
        in_specs=[pl.BlockSpec(memory_space=pltpu.SMEM), any_, any_, vm, vm] + [any_] * 5,
        out_specs=(any_, vm, vm),
        scratch_shapes=[
            VMEM((count, width), f32),
            VMEM((count, width), bf),
            VMEM((count, width), bf),
            VMEM((3, count, width), bf),
            VMEM((3, count, width), bf),
            VMEM((2, count, width), f32),
            VMEM((2, count, 128), f32),
            VMEM((2, 2, count, WIDTH), bf),
            VMEM((3, 2, width, WIDTH), bf),
            VMEM((3, blocks, WINDOW, 2 * BLOCK), bf),
            VMEM((slots, 128), f32),
            VMEM((slots, 128), f32),
            VMEM((EARLY, 8, width), f32),
            VMEM((8, 8, width), f32),
            VMEM((LAYERS, steps + 1, EARLY, width), f32),
            VMEM((LAYERS, steps, 4, EARLY, width), f32),
            VMEM((steps + 1, 8, width), f32),
            VMEM((steps, 4, 8, width), f32),
            DMA((3, 2)), DMA((3,)), DMA((2,)), DMA((2,)), DMA((2,)), DMA((3,)), DMA, DMA((4,)),
            DMA((LAYERS, steps, 4)), DMA((LAYERS, steps, 4)), DMA((steps, 4)), DMA((steps, 4)),
        ],
        compiler_params=pltpu.CompilerParams(
            vmem_limit_bytes=60 << 20,
            **({"collective_id": 1, "has_side_effects": True} if places else {}),
        ),
    )(lengths, wbuf, cotangent, gain_attn, gain_ffn, *saved)


def finish_kernel(unit, sums, late, query, value, out, inner, outer, attn, ffn):
    width = sums.shape[2]
    devices = width // unit
    for l in range(LAYERS):
        here = slice(l, l + 1)
        for row, ref in ((D_OUT, out), (D_OUTER, outer), (D_ATTN, attn), (D_FFN, ffn)):
            ref[here, :] = sums[l, row : row + 1, :]
        query[here, :] = late[2 * l : 2 * l + 1, :]
        value[here, :] = late[2 * l + 1 : 2 * l + 2, :]
        for b in range(inner.shape[1] // 128):
            block = None
            for piece in range(128 // unit):
                device, quarter = divmod(b * (128 // unit) + piece, inner.shape[1] // width)
                source = device * unit
                row = D_INNER + quarter
                first = source // 128 * 128
                x = sums[l, row : row + 1, first : first + 128]
                shift = (piece * unit - source) % 128
                if shift:
                    x = pltpu.roll(x, shift, axis=1)
                if block is None:
                    block = x
                else:
                    lane = lax.broadcasted_iota(jnp.int32, x.shape, 1)
                    block = jnp.where(lane >= piece * unit, x, block)
            inner[here, b * 128 : (b + 1) * 128] = block


def finish(unit, hidden, sums, late):
    width = sums.shape[2]
    vm = pl.BlockSpec(memory_space=VMEM)
    sizes = (width, width, width, hidden, width, width, width)
    return pl.pallas_call(
        functools.partial(finish_kernel, unit),
        out_shape=tuple(jax.ShapeDtypeStruct((LAYERS, n), jnp.float32) for n in sizes),
        in_specs=[vm, vm],
        out_specs=(vm,) * 7,
    )(sums, late)


def per_device(
    devices,
    tokens,
    lengths,
    w_query,
    w_key,
    w_value,
    w_out,
    w_inner,
    w_outer,
    bias_query,
    bias_value,
    bias_out,
    bias_inner,
    bias_outer,
    shift_attn,
    shift_ffn,
    gain_attn,
    gain_ffn,
    cotangent,
):
    rows, slots, width = tokens.shape
    hidden = bias_inner.shape[1]
    unit = w_query.shape[1]
    count = rows * slots
    vectors = (
        bias_query, bias_value, bias_out, bias_outer, shift_attn, shift_ffn, gain_attn, gain_ffn,
    )
    matrices = (w_query, w_key, w_value, w_out, w_inner, w_outer)
    wbuf, out, *saved = forward(
        devices, lengths, matrices, tokens.reshape(count, width), vectors, bias_inner, rows, slots
    )
    wbuf = wbuf.reshape(LAYERS * GROUPS, width, WIDTH)
    grad, sums, late = backward(
        devices, lengths, wbuf, cotangent.reshape(count, width), gain_attn, gain_ffn, saved, rows, slots
    )
    return (
        out.reshape(rows, slots, width),
        grad.reshape(rows, slots, width),
        *finish(unit, hidden, sums, late),
    )


def solution(mesh):
    rows, whole = P("dp", None, None), P()
    weight = P(None, "dp", None)
    placed = (rows, P("dp", None)) + (weight,) * 6 + (whole,) * 9 + (rows,)
    return jax.shard_map(
        functools.partial(per_device, mesh.shape["dp"]),
        mesh=mesh,
        in_specs=placed,
        out_specs=(rows, rows) + (whole,) * 7,
        check_vma=False,
    )
```

```python
import functools

import jax
import jax.numpy as jnp
from jax import lax
from jax.experimental import pallas as pl
from jax.experimental.pallas import tpu as pltpu
from jax.sharding import PartitionSpec as P

HEADS = 16
LAYERS = 2
EPSILON = 1e-12
NEGATIVE = -1e9
PADDING_ID = 1000
MESH = pl.DeviceIdType.MESH
HBM = pltpu.MemorySpace.HBM
VMEM = pltpu.VMEM
DMA = pltpu.SemaphoreType.DMA

WIDTH = 512
GROUPS = 24
AT_OUT, AT_INNER, AT_OUTER = 6, 8, 16
BLOCK = 128
WINDOW = 256
ROW_TILE = 128
ROOT_HALF = 0.7071067811865476
DENSITY = 0.3989422804014327
B_Q, B_V, B_OUT, B_OUTER, S_ATTN, S_FFN, G_ATTN, G_FFN = range(8)
D_OUT, D_OUTER, D_ATTN, D_FFN, D_INNER = range(5)
EARLY = 8


def chip_dims(devices):
    bits = (devices // 2).bit_length() - 1
    first = -(-bits // 3)
    second = -(-(bits - first) // 2)
    return (1 << first, 1 << second, 1 << (bits - first - second))


RELAY = 4
ORDERS = (((0, 4, 2, 1, 3), (1, 0, 4, 2, 3)), ((0, 4, 1, 2, 3), (2, 0, 4, 1, 3)))
STARTS = ((0, 2, 4, 6, 8, 10), (0, 2, 4, 6, 8, 10))
DEPTH = 10
SLOTS = 4


class Gather:
    def __init__(self, dims, own, buf, ssem, rsem, total):
        self.dims, self.own, self.buf = dims, own, buf
        self.ssem, self.rsem, self.total = ssem, rsem, total
        self.me = lax.axis_index("dp")
        _, n1, n2 = dims
        self.core = lax.rem(self.me, 2)
        chip = self.me // 2
        self.at = (chip // (n1 * n2), lax.rem(chip // n2, n1), lax.rem(chip, n2))
        self.step = (n1 * n2 * 2, n2 * 2, 2)
        self.relay = dims[0] == 4
        self.orders, self.starts = ORDERS, STARTS
        if not self.relay:
            self.orders = tuple(
                tuple(tuple(d for d in order if d != RELAY) for order in pair) for pair in ORDERS
            )
            self.starts = ((0, 2, 4, 6, 8), (0, 2, 4, 6, 8))
        self.phases = len(self.orders[0][0])
        rows, cols = own.shape[-2:]
        half = cols // 2
        if rows % 32 == 0:
            q = rows // 4
            self.parts = (
                ((pl.ds(0, q), pl.ds(0, cols)), (pl.ds(q, q), pl.ds(0, half))),
                ((pl.ds(2 * q, 2 * q), pl.ds(0, cols)), (pl.ds(q, q), pl.ds(half, half))),
            )
        else:
            self.parts = tuple(((pl.ds(0, rows), pl.ds(c * half, half)),) for c in range(2))

    def peers(self, dim):
        if dim == 3:
            return [self.me + 1 - 2 * self.core]
        out = []
        for d in range(1, self.dims[dim]):
            to = lax.rem(self.at[dim] + d, self.dims[dim])
            out.append(self.me + (to - self.at[dim]) * self.step[dim])
        return out

    def moves(self, g, par, s, p):
        order = self.orders[par][s]
        dim, full = order[p], order[:p]
        n0, n1, n2 = self.dims
        first = (0, n0, n0 + n1 - 1, n0 + n1 + n2 - 2, n0 - 1)[dim]
        where = [pl.ds(0, self.dims[d]) if d in full else self.at[d] for d in range(3)]
        slot = lax.rem(g, SLOTS)
        z = self.at[0]
        if dim == RELAY:
            middle = (z == 1) | (z == 2)
            where[0] = jnp.where(z < 2, 3, 0)
            targets = [self.me + (3 - where[0] - z) * self.step[0]]
            guards = [(middle, jnp.logical_not(middle))]
        else:
            targets = self.peers(dim)
            guards = [(None, None)] * len(targets)
            if dim == 0 and self.relay:
                guards = [
                    (jnp.abs(lax.rem(z + d, 4) - z) != 3, jnp.abs(lax.rem(z + 4 - d, 4) - z) != 3)
                    if d != 2
                    else (None, None)
                    for d in (1, 2, 3)
                ]
        out = []
        for n, sub in enumerate(self.parts[s]):
            dst = self.buf.at[(g,) + tuple(where) + (self.core,) + sub]
            src = self.own.at[(g,) + sub] if p == 0 else dst
            for i, (to, guard) in enumerate(zip(targets, guards)):
                copy = pltpu.make_async_remote_copy(
                    src_ref=src,
                    dst_ref=dst,
                    send_sem=self.ssem.at[slot, s, n, first + i],
                    recv_sem=self.rsem.at[slot, s, n, first + i],
                    device_id=(to,),
                    device_id_type=MESH,
                )
                out.append((copy, *guard))
        return out

    def greet(self):
        bar = pltpu.get_barrier_semaphore()
        for d in range(4):
            for to in self.peers(d):
                pl.semaphore_signal(bar, inc=1, device_id=(to,), device_id_type=MESH)

    def meet(self):
        pl.semaphore_wait(pltpu.get_barrier_semaphore(), sum(self.dims) - 3 + 1)

    def pump(self, step, par):
        for p in range(self.phases, -1, -1):
            for s in range(2):
                g = step - self.starts[s][p]
                kind = (par - self.starts[s][p]) % 2

                @pl.when((g >= 0) & (g < self.total))
                def _():
                    if p > 0:
                        for copy, sends, receives in self.moves(g, kind, s, p - 1):
                            if sends is None:
                                copy.wait()
                            else:
                                pl.when(sends)(copy.wait_send)
                                pl.when(receives)(copy.wait_recv)
                    if p < self.phases:
                        for copy, sends, _ in self.moves(g, kind, s, p):
                            if sends is None:
                                copy.start()
                            else:
                                pl.when(sends)(copy.start)


def matmul(left, right):
    return jnp.dot(left, right, preferred_element_type=jnp.float32)


def matmul_nt(left, right):
    return lax.dot_general(
        left, right, (((1,), (1,)), ((), ())), preferred_element_type=jnp.float32
    )


def matmul_tn(left, right):
    return lax.dot_general(
        left, right, (((0,), (0,)), ((), ())), preferred_element_type=jnp.float32
    )


def loop(count, body):
    lax.fori_loop(0, count, lambda i, c: (body(i), c)[1], 0)


def tile(i, size):
    return pl.ds(pl.multiple_of(i * size, size), size)


def window_starts(slots):
    return [
        min(max(b * BLOCK - (WINDOW - BLOCK) // 2, 0), slots - WINDOW)
        for b in range(slots // BLOCK)
    ]


def pair_stack(rows):
    lane = lax.broadcasted_iota(jnp.int32, rows.shape, 1)
    zero = jnp.zeros_like(rows)
    half = rows.shape[1] // 2
    return jnp.concatenate(
        [jnp.where(lane < half, rows, zero), jnp.where(lane < half, zero, rows)], axis=0
    )


def pair_join(stacked):
    rows = stacked.shape[0] // 2
    lane = lax.broadcasted_iota(jnp.int32, (rows, stacked.shape[1]), 1)
    return jnp.where(lane < stacked.shape[1] // 2, stacked[:rows], stacked[rows:])


def permute_hidden(load, store, unit, hidden):
    devices = hidden // (4 * unit)
    for b in range(hidden // 128):
        block = None
        for piece in range(128 // unit):
            quarter, device = divmod(b * (128 // unit) + piece, devices)
            source = (4 * device + quarter) * unit
            x = load(source // 128)
            shift = (piece * unit - source) % 128
            if shift:
                x = pltpu.roll(x, shift, axis=1)
            if block is None:
                block = x
            else:
                lane = lax.broadcasted_iota(jnp.int32, x.shape, 1)
                block = jnp.where(lane >= piece * unit, x, block)
        store(b, block)


def store_block(own, first, b, x):
    per = WIDTH // 128
    own[first + b // per, :, b % per * 128 : (b % per + 1) * 128] = x.astype(own.dtype)


def slot_ids(lengths, r, position):
    segments = lengths.shape[1]
    number = jnp.zeros_like(position)
    end = jnp.int32(0)
    for j in range(segments):
        end = end + lengths[r, j]
        number = number + (position >= end).astype(jnp.int32)
    return jnp.where(number < segments - 1, number, PADDING_ID + position)


def fold(x):
    rows, width = x.shape
    return jnp.sum(x.reshape(rows // 8, 8, width), axis=0)


def norm_back(up, xhat, scale, gain_row):
    scaled = up * gain_row
    m1 = jnp.mean(scaled, axis=1, keepdims=True)
    m2 = jnp.mean(scaled * xhat, axis=1, keepdims=True)
    return scale * (scaled - m1 - xhat * m2)


def forward_kernel(
    dims, devices_dims,
    lengths, w_query, w_key, w_value, w_out, w_inner, w_outer, tokens, cotangent, *rest,
):
    vectors, rest = rest[:8], rest[8:]
    (
        inner_raw, wbuf, out, first_sums, saved_f, saved_qkv, saved_p, saved_x, saved_s, saved_d,
        h, a, qkv, o, z, u, w, p_stage, d_stage, x_stage, s_stage, own, id_row, id_col, inner_bias, cot,
        wsem, psem, dsem, xsem, ssem, qsem, tsem, hsem, csem, send_sem, recv_sem,
    ) = rest
    rows, slots = dims
    count = h.shape[0]
    pairs = HEADS // 2
    total = LAYERS * GROUPS
    gather = Gather(devices_dims, own, wbuf, send_sem, recv_sem, total)

    def wload(g):
        slot = lax.rem(g, 2)
        return pltpu.make_async_copy(wbuf.at[g], w.at[slot], wsem.at[slot])

    def weights(g):
        @pl.when(g + 1 < total)
        def _():
            wload(g + 1).start()

        wload(g).wait()
        return w[lax.rem(g, 2)].reshape(h.shape[1], WIDTH)

    def pump(half):
        for par in range(2):

            @pl.when(lax.rem(half, 2) == par)
            def _():
                gather.pump(half + DEPTH, par)

    gather.greet()
    load = pltpu.make_async_copy(tokens, a, tsem)
    load.start()
    load_cot = pltpu.make_async_copy(cotangent, cot, csem)
    load_cot.start()
    unit = own.shape[1]

    def cast(l, m):
        matrix = (w_query, w_key, w_value, w_out)[m]
        for c in range(2):
            own[l * GROUPS + 2 * m + c] = matrix[l, :, tile(c, WIDTH)].astype(jnp.bfloat16)

    def here(first, count):
        blocks = pl.ds(first, count)
        return pltpu.make_async_copy(
            own.at[blocks], wbuf.at[(blocks,) + gather.at + (gather.core,)], hsem
        )

    def start(i):
        gather.pump(i, i % 2)

    for m in range(4):
        cast(0, m)
    here(0, AT_INNER).start()
    gather.meet()
    start(0)
    here(0, AT_INNER).wait()
    start(1)
    for l in range(LAYERS):
        at = l * GROUPS
        for m in range(4):
            if l > 0:
                cast(l, m)
        for c in range(2):
            for kc in range(4):
                piece = w_outer[l, kc * unit : (kc + 1) * unit, c * WIDTH : (c + 1) * WIDTH]
                own[at + AT_OUTER + 4 * c + kc] = piece.astype(jnp.bfloat16)
        permute_hidden(
            lambda b: w_inner[l, :, b * 128 : (b + 1) * 128],
            lambda b, x: store_block(own, at + AT_INNER, b, x),
            unit,
            w_inner.shape[2],
        )
        if l == 0:
            start(2)
    here(AT_INNER, total - AT_INNER).start()
    start(3)
    here(AT_INNER, total - AT_INNER).wait()

    def keep_bias(b, x):
        inner_bias[:, b * 128 : (b + 1) * 128] = x

    permute_hidden(
        lambda b: inner_raw[:, b * 128 : (b + 1) * 128], keep_bias, unit, w_inner.shape[2]
    )
    for r in range(rows):
        id_row[r] = slot_ids(lengths, r, lax.broadcasted_iota(jnp.int32, (8, slots), 1))
        id_col[r] = slot_ids(lengths, r, lax.broadcasted_iota(jnp.int32, (slots, 128), 0))
    first_sums[...] = jnp.zeros_like(first_sums)
    load_cot.wait()
    load.wait()

    def widen(i):
        h[tile(i, ROW_TILE), :] = a[tile(i, ROW_TILE), :].astype(jnp.float32)

    loop(count // ROW_TILE, widen)

    for i in range(4, DEPTH):
        start(i)
    pump(0)
    wload(0).start()

    def normalize(l, which):
        bias, gain, shift = ((B_OUT, G_ATTN, S_ATTN), (B_OUTER, G_FFN, S_FFN))[which]
        store_x = pltpu.make_async_copy(x_stage, saved_x.at[l, which], xsem)
        store_s = pltpu.make_async_copy(s_stage, saved_s.at[l, which], ssem)
        if which == 1:
            store_x.wait()
            store_s.wait()
        else:

            @pl.when(l > 0)
            def _():
                store_x.wait()
                store_s.wait()

        def body(i):
            t = tile(i, ROW_TILE)
            r = h[t, :] + vectors[bias][pl.ds(l, 1), :]
            centered = r - jnp.mean(r, axis=1, keepdims=True)
            var = jnp.mean(centered * centered, axis=1, keepdims=True)
            scale = lax.rsqrt(var + EPSILON)
            xhat = centered * scale
            x_stage[t, :] = xhat
            s_stage[t, :] = jnp.broadcast_to(scale, (ROW_TILE, 128))
            y = xhat * vectors[gain][pl.ds(l, 1), :] + vectors[shift][pl.ds(l, 1), :]
            h[t, :] = y
            a[t, :] = y.astype(jnp.bfloat16)
            if which == 1:

                @pl.when(l == LAYERS - 1)
                def _():
                    r = i // (slots // ROW_TILE)
                    real = slots - lengths[r, lengths.shape[1] - 1]
                    slot = lax.rem(i * ROW_TILE, slots) + lax.broadcasted_iota(
                        jnp.int32, (ROW_TILE, h.shape[1]), 0
                    )
                    up = jnp.where(slot < real, cot[t, :].astype(jnp.float32), 0.0)
                    down = norm_back(up, xhat, scale, vectors[gain][pl.ds(l, 1), :])
                    x_stage[t, :] = down
                    low = down.astype(jnp.bfloat16)
                    cot[t, :] = low
                    first_sums[0] += fold(up)
                    first_sums[1] += fold(low.astype(jnp.float32))

        loop(count // ROW_TILE, body)
        store_x.start()
        store_s.start()

    def layer(l):
        base = l * GROUPS

        @pl.when(l > 0)
        def _():
            for m in range(3):
                pltpu.make_async_copy(qkv.at[m], saved_qkv.at[l, m], qsem.at[m]).wait()

        def project(i):
            pump(base + i + 1)
            m = i // 2
            cols = tile(i % 2, WIDTH)
            bias_q = vectors[B_Q][pl.ds(l, 1), cols]
            bias_v = vectors[B_V][pl.ds(l, 1), cols]
            bias = jnp.where(m == 0, bias_q, jnp.where(m == 1, jnp.zeros_like(bias_v), bias_v))
            y = matmul(a[...], weights(base + i)) + bias
            y = y * jnp.where(m == 0, jnp.float32((h.shape[1] // HEADS) ** -0.5), jnp.float32(1))
            qkv[m, :, cols] = y.astype(jnp.bfloat16)

        loop(6, project)
        for m in range(3):
            pltpu.make_async_copy(qkv.at[m], saved_qkv.at[l, m], qsem.at[m]).start()

        def attend(i):
            @pl.when(lax.rem(i, 3) == 0)
            def _():
                pump(base + 7 + i // 3)

            r = i // pairs
            lanes = tile(lax.rem(i, pairs), 128)
            slot = lax.rem(i, 2)
            store_p = pltpu.make_async_copy(p_stage.at[slot], saved_p.at[l, i], psem.at[slot])

            @pl.when((i >= 2) | (l > 0))
            def _():
                store_p.wait()

            top = pl.multiple_of(r * slots, slots)
            starts = window_starts(slots)
            scores = [
                matmul_nt(
                    qkv[1, pl.ds(top + start, WINDOW), lanes],
                    pair_stack(qkv[0, pl.ds(top + b * BLOCK, BLOCK), lanes]),
                )
                for b, start in enumerate(starts)
            ]
            for b, start in enumerate(starts):
                vm = qkv[2, pl.ds(top + start, WINDOW), lanes]
                same = id_col[r, start : start + WINDOW, :] == id_row[r, :1, b * BLOCK : (b + 1) * BLOCK]
                s = jnp.where(jnp.concatenate([same, same], axis=1), scores[b], NEGATIVE)
                e = jnp.exp(s - jnp.max(s, axis=0, keepdims=True))
                p = e * (1.0 / jnp.sum(e, axis=0, keepdims=True))
                p = p.astype(jnp.bfloat16)
                p_stage[slot, b] = p
                o[pl.ds(top + b * BLOCK, BLOCK), lanes] = pair_join(matmul_tn(p, vm)).astype(jnp.bfloat16)
            store_p.start()

        loop(rows * pairs, attend)

        def attn_out(i):
            pump(base + 13 + i)
            cols = tile(i, WIDTH)
            h[:, cols] += matmul(o[...], weights(base + AT_OUT + i))

        loop(2, attn_out)
        normalize(l, 0)

        def inner(i):
            @pl.when(lax.rem(i, 3) < 2)
            def _():
                pump(base + 15 + i - i // 3)

            cols = tile(i, WIDTH)
            u[...] = matmul(a[...], weights(base + AT_INNER + i)) + inner_bias[pl.ds(l, 1), cols]
            slot = lax.rem(i, 2)
            store_d = pltpu.make_async_copy(d_stage.at[slot], saved_d.at[l, i], dsem.at[slot])

            @pl.when((i >= 2) | (l > 0))
            def _():
                store_d.wait()

            def activate(t):
                part = tile(t, ROW_TILE)
                x = u[part, :]
                cdf = 0.5 + 0.5 * lax.erf(x * ROOT_HALF)
                z[i // 2, part, tile(i % 2, WIDTH)] = (x * cdf).astype(jnp.bfloat16)
                slope = cdf + x * (DENSITY * jnp.exp(-0.5 * x * x))
                d_stage[slot, part, :] = slope.astype(jnp.bfloat16)

            loop(count // ROW_TILE, activate)
            store_d.start()

        loop(8, inner)

        def outer(i):
            @pl.when((lax.rem(i, 2) == 0) & (i > 0))
            def _():
                pump(base + 20 + i // 2)

            @pl.when(i == 7)
            def _():
                pump(base + 24)

            cols = tile(i // 4, WIDTH)
            h[:, cols] += matmul(z[lax.rem(i, 4)], weights(base + AT_OUTER + i))

        loop(8, outer)
        normalize(l, 1)

    loop(LAYERS, layer)
    store = pltpu.make_async_copy(a, out, tsem)
    store.start()
    store_f = pltpu.make_async_copy(cot, saved_f, csem)
    store_f.start()
    last = LAYERS - 1
    for m in range(3):
        pltpu.make_async_copy(qkv.at[m], saved_qkv.at[last, m], qsem.at[m]).wait()
    for i in range(2):
        pltpu.make_async_copy(p_stage.at[i], saved_p.at[last, i], psem.at[i]).wait()
        pltpu.make_async_copy(d_stage.at[i], saved_d.at[last, i], dsem.at[i]).wait()
    pltpu.make_async_copy(x_stage, saved_x.at[last, 1], xsem).wait()
    pltpu.make_async_copy(s_stage, saved_s.at[last, 1], ssem).wait()
    store.wait()
    store_f.wait()


def forward(devices, lengths, matrices, tokens, cotangent, vectors, inner_bias, rows, slots):
    count, width = tokens.shape
    hidden = inner_bias.shape[-1]
    unit = matrices[0].shape[1]
    bf, f32 = jnp.bfloat16, jnp.float32
    blocks = slots // BLOCK
    devices_dims = chip_dims(devices)
    held = devices_dims + (2, unit, WIDTH)
    sems = sum(devices_dims) - 1
    any_ = pl.BlockSpec(memory_space=HBM)
    vm = pl.BlockSpec(memory_space=VMEM)
    return pl.pallas_call(
        functools.partial(forward_kernel, (rows, slots), devices_dims),
        out_shape=(
            jax.ShapeDtypeStruct((LAYERS * GROUPS,) + held, bf),
            jax.ShapeDtypeStruct((count, width), bf),
            jax.ShapeDtypeStruct((2, 8, width), f32),
            jax.ShapeDtypeStruct((count, width), bf),
            jax.ShapeDtypeStruct((LAYERS, 3, count, width), bf),
            jax.ShapeDtypeStruct((LAYERS, rows * HEADS // 2, blocks, WINDOW, 2 * BLOCK), bf),
            jax.ShapeDtypeStruct((LAYERS, 2, count, width), f32),
            jax.ShapeDtypeStruct((LAYERS, 2, count, 128), f32),
            jax.ShapeDtypeStruct((LAYERS, hidden // WIDTH, count, WIDTH), bf),
        ),
        in_specs=[pl.BlockSpec(memory_space=pltpu.SMEM)] + [vm] * 6 + [any_] * 2 + [vm] * 9,
        out_specs=(any_, any_, vm) + (any_,) * 6,
        scratch_shapes=[
            VMEM((count, width), f32),
            VMEM((count, width), bf),
            VMEM((3, count, width), bf),
            VMEM((count, width), bf),
            VMEM((hidden // width, count, width), bf),
            VMEM((count, WIDTH), f32),
            VMEM((2,) + held, bf),
            VMEM((2, blocks, WINDOW, 2 * BLOCK), bf),
            VMEM((2, count, WIDTH), bf),
            VMEM((count, width), f32),
            VMEM((count, 128), f32),
            VMEM((LAYERS * GROUPS, unit, WIDTH), bf),
            VMEM((rows, 8, slots), jnp.int32),
            VMEM((rows, slots, 128), jnp.int32),
            VMEM((LAYERS, hidden), f32),
            VMEM((count, width), bf),
            DMA((2,)), DMA((2,)), DMA((2,)), DMA, DMA, DMA((3,)), DMA, DMA, DMA,
            DMA((SLOTS, 2, 2, sems)), DMA((SLOTS, 2, 2, sems)),
        ],
        compiler_params=pltpu.CompilerParams(
            vmem_limit_bytes=58 << 20, collective_id=0, has_side_effects=True
        ),
    )(lengths, *matrices, tokens, cotangent, *vectors, inner_bias)


def digits(devices):
    out, stride = [], 1
    while stride < devices:
        size = 2 if stride == 1 else min(4, devices // stride)
        out.append((stride, size))
        stride *= size
    return out


class Exchange:
    def __init__(self, me, places, held, got, ssem, rsem):
        self.me, self.places = me, places
        self.held, self.got, self.ssem, self.rsem = held, got, ssem, rsem

    def copies(self, k):
        stride, size = self.places[k]
        digit = lax.rem(self.me // stride, size)
        out = []
        for d in range(1, size):
            to = self.me + (lax.rem(digit + d, size) - digit) * stride
            out.append(
                pltpu.make_async_remote_copy(
                    src_ref=self.held.at[k],
                    dst_ref=self.got.at[k, digit],
                    send_sem=self.ssem.at[k, d],
                    recv_sem=self.rsem.at[k, d],
                    device_id=(to,),
                    device_id_type=MESH,
                )
            )
        return out, digit, size

    def step(self, k):
        if k > 0:
            copies, digit, size = self.copies(k - 1)
            for c in copies:
                c.wait()
            self.got[k - 1, digit] = self.held[k - 1]
            total = self.got[k - 1, 0]
            for j in range(1, size):
                total = total + self.got[k - 1, j]
            self.held[k] = total
        if k < len(self.places):
            for c in self.copies(k)[0]:
                c.start()


def backward_kernel(
    dims, places,
    wbuf, gain_attn, gain_ffn, first_sums, saved_f, saved_qkv, saved_p, saved_x, saved_s, saved_d,
    grad, sums, late_sums,
    g, db, du, qkv, dqkv, x, sc, d, w, p, dk, dv, part, late,
    held, got, late_held, late_got,
    wsem, psem, dsem, xsem, ssem, qsem, csem, gsem, send_sem, recv_sem, late_send, late_recv,
):
    rows, slots = dims
    count, width = g.shape
    pairs = HEADS // 2
    per_layer = GROUPS // 2
    total = LAYERS * per_layer
    items = rows * pairs
    steps = len(places)
    chunk = 256
    chunks = [slice(c * chunk, (c + 1) * chunk) for c in range(width // chunk)]

    def wload(i):
        l = LAYERS - 1 - i // per_layer
        j = lax.rem(i, per_layer)
        outer = (j < 8) & (lax.rem(j, 2) == 0)
        ffn = jnp.where(outer, AT_OUTER + j // 2, AT_INNER + j // 2 * 2)
        block = l * GROUPS + jnp.where(j < 8, ffn, jnp.where(j == 8, AT_OUT, 2 * (j - 9)))
        slot = lax.rem(i, 3)
        apart = jnp.where(outer, 4, 1)
        return [
            pltpu.make_async_copy(wbuf.at[block + c * apart], w.at[slot, c], wsem.at[slot, c])
            for c in range(2)
        ]

    def weights(i):
        @pl.when(i + 2 < total)
        def _():
            for c in wload(i + 2):
                c.start()

        for c in wload(i):
            c.wait()
        return lax.rem(i, 3)

    def product(left, slot, n):
        return matmul_nt(left[:, :WIDTH], w[slot, 0, n, :]) + matmul_nt(left[:, WIDTH:], w[slot, 1, n, :])

    def xload(l, which):
        return (
            pltpu.make_async_copy(saved_x.at[l, which], x.at[which], xsem.at[which]),
            pltpu.make_async_copy(saved_s.at[l, which], sc.at[which], ssem.at[which]),
        )

    def dload(l, quarter):
        slot = lax.rem(quarter, 2)
        return pltpu.make_async_copy(saved_d.at[l, pl.ds(2 * quarter, 2)], d.at[slot], dsem.at[slot])

    def pload(l, i):
        slot = lax.rem(i, 3)
        return pltpu.make_async_copy(saved_p.at[l, i], p.at[slot], psem.at[slot])

    def qload(l):
        return [pltpu.make_async_copy(saved_qkv.at[l, m], qkv.at[m], qsem.at[m]) for m in range(3)]

    top_layer = LAYERS - 1
    opening = [
        pltpu.make_async_copy(saved_f, db, csem.at[0]),
        pltpu.make_async_copy(saved_x.at[top_layer, 1], g, csem.at[1]),
    ]
    opening[0].start()
    for c in wload(0):
        c.start()
    dload(top_layer, 0).start()
    for c in wload(1):
        c.start()
    opening[1].start()
    for c in xload(top_layer, 0):
        c.start()
    if top_layer:
        for c in xload(top_layer - 1, 1):
            c.start()
    me = lax.axis_index("dp")
    if steps:
        barrier = pltpu.get_barrier_semaphore()
        for stride, size in places:
            digit = lax.rem(me // stride, size)
            for k in range(1, size):
                to = me + (lax.rem(digit + k, size) - digit) * stride
                pl.semaphore_signal(barrier, inc=1, device_id=(to,), device_id_type=MESH)
    for c in opening:
        c.wait()
    part[D_FFN] = first_sums[0]
    part[D_OUTER] = first_sums[1]
    if steps:
        pl.semaphore_wait(barrier, sum(size - 1 for _, size in places))

    def normalize_back(l, which):
        gain = (gain_attn, gain_ffn)[which]
        row_shift = (D_ATTN, D_FFN)[which]
        row_bias = (D_OUT, D_OUTER)[which]
        for c in xload(l, which):
            c.wait()

        def body(i, carry):
            t = tile(i, ROW_TILE)
            up = g[t, :]
            xh = x[which, t, :]
            down = norm_back(up, xh, sc[which, t, :1], gain[pl.ds(l, 1), :])
            g[t, :] = down
            low = down.astype(jnp.bfloat16)
            db[t, :] = low
            return carry[0] + fold(up), carry[1] + fold(low.astype(jnp.float32))

        zero = jnp.zeros((8, width), jnp.float32)
        shift_sum, bias_sum = lax.fori_loop(0, count // ROW_TILE, body, (zero, zero))
        part[row_shift] = shift_sum
        part[row_bias] = bias_sum

        @pl.when(l > 0)
        def _():
            for c in xload(l - 1, which):
                c.start()

    last_sums = Exchange(me, places, late_held, late_got, late_send, late_recv)

    def layer(step):
        l = top_layer - step
        base = step * per_layer

        @pl.when(step > 0)
        def _():
            normalize_back(l, 1)

        def quarter(kc):
            @pl.when(kc + 1 < 4)
            def _():
                dload(l, kc + 1).start()

            @pl.when(kc == 1)
            def _():
                for c in qload(l):
                    c.start()

            slot = weights(base + 2 * kc)
            dload(l, kc).wait()
            for c, n in enumerate(chunks):
                within = slice(c * chunk % WIDTH, c * chunk % WIDTH + chunk)
                slope = d[lax.rem(kc, 2), c * chunk // WIDTH, :, within].astype(jnp.float32)
                low = (product(db, slot, n) * slope).astype(jnp.bfloat16)
                du[:, n] = low
                part[D_INNER + kc, :, n] = fold(low.astype(jnp.float32))
            slot = weights(base + 2 * kc + 1)
            for n in chunks:
                g[:, n] += product(du, slot, n)

        loop(4, quarter)

        @pl.when(l > 0)
        def _():
            dload(l - 1, 0).start()

        pload(l, 0).start()
        pload(l, 1).start()
        normalize_back(l, 0)
        slot = weights(base + 8)
        for n in chunks:
            du[:, n] = product(db, slot, n).astype(jnp.bfloat16)
        for c in qload(l):
            c.wait()
        early = Exchange(me, places, held.at[l], got.at[l], send_sem.at[l], recv_sem.at[l])
        held[l, 0] = jnp.sum(part[...], axis=1)
        early.step(0)

        def attend(i):
            for k in range(1, steps + 1):

                @pl.when(i == 3 * k)
                def _():
                    early.step(k)

            r = i // pairs
            lanes = tile(lax.rem(i, pairs), 128)
            slot = lax.rem(i, 3)

            @pl.when(i + 2 < items)
            def _():
                pload(l, i + 2).start()

            pload(l, i).wait()
            dk[...] = jnp.zeros_like(dk)
            dv[...] = jnp.zeros_like(dv)
            top = pl.multiple_of(r * slots, slots)
            starts = window_starts(slots)
            mine = [pl.ds(top + b * BLOCK, BLOCK) for b in range(len(starts))]
            reach = [pl.ds(top + start, WINDOW) for start in starts]
            stacked = [pair_stack(du[rows_, lanes]) for rows_ in mine]
            dps = [matmul_nt(qkv[2, keys, lanes], om) for keys, om in zip(reach, stacked)]
            for b, start in enumerate(starts):
                qm = pair_stack(qkv[0, mine[b], lanes])
                pb = p[slot, b]
                pf = pb.astype(jnp.float32)
                weighted = pf * dps[b]
                ds = weighted - pf * jnp.sum(weighted, axis=0, keepdims=True)
                ds = ds.astype(jnp.bfloat16)
                dk[start : start + WINDOW, :] += matmul(ds, qm)
                dv[start : start + WINDOW, :] += matmul(pb, stacked[b])
                dq = pair_join(matmul_tn(ds, qkv[1, reach[b], lanes]))
                dqkv[0, mine[b], lanes] = (dq * (width // HEADS) ** -0.5).astype(jnp.bfloat16)
            every = pl.ds(top, slots)
            dqkv[1, every, lanes] = dk[...].astype(jnp.bfloat16)
            dqkv[2, every, lanes] = dv[...].astype(jnp.bfloat16)

        loop(items, attend)
        sums[l] = held[l, steps]
        for m, row in ((0, 0), (2, 1)):

            def add(t, carry):
                return carry + fold(dqkv[m, tile(t, ROW_TILE), :].astype(jnp.float32))

            late[2 * l + row] = lax.fori_loop(
                0, count // ROW_TILE, add, jnp.zeros((8, width), jnp.float32)
            )

        @pl.when(l == 0)
        def _():
            late_held[0] = jnp.sum(late[...], axis=1)
            last_sums.step(0)

        for m in range(3):
            slot = weights(base + 9 + m)
            for c, n in enumerate(chunks):
                g[:, n] += product(dqkv.at[m], slot, n)
                if m == 2:

                    @pl.when(l == 0)
                    def _():
                        pltpu.make_async_copy(g.at[:, n], grad.at[:, n], gsem.at[c]).start()

            if m + 1 < steps:

                @pl.when(l == 0)
                def _():
                    last_sums.step(m + 1)

    late[...] = jnp.zeros_like(late)
    loop(LAYERS, layer)
    for k in range(min(steps, 3), steps + 1):
        if k > 0:
            last_sums.step(k)
    late_sums[...] = late_held[steps]
    for c, n in enumerate(chunks):
        pltpu.make_async_copy(g.at[:, n], grad.at[:, n], gsem.at[c]).wait()


def backward(devices, wbuf, gain_attn, gain_ffn, first_sums, saved, rows, slots):
    count, width = saved[0].shape
    bf, f32 = jnp.bfloat16, jnp.float32
    blocks = slots // BLOCK
    places = digits(devices)
    steps = max(len(places), 1)
    any_ = pl.BlockSpec(memory_space=HBM)
    vm = pl.BlockSpec(memory_space=VMEM)
    return pl.pallas_call(
        functools.partial(backward_kernel, (rows, slots), places),
        out_shape=(
            jax.ShapeDtypeStruct((count, width), f32),
            jax.ShapeDtypeStruct((LAYERS, EARLY, width), f32),
            jax.ShapeDtypeStruct((8, width), f32),
        ),
        in_specs=[any_, vm, vm, vm] + [any_] * 6,
        out_specs=(any_, vm, vm),
        scratch_shapes=[
            VMEM((count, width), f32),
            VMEM((count, width), bf),
            VMEM((count, width), bf),
            VMEM((3, count, width), bf),
            VMEM((3, count, width), bf),
            VMEM((2, count, width), f32),
            VMEM((2, count, 128), f32),
            VMEM((2, 2, count, WIDTH), bf),
            VMEM((3, 2, width, WIDTH), bf),
            VMEM((3, blocks, WINDOW, 2 * BLOCK), bf),
            VMEM((slots, 128), f32),
            VMEM((slots, 128), f32),
            VMEM((EARLY, 8, width), f32),
            VMEM((8, 8, width), f32),
            VMEM((LAYERS, steps + 1, EARLY, width), f32),
            VMEM((LAYERS, steps, 4, EARLY, width), f32),
            VMEM((steps + 1, 8, width), f32),
            VMEM((steps, 4, 8, width), f32),
            DMA((3, 2)), DMA((3,)), DMA((2,)), DMA((2,)), DMA((2,)), DMA((3,)), DMA((2,)), DMA((4,)),
            DMA((LAYERS, steps, 4)), DMA((LAYERS, steps, 4)), DMA((steps, 4)), DMA((steps, 4)),
        ],
        compiler_params=pltpu.CompilerParams(
            vmem_limit_bytes=60 << 20,
            **({"collective_id": 1, "has_side_effects": True} if places else {}),
        ),
    )(wbuf, gain_attn, gain_ffn, first_sums, *saved)


def finish_kernel(unit, sums, late, query, value, out, inner, outer, attn, ffn):
    width = sums.shape[2]
    devices = width // unit
    for l in range(LAYERS):
        here = slice(l, l + 1)
        for row, ref in ((D_OUT, out), (D_OUTER, outer), (D_ATTN, attn), (D_FFN, ffn)):
            ref[here, :] = sums[l, row : row + 1, :]
        query[here, :] = late[2 * l : 2 * l + 1, :]
        value[here, :] = late[2 * l + 1 : 2 * l + 2, :]
        for b in range(inner.shape[1] // 128):
            block = None
            for piece in range(128 // unit):
                device, quarter = divmod(b * (128 // unit) + piece, inner.shape[1] // width)
                source = device * unit
                row = D_INNER + quarter
                first = source // 128 * 128
                x = sums[l, row : row + 1, first : first + 128]
                shift = (piece * unit - source) % 128
                if shift:
                    x = pltpu.roll(x, shift, axis=1)
                if block is None:
                    block = x
                else:
                    lane = lax.broadcasted_iota(jnp.int32, x.shape, 1)
                    block = jnp.where(lane >= piece * unit, x, block)
            inner[here, b * 128 : (b + 1) * 128] = block


def finish(unit, hidden, sums, late):
    width = sums.shape[2]
    vm = pl.BlockSpec(memory_space=VMEM)
    sizes = (width, width, width, hidden, width, width, width)
    return pl.pallas_call(
        functools.partial(finish_kernel, unit),
        out_shape=tuple(jax.ShapeDtypeStruct((LAYERS, n), jnp.float32) for n in sizes),
        in_specs=[vm, vm],
        out_specs=(vm,) * 7,
    )(sums, late)


def per_device(
    devices,
    tokens,
    lengths,
    w_query,
    w_key,
    w_value,
    w_out,
    w_inner,
    w_outer,
    bias_query,
    bias_value,
    bias_out,
    bias_inner,
    bias_outer,
    shift_attn,
    shift_ffn,
    gain_attn,
    gain_ffn,
    cotangent,
):
    rows, slots, width = tokens.shape
    hidden = bias_inner.shape[1]
    unit = w_query.shape[1]
    count = rows * slots
    vectors = (
        bias_query, bias_value, bias_out, bias_outer, shift_attn, shift_ffn, gain_attn, gain_ffn,
    )
    matrices = (w_query, w_key, w_value, w_out, w_inner, w_outer)
    wbuf, out, first_sums, *saved = forward(
        devices, lengths, matrices, tokens.reshape(count, width), cotangent.reshape(count, width),
        vectors, bias_inner, rows, slots,
    )
    wbuf = wbuf.reshape(LAYERS * GROUPS, width, WIDTH)
    grad, sums, late = backward(
        devices, wbuf, gain_attn, gain_ffn, first_sums, saved, rows, slots
    )
    return (
        out.reshape(rows, slots, width),
        grad.reshape(rows, slots, width),
        *finish(unit, hidden, sums, late),
    )


def solution(mesh):
    rows, whole = P("dp", None, None), P()
    weight = P(None, "dp", None)
    placed = (rows, P("dp", None)) + (weight,) * 6 + (whole,) * 9 + (rows,)
    return jax.shard_map(
        functools.partial(per_device, mesh.shape["dp"]),
        mesh=mesh,
        in_specs=placed,
        out_specs=(rows, rows) + (whole,) * 7,
        check_vma=False,
    )
```

```python
import functools

import jax
import jax.numpy as jnp
from jax import lax
from jax.experimental import pallas as pl
from jax.experimental.pallas import tpu as pltpu
from jax.sharding import PartitionSpec as P

HEADS = 16
LAYERS = 2
EPSILON = 1e-12
NEGATIVE = -1e9
PADDING_ID = 1000
MESH = pl.DeviceIdType.MESH
HBM = pltpu.MemorySpace.HBM
VMEM = pltpu.VMEM
DMA = pltpu.SemaphoreType.DMA

WIDTH = 512
GROUPS = 24
AT_OUT, AT_INNER, AT_OUTER = 6, 8, 16
BLOCK = 128
WINDOW = 256
ROW_TILE = 128
ROOT_HALF = 0.7071067811865476
DENSITY = 0.3989422804014327
B_Q, B_V, B_OUT, B_OUTER, S_ATTN, S_FFN, G_ATTN, G_FFN = range(8)
D_OUT, D_OUTER, D_ATTN, D_FFN, D_INNER = range(5)
EARLY = 8


def chip_dims(devices):
    bits = (devices // 2).bit_length() - 1
    first = -(-bits // 3)
    second = -(-(bits - first) // 2)
    return (1 << first, 1 << second, 1 << (bits - first - second))


RELAY = 4
ORDERS = ((0, 4, 2, 1, 3), (0, 4, 1, 2, 3), (1, 0, 4, 2, 3), (2, 0, 4, 1, 3))
STARTS = (0, 2, 4, 6, 8, 9)
DEPTH = STARTS[-1]
SLOTS = 4


class Gather:
    def __init__(self, dims, own, buf, ssem, rsem, total):
        self.dims, self.own, self.buf = dims, own, buf
        self.ssem, self.rsem, self.total = ssem, rsem, total
        self.me = lax.axis_index("dp")
        _, n1, n2 = dims
        self.core = lax.rem(self.me, 2)
        chip = self.me // 2
        self.at = (chip // (n1 * n2), lax.rem(chip // n2, n1), lax.rem(chip, n2))
        self.step = (n1 * n2 * 2, n2 * 2, 2)
        self.relay = dims[0] == 4
        self.orders = ORDERS
        if not self.relay:
            self.orders = tuple(tuple(d for d in order if d != RELAY) for order in ORDERS)
        self.phases = len(self.orders[0])
        rows, cols = own.shape[-2:]
        q, c = rows // 4, cols // 4
        if rows % 32 == 0:
            self.parts = (
                ((pl.ds(0, q), pl.ds(0, 3 * c)),),
                ((pl.ds(q, q), pl.ds(0, 3 * c)),),
                ((pl.ds(2 * q, q), pl.ds(0, cols)), (pl.ds(0, q), pl.ds(3 * c, c))),
                ((pl.ds(3 * q, q), pl.ds(0, cols)), (pl.ds(q, q), pl.ds(3 * c, c))),
            )
        else:
            self.parts = tuple(((pl.ds(0, rows), pl.ds(n * c, c)),) for n in range(4))

    def peers(self, dim):
        if dim == 3:
            return [self.me + 1 - 2 * self.core]
        out = []
        for d in range(1, self.dims[dim]):
            to = lax.rem(self.at[dim] + d, self.dims[dim])
            out.append(self.me + (to - self.at[dim]) * self.step[dim])
        return out

    def moves(self, g, s, p):
        order = self.orders[s]
        dim, full = order[p], order[:p]
        n0, n1, n2 = self.dims
        first = (0, n0, n0 + n1 - 1, n0 + n1 + n2 - 2, n0 - 1)[dim]
        where = [pl.ds(0, self.dims[d]) if d in full else self.at[d] for d in range(3)]
        slot = lax.rem(g, SLOTS)
        z = self.at[0]
        if dim == RELAY:
            middle = (z == 1) | (z == 2)
            where[0] = jnp.where(z < 2, 3, 0)
            targets = [self.me + (3 - where[0] - z) * self.step[0]]
            guards = [(middle, jnp.logical_not(middle))]
        else:
            targets = self.peers(dim)
            guards = [(None, None)] * len(targets)
            if dim == 0 and self.relay:
                guards = [
                    (jnp.abs(lax.rem(z + d, 4) - z) != 3, jnp.abs(lax.rem(z + 4 - d, 4) - z) != 3)
                    if d != 2
                    else (None, None)
                    for d in (1, 2, 3)
                ]
        out = []
        for n, sub in enumerate(self.parts[s], sum(len(part) for part in self.parts[:s])):
            dst = self.buf.at[(g,) + tuple(where) + (self.core,) + sub]
            src = self.own.at[(g,) + sub] if p == 0 else dst
            for i, (to, guard) in enumerate(zip(targets, guards)):
                copy = pltpu.make_async_remote_copy(
                    src_ref=src,
                    dst_ref=dst,
                    send_sem=self.ssem.at[slot, n, first + i],
                    recv_sem=self.rsem.at[slot, n, first + i],
                    device_id=(to,),
                    device_id_type=MESH,
                )
                out.append((copy, *guard))
        return out

    def greet(self):
        bar = pltpu.get_barrier_semaphore()
        for d in range(4):
            for to in self.peers(d):
                pl.semaphore_signal(bar, inc=1, device_id=(to,), device_id_type=MESH)

    def meet(self):
        pl.semaphore_wait(pltpu.get_barrier_semaphore(), sum(self.dims) - 3 + 1)

    def pump(self, step):
        for p in range(self.phases, -1, -1):
            g = step - (DEPTH if p == self.phases else STARTS[p])

            @pl.when((g >= 0) & (g < self.total))
            def _():
                for s in range(len(self.orders)):
                    if p > 0:
                        for copy, sends, receives in self.moves(g, s, p - 1):
                            if sends is None:
                                copy.wait()
                            else:
                                pl.when(sends)(copy.wait_send)
                                pl.when(receives)(copy.wait_recv)
                    if p < self.phases:
                        for copy, sends, _ in self.moves(g, s, p):
                            if sends is None:
                                copy.start()
                            else:
                                pl.when(sends)(copy.start)


def matmul(left, right):
    return jnp.dot(left, right, preferred_element_type=jnp.float32)


def matmul_nt(left, right):
    return lax.dot_general(
        left, right, (((1,), (1,)), ((), ())), preferred_element_type=jnp.float32
    )


def matmul_tn(left, right):
    return lax.dot_general(
        left, right, (((0,), (0,)), ((), ())), preferred_element_type=jnp.float32
    )


def loop(count, body):
    lax.fori_loop(0, count, lambda i, c: (body(i), c)[1], 0)


def tile(i, size):
    return pl.ds(pl.multiple_of(i * size, size), size)


def window_starts(slots):
    return [
        min(max(b * BLOCK - (WINDOW - BLOCK) // 2, 0), slots - WINDOW)
        for b in range(slots // BLOCK)
    ]


def pair_stack(rows):
    lane = lax.broadcasted_iota(jnp.int32, rows.shape, 1)
    zero = jnp.zeros_like(rows)
    half = rows.shape[1] // 2
    return jnp.concatenate(
        [jnp.where(lane < half, rows, zero), jnp.where(lane < half, zero, rows)], axis=0
    )


def pair_join(stacked):
    rows = stacked.shape[0] // 2
    lane = lax.broadcasted_iota(jnp.int32, (rows, stacked.shape[1]), 1)
    return jnp.where(lane < stacked.shape[1] // 2, stacked[:rows], stacked[rows:])


def permute_hidden(load, store, unit, hidden):
    devices = hidden // (4 * unit)
    for b in range(hidden // 128):
        block = None
        for piece in range(128 // unit):
            quarter, device = divmod(b * (128 // unit) + piece, devices)
            source = (4 * device + quarter) * unit
            x = load(source // 128)
            shift = (piece * unit - source) % 128
            if shift:
                x = pltpu.roll(x, shift, axis=1)
            if block is None:
                block = x
            else:
                lane = lax.broadcasted_iota(jnp.int32, x.shape, 1)
                block = jnp.where(lane >= piece * unit, x, block)
        store(b, block)


def store_block(own, first, b, x):
    per = WIDTH // 128
    own[first + b // per, :, b % per * 128 : (b % per + 1) * 128] = x.astype(own.dtype)


def slot_ids(lengths, r, position):
    segments = lengths.shape[1]
    number = jnp.zeros_like(position)
    end = jnp.int32(0)
    for j in range(segments):
        end = end + lengths[r, j]
        number = number + (position >= end).astype(jnp.int32)
    return jnp.where(number < segments - 1, number, PADDING_ID + position)


def fold(x):
    rows, width = x.shape
    return jnp.sum(x.reshape(rows // 8, 8, width), axis=0)


def norm_back(up, xhat, scale, gain_row):
    scaled = up * gain_row
    m1 = jnp.mean(scaled, axis=1, keepdims=True)
    m2 = jnp.mean(scaled * xhat, axis=1, keepdims=True)
    return scale * (scaled - m1 - xhat * m2)


def forward_kernel(
    dims, devices_dims,
    lengths, w_query, w_key, w_value, w_out, w_inner, w_outer, tokens, cotangent, *rest,
):
    vectors, rest = rest[:8], rest[8:]
    (
        inner_raw, wbuf, out, first_sums, saved_f, saved_qkv, saved_p, saved_x, saved_s, saved_d,
        h, a, qkv, o, z, u, w, p_stage, d_stage, x_stage, s_stage, own, id_row, id_col, inner_bias, cot,
        wsem, psem, dsem, xsem, ssem, qsem, tsem, hsem, csem, send_sem, recv_sem,
    ) = rest
    rows, slots = dims
    count = h.shape[0]
    pairs = HEADS // 2
    total = LAYERS * GROUPS
    gather = Gather(devices_dims, own, wbuf, send_sem, recv_sem, total)

    def wload(g):
        slot = lax.rem(g, 2)
        return pltpu.make_async_copy(wbuf.at[g], w.at[slot], wsem.at[slot])

    def weights(g):
        @pl.when(g + 1 < total)
        def _():
            wload(g + 1).start()

        wload(g).wait()
        return w[lax.rem(g, 2)].reshape(h.shape[1], WIDTH)

    def pump(half):
        gather.pump(half + DEPTH)

    gather.greet()
    load = pltpu.make_async_copy(tokens, a, tsem)
    load.start()
    load_cot = pltpu.make_async_copy(cotangent, cot, csem)
    load_cot.start()
    unit = own.shape[1]

    def cast(l, m):
        matrix = (w_query, w_key, w_value, w_out)[m]
        for c in range(2):
            own[l * GROUPS + 2 * m + c] = matrix[l, :, tile(c, WIDTH)].astype(jnp.bfloat16)

    def here(first, count):
        blocks = pl.ds(first, count)
        return pltpu.make_async_copy(
            own.at[blocks], wbuf.at[(blocks,) + gather.at + (gather.core,)], hsem
        )

    def start(i):
        gather.pump(i)

    for m in range(4):
        cast(0, m)
    here(0, AT_INNER).start()
    gather.meet()
    start(0)
    here(0, AT_INNER).wait()
    start(1)
    for l in range(LAYERS):
        at = l * GROUPS
        for m in range(4):
            if l > 0:
                cast(l, m)
        for c in range(2):
            for kc in range(4):
                piece = w_outer[l, kc * unit : (kc + 1) * unit, c * WIDTH : (c + 1) * WIDTH]
                own[at + AT_OUTER + 4 * c + kc] = piece.astype(jnp.bfloat16)
        permute_hidden(
            lambda b: w_inner[l, :, b * 128 : (b + 1) * 128],
            lambda b, x: store_block(own, at + AT_INNER, b, x),
            unit,
            w_inner.shape[2],
        )
        if l == 0:
            start(2)
    here(AT_INNER, total - AT_INNER).start()
    start(3)
    here(AT_INNER, total - AT_INNER).wait()

    def keep_bias(b, x):
        inner_bias[:, b * 128 : (b + 1) * 128] = x

    permute_hidden(
        lambda b: inner_raw[:, b * 128 : (b + 1) * 128], keep_bias, unit, w_inner.shape[2]
    )
    for r in range(rows):
        id_row[r] = slot_ids(lengths, r, lax.broadcasted_iota(jnp.int32, (8, slots), 1))
        id_col[r] = slot_ids(lengths, r, lax.broadcasted_iota(jnp.int32, (slots, 128), 0))
    first_sums[...] = jnp.zeros_like(first_sums)
    load_cot.wait()
    load.wait()

    def widen(i):
        h[tile(i, ROW_TILE), :] = a[tile(i, ROW_TILE), :].astype(jnp.float32)

    loop(count // ROW_TILE, widen)

    for i in range(4, DEPTH):
        start(i)
    pump(0)
    wload(0).start()

    def normalize(l, which):
        bias, gain, shift = ((B_OUT, G_ATTN, S_ATTN), (B_OUTER, G_FFN, S_FFN))[which]
        store_x = pltpu.make_async_copy(x_stage, saved_x.at[l, which], xsem)
        store_s = pltpu.make_async_copy(s_stage, saved_s.at[l, which], ssem)
        if which == 1:
            store_x.wait()
            store_s.wait()
        else:

            @pl.when(l > 0)
            def _():
                store_x.wait()
                store_s.wait()

        def body(i):
            t = tile(i, ROW_TILE)
            r = h[t, :] + vectors[bias][pl.ds(l, 1), :]
            centered = r - jnp.mean(r, axis=1, keepdims=True)
            var = jnp.mean(centered * centered, axis=1, keepdims=True)
            scale = lax.rsqrt(var + EPSILON)
            xhat = centered * scale
            x_stage[t, :] = xhat
            s_stage[t, :] = jnp.broadcast_to(scale, (ROW_TILE, 128))
            y = xhat * vectors[gain][pl.ds(l, 1), :] + vectors[shift][pl.ds(l, 1), :]
            h[t, :] = y
            a[t, :] = y.astype(jnp.bfloat16)
            if which == 1:

                @pl.when(l == LAYERS - 1)
                def _():
                    r = i // (slots // ROW_TILE)
                    real = slots - lengths[r, lengths.shape[1] - 1]
                    slot = lax.rem(i * ROW_TILE, slots) + lax.broadcasted_iota(
                        jnp.int32, (ROW_TILE, h.shape[1]), 0
                    )
                    up = jnp.where(slot < real, cot[t, :].astype(jnp.float32), 0.0)
                    down = norm_back(up, xhat, scale, vectors[gain][pl.ds(l, 1), :])
                    x_stage[t, :] = down
                    low = down.astype(jnp.bfloat16)
                    cot[t, :] = low
                    first_sums[0] += fold(up)
                    first_sums[1] += fold(low.astype(jnp.float32))

        loop(count // ROW_TILE, body)
        store_x.start()
        store_s.start()

    def layer(l):
        base = l * GROUPS

        @pl.when(l > 0)
        def _():
            for m in range(3):
                pltpu.make_async_copy(qkv.at[m], saved_qkv.at[l, m], qsem.at[m]).wait()

        def project(i):
            pump(base + i + 1)
            m = i // 2
            cols = tile(i % 2, WIDTH)
            bias_q = vectors[B_Q][pl.ds(l, 1), cols]
            bias_v = vectors[B_V][pl.ds(l, 1), cols]
            bias = jnp.where(m == 0, bias_q, jnp.where(m == 1, jnp.zeros_like(bias_v), bias_v))
            y = matmul(a[...], weights(base + i)) + bias
            y = y * jnp.where(m == 0, jnp.float32((h.shape[1] // HEADS) ** -0.5), jnp.float32(1))
            qkv[m, :, cols] = y.astype(jnp.bfloat16)

        loop(6, project)
        for m in range(3):
            pltpu.make_async_copy(qkv.at[m], saved_qkv.at[l, m], qsem.at[m]).start()

        def attend(i):
            @pl.when(lax.rem(i, 4) == 0)
            def _():
                pump(base + 7 + i // 4)


            r = i // pairs
            lanes = tile(lax.rem(i, pairs), 128)
            slot = lax.rem(i, 2)
            store_p = pltpu.make_async_copy(p_stage.at[slot], saved_p.at[l, i], psem.at[slot])

            @pl.when((i >= 2) | (l > 0))
            def _():
                store_p.wait()

            top = pl.multiple_of(r * slots, slots)
            starts = window_starts(slots)
            scores = [
                matmul_nt(
                    qkv[1, pl.ds(top + start, WINDOW), lanes],
                    pair_stack(qkv[0, pl.ds(top + b * BLOCK, BLOCK), lanes]),
                )
                for b, start in enumerate(starts)
            ]
            for b, start in enumerate(starts):
                vm = qkv[2, pl.ds(top + start, WINDOW), lanes]
                same = id_col[r, start : start + WINDOW, :] == id_row[r, :1, b * BLOCK : (b + 1) * BLOCK]
                s = jnp.where(jnp.concatenate([same, same], axis=1), scores[b], NEGATIVE)
                e = jnp.exp(s - jnp.max(s, axis=0, keepdims=True))
                p = e * (1.0 / jnp.sum(e, axis=0, keepdims=True))
                p = p.astype(jnp.bfloat16)
                p_stage[slot, b] = p
                o[pl.ds(top + b * BLOCK, BLOCK), lanes] = pair_join(matmul_tn(p, vm)).astype(jnp.bfloat16)
            store_p.start()

        loop(rows * pairs, attend)

        def attn_out(i):
            @pl.when(i == 1)
            def _():
                pump(base + 11)

            cols = tile(i, WIDTH)
            h[:, cols] += matmul(o[...], weights(base + AT_OUT + i))

        loop(2, attn_out)
        normalize(l, 0)

        def inner(i):
            pump(base + 12 + i)


            cols = tile(i, WIDTH)
            u[...] = matmul(a[...], weights(base + AT_INNER + i)) + inner_bias[pl.ds(l, 1), cols]
            slot = lax.rem(i, 2)
            store_d = pltpu.make_async_copy(d_stage.at[slot], saved_d.at[l, i], dsem.at[slot])

            @pl.when((i >= 2) | (l > 0))
            def _():
                store_d.wait()

            def activate(t):
                part = tile(t, ROW_TILE)
                x = u[part, :]
                cdf = 0.5 + 0.5 * lax.erf(x * ROOT_HALF)
                z[i // 2, part, tile(i % 2, WIDTH)] = (x * cdf).astype(jnp.bfloat16)
                slope = cdf + x * (DENSITY * jnp.exp(-0.5 * x * x))
                d_stage[slot, part, :] = slope.astype(jnp.bfloat16)

            loop(count // ROW_TILE, activate)
            store_d.start()

        loop(8, inner)

        def outer(i):
            @pl.when(i == 0)
            def _():
                pump(base + 20)

            @pl.when(i == 1)
            def _():
                pump(base + 21)

            @pl.when(i == 3)
            def _():
                pump(base + 22)

            @pl.when(i == 5)
            def _():
                pump(base + 23)

            @pl.when(i == 7)
            def _():
                pump(base + 24)


            cols = tile(i // 4, WIDTH)
            h[:, cols] += matmul(z[lax.rem(i, 4)], weights(base + AT_OUTER + i))

        loop(8, outer)
        normalize(l, 1)

    loop(LAYERS, layer)
    store = pltpu.make_async_copy(a, out, tsem)
    store.start()
    store_f = pltpu.make_async_copy(cot, saved_f, csem)
    store_f.start()
    last = LAYERS - 1
    for m in range(3):
        pltpu.make_async_copy(qkv.at[m], saved_qkv.at[last, m], qsem.at[m]).wait()
    for i in range(2):
        pltpu.make_async_copy(p_stage.at[i], saved_p.at[last, i], psem.at[i]).wait()
        pltpu.make_async_copy(d_stage.at[i], saved_d.at[last, i], dsem.at[i]).wait()
    pltpu.make_async_copy(x_stage, saved_x.at[last, 1], xsem).wait()
    pltpu.make_async_copy(s_stage, saved_s.at[last, 1], ssem).wait()
    store.wait()
    store_f.wait()


def forward(devices, lengths, matrices, tokens, cotangent, vectors, inner_bias, rows, slots):
    count, width = tokens.shape
    hidden = inner_bias.shape[-1]
    unit = matrices[0].shape[1]
    bf, f32 = jnp.bfloat16, jnp.float32
    blocks = slots // BLOCK
    devices_dims = chip_dims(devices)
    held = devices_dims + (2, unit, WIDTH)
    sems = sum(devices_dims) - 1
    any_ = pl.BlockSpec(memory_space=HBM)
    vm = pl.BlockSpec(memory_space=VMEM)
    return pl.pallas_call(
        functools.partial(forward_kernel, (rows, slots), devices_dims),
        out_shape=(
            jax.ShapeDtypeStruct((LAYERS * GROUPS,) + held, bf),
            jax.ShapeDtypeStruct((count, width), bf),
            jax.ShapeDtypeStruct((2, 8, width), f32),
            jax.ShapeDtypeStruct((count, width), bf),
            jax.ShapeDtypeStruct((LAYERS, 3, count, width), bf),
            jax.ShapeDtypeStruct((LAYERS, rows * HEADS // 2, blocks, WINDOW, 2 * BLOCK), bf),
            jax.ShapeDtypeStruct((LAYERS, 2, count, width), f32),
            jax.ShapeDtypeStruct((LAYERS, 2, count, 128), f32),
            jax.ShapeDtypeStruct((LAYERS, hidden // WIDTH, count, WIDTH), bf),
        ),
        in_specs=[pl.BlockSpec(memory_space=pltpu.SMEM)] + [vm] * 6 + [any_] * 2 + [vm] * 9,
        out_specs=(any_, any_, vm) + (any_,) * 6,
        scratch_shapes=[
            VMEM((count, width), f32),
            VMEM((count, width), bf),
            VMEM((3, count, width), bf),
            VMEM((count, width), bf),
            VMEM((hidden // width, count, width), bf),
            VMEM((count, WIDTH), f32),
            VMEM((2,) + held, bf),
            VMEM((2, blocks, WINDOW, 2 * BLOCK), bf),
            VMEM((2, count, WIDTH), bf),
            VMEM((count, width), f32),
            VMEM((count, 128), f32),
            VMEM((LAYERS * GROUPS, unit, WIDTH), bf),
            VMEM((rows, 8, slots), jnp.int32),
            VMEM((rows, slots, 128), jnp.int32),
            VMEM((LAYERS, hidden), f32),
            VMEM((count, width), bf),
            DMA((2,)), DMA((2,)), DMA((2,)), DMA, DMA, DMA((3,)), DMA, DMA, DMA,
            DMA((SLOTS, 6, sems)), DMA((SLOTS, 6, sems)),
        ],
        compiler_params=pltpu.CompilerParams(
            vmem_limit_bytes=58 << 20, collective_id=0, has_side_effects=True
        ),
    )(lengths, *matrices, tokens, cotangent, *vectors, inner_bias)


def digits(devices):
    out, stride = [], 1
    while stride < devices:
        size = 2 if stride == 1 else min(4, devices // stride)
        out.append((stride, size))
        stride *= size
    return out


class Exchange:
    def __init__(self, me, places, held, got, ssem, rsem):
        self.me, self.places = me, places
        self.held, self.got, self.ssem, self.rsem = held, got, ssem, rsem

    def copies(self, k):
        stride, size = self.places[k]
        digit = lax.rem(self.me // stride, size)
        out = []
        for d in range(1, size):
            to = self.me + (lax.rem(digit + d, size) - digit) * stride
            out.append(
                pltpu.make_async_remote_copy(
                    src_ref=self.held.at[k],
                    dst_ref=self.got.at[k, digit],
                    send_sem=self.ssem.at[k, d],
                    recv_sem=self.rsem.at[k, d],
                    device_id=(to,),
                    device_id_type=MESH,
                )
            )
        return out, digit, size

    def step(self, k):
        if k > 0:
            copies, digit, size = self.copies(k - 1)
            for c in copies:
                c.wait()
            self.got[k - 1, digit] = self.held[k - 1]
            total = self.got[k - 1, 0]
            for j in range(1, size):
                total = total + self.got[k - 1, j]
            self.held[k] = total
        if k < len(self.places):
            for c in self.copies(k)[0]:
                c.start()


def backward_kernel(
    dims, places,
    wbuf, gain_attn, gain_ffn, first_sums, saved_f, saved_qkv, saved_p, saved_x, saved_s, saved_d,
    grad, sums, late_sums,
    g, db, du, qkv, dqkv, x, sc, d, w, p, dk, dv, part, late,
    held, got, late_held, late_got,
    wsem, psem, dsem, xsem, ssem, qsem, csem, gsem, send_sem, recv_sem, late_send, late_recv,
):
    rows, slots = dims
    count, width = g.shape
    pairs = HEADS // 2
    per_layer = GROUPS // 2
    total = LAYERS * per_layer
    items = rows * pairs
    steps = len(places)
    chunk = 256
    chunks = [slice(c * chunk, (c + 1) * chunk) for c in range(width // chunk)]

    def wload(i):
        l = LAYERS - 1 - i // per_layer
        j = lax.rem(i, per_layer)
        outer = (j < 8) & (lax.rem(j, 2) == 0)
        ffn = jnp.where(outer, AT_OUTER + j // 2, AT_INNER + j // 2 * 2)
        block = l * GROUPS + jnp.where(j < 8, ffn, jnp.where(j == 8, AT_OUT, 2 * (j - 9)))
        slot = lax.rem(i, 3)
        apart = jnp.where(outer, 4, 1)
        return [
            pltpu.make_async_copy(wbuf.at[block + c * apart], w.at[slot, c], wsem.at[slot, c])
            for c in range(2)
        ]

    def weights(i):
        @pl.when(i + 2 < total)
        def _():
            for c in wload(i + 2):
                c.start()

        for c in wload(i):
            c.wait()
        return lax.rem(i, 3)

    def product(left, slot, n):
        return matmul_nt(left[:, :WIDTH], w[slot, 0, n, :]) + matmul_nt(left[:, WIDTH:], w[slot, 1, n, :])

    def xload(l, which):
        return (
            pltpu.make_async_copy(saved_x.at[l, which], x.at[which], xsem.at[which]),
            pltpu.make_async_copy(saved_s.at[l, which], sc.at[which], ssem.at[which]),
        )

    def dload(l, quarter):
        slot = lax.rem(quarter, 2)
        return pltpu.make_async_copy(saved_d.at[l, pl.ds(2 * quarter, 2)], d.at[slot], dsem.at[slot])

    def pload(l, i):
        slot = lax.rem(i, 3)
        return pltpu.make_async_copy(saved_p.at[l, i], p.at[slot], psem.at[slot])

    def qload(l):
        return [pltpu.make_async_copy(saved_qkv.at[l, m], qkv.at[m], qsem.at[m]) for m in range(3)]

    top_layer = LAYERS - 1
    opening = [
        pltpu.make_async_copy(saved_f, db, csem.at[0]),
        pltpu.make_async_copy(saved_x.at[top_layer, 1], g, csem.at[1]),
    ]
    opening[0].start()
    for c in wload(0):
        c.start()
    dload(top_layer, 0).start()
    for c in wload(1):
        c.start()
    opening[1].start()
    for c in xload(top_layer, 0):
        c.start()
    if top_layer:
        for c in xload(top_layer - 1, 1):
            c.start()
    me = lax.axis_index("dp")
    if steps:
        barrier = pltpu.get_barrier_semaphore()
        for stride, size in places:
            digit = lax.rem(me // stride, size)
            for k in range(1, size):
                to = me + (lax.rem(digit + k, size) - digit) * stride
                pl.semaphore_signal(barrier, inc=1, device_id=(to,), device_id_type=MESH)
    for c in opening:
        c.wait()
    part[D_FFN] = first_sums[0]
    part[D_OUTER] = first_sums[1]
    if steps:
        pl.semaphore_wait(barrier, sum(size - 1 for _, size in places))

    def normalize_back(l, which):
        gain = (gain_attn, gain_ffn)[which]
        row_shift = (D_ATTN, D_FFN)[which]
        row_bias = (D_OUT, D_OUTER)[which]
        for c in xload(l, which):
            c.wait()

        def body(i, carry):
            t = tile(i, ROW_TILE)
            up = g[t, :]
            xh = x[which, t, :]
            down = norm_back(up, xh, sc[which, t, :1], gain[pl.ds(l, 1), :])
            g[t, :] = down
            low = down.astype(jnp.bfloat16)
            db[t, :] = low
            return carry[0] + fold(up), carry[1] + fold(low.astype(jnp.float32))

        zero = jnp.zeros((8, width), jnp.float32)
        shift_sum, bias_sum = lax.fori_loop(0, count // ROW_TILE, body, (zero, zero))
        part[row_shift] = shift_sum
        part[row_bias] = bias_sum

        @pl.when(l > 0)
        def _():
            for c in xload(l - 1, which):
                c.start()

    last_sums = Exchange(me, places, late_held, late_got, late_send, late_recv)

    def layer(step):
        l = top_layer - step
        base = step * per_layer

        @pl.when(step > 0)
        def _():
            normalize_back(l, 1)

        def quarter(kc):
            @pl.when(kc + 1 < 4)
            def _():
                dload(l, kc + 1).start()

            @pl.when(kc == 1)
            def _():
                for c in qload(l):
                    c.start()

            slot = weights(base + 2 * kc)
            dload(l, kc).wait()
            for c, n in enumerate(chunks):
                within = slice(c * chunk % WIDTH, c * chunk % WIDTH + chunk)
                slope = d[lax.rem(kc, 2), c * chunk // WIDTH, :, within].astype(jnp.float32)
                low = (product(db, slot, n) * slope).astype(jnp.bfloat16)
                du[:, n] = low
                part[D_INNER + kc, :, n] = fold(low.astype(jnp.float32))
            slot = weights(base + 2 * kc + 1)
            for n in chunks:
                g[:, n] += product(du, slot, n)

        loop(4, quarter)

        @pl.when(l > 0)
        def _():
            dload(l - 1, 0).start()

        pload(l, 0).start()
        pload(l, 1).start()
        normalize_back(l, 0)
        slot = weights(base + 8)
        for n in chunks:
            du[:, n] = product(db, slot, n).astype(jnp.bfloat16)
        for c in qload(l):
            c.wait()
        early = Exchange(me, places, held.at[l], got.at[l], send_sem.at[l], recv_sem.at[l])
        held[l, 0] = jnp.sum(part[...], axis=1)
        early.step(0)

        def attend(i):
            for k in range(1, steps + 1):

                @pl.when(i == (items - 1) // steps * k)
                def _():
                    early.step(k)

            r = i // pairs
            lanes = tile(lax.rem(i, pairs), 128)
            slot = lax.rem(i, 3)

            @pl.when(i + 2 < items)
            def _():
                pload(l, i + 2).start()

            pload(l, i).wait()
            dk[...] = jnp.zeros_like(dk)
            dv[...] = jnp.zeros_like(dv)
            top = pl.multiple_of(r * slots, slots)
            starts = window_starts(slots)
            mine = [pl.ds(top + b * BLOCK, BLOCK) for b in range(len(starts))]
            reach = [pl.ds(top + start, WINDOW) for start in starts]
            stacked = [pair_stack(du[rows_, lanes]) for rows_ in mine]
            dps = [matmul_nt(qkv[2, keys, lanes], om) for keys, om in zip(reach, stacked)]
            for b, start in enumerate(starts):
                qm = pair_stack(qkv[0, mine[b], lanes])
                pb = p[slot, b]
                pf = pb.astype(jnp.float32)
                weighted = pf * dps[b]
                ds = weighted - pf * jnp.sum(weighted, axis=0, keepdims=True)
                ds = ds.astype(jnp.bfloat16)
                dk[start : start + WINDOW, :] += matmul(ds, qm)
                dv[start : start + WINDOW, :] += matmul(pb, stacked[b])
                dq = pair_join(matmul_tn(ds, qkv[1, reach[b], lanes]))
                dqkv[0, mine[b], lanes] = (dq * (width // HEADS) ** -0.5).astype(jnp.bfloat16)
            every = pl.ds(top, slots)
            dqkv[1, every, lanes] = dk[...].astype(jnp.bfloat16)
            dqkv[2, every, lanes] = dv[...].astype(jnp.bfloat16)

        loop(items, attend)
        sums[l] = held[l, steps]
        for m, row in ((0, 0), (2, 1)):

            def add(t, carry):
                return carry + fold(dqkv[m, tile(t, ROW_TILE), :].astype(jnp.float32))

            late[2 * l + row] = lax.fori_loop(
                0, count // ROW_TILE, add, jnp.zeros((8, width), jnp.float32)
            )

        @pl.when(l == 0)
        def _():
            late_held[0] = jnp.sum(late[...], axis=1)
            last_sums.step(0)

        for m in range(3):
            slot = weights(base + 9 + m)
            for c, n in enumerate(chunks):
                g[:, n] += product(dqkv.at[m], slot, n)
                if m == 2:

                    @pl.when(l == 0)
                    def _():
                        pltpu.make_async_copy(g.at[:, n], grad.at[:, n], gsem.at[c]).start()

            if m + 1 < steps:

                @pl.when(l == 0)
                def _():
                    last_sums.step(m + 1)

    late[...] = jnp.zeros_like(late)
    loop(LAYERS, layer)
    for k in range(min(steps, 3), steps + 1):
        if k > 0:
            last_sums.step(k)
    late_sums[...] = late_held[steps]
    for c, n in enumerate(chunks):
        pltpu.make_async_copy(g.at[:, n], grad.at[:, n], gsem.at[c]).wait()


def backward(devices, wbuf, gain_attn, gain_ffn, first_sums, saved, rows, slots):
    count, width = saved[0].shape
    bf, f32 = jnp.bfloat16, jnp.float32
    blocks = slots // BLOCK
    places = digits(devices)
    steps = max(len(places), 1)
    any_ = pl.BlockSpec(memory_space=HBM)
    vm = pl.BlockSpec(memory_space=VMEM)
    return pl.pallas_call(
        functools.partial(backward_kernel, (rows, slots), places),
        out_shape=(
            jax.ShapeDtypeStruct((count, width), f32),
            jax.ShapeDtypeStruct((LAYERS, EARLY, width), f32),
            jax.ShapeDtypeStruct((8, width), f32),
        ),
        in_specs=[any_, vm, vm, vm] + [any_] * 6,
        out_specs=(any_, vm, vm),
        scratch_shapes=[
            VMEM((count, width), f32),
            VMEM((count, width), bf),
            VMEM((count, width), bf),
            VMEM((3, count, width), bf),
            VMEM((3, count, width), bf),
            VMEM((2, count, width), f32),
            VMEM((2, count, 128), f32),
            VMEM((2, 2, count, WIDTH), bf),
            VMEM((3, 2, width, WIDTH), bf),
            VMEM((3, blocks, WINDOW, 2 * BLOCK), bf),
            VMEM((slots, 128), f32),
            VMEM((slots, 128), f32),
            VMEM((EARLY, 8, width), f32),
            VMEM((8, 8, width), f32),
            VMEM((LAYERS, steps + 1, EARLY, width), f32),
            VMEM((LAYERS, steps, 4, EARLY, width), f32),
            VMEM((steps + 1, 8, width), f32),
            VMEM((steps, 4, 8, width), f32),
            DMA((3, 2)), DMA((3,)), DMA((2,)), DMA((2,)), DMA((2,)), DMA((3,)), DMA((2,)), DMA((4,)),
            DMA((LAYERS, steps, 4)), DMA((LAYERS, steps, 4)), DMA((steps, 4)), DMA((steps, 4)),
        ],
        compiler_params=pltpu.CompilerParams(
            vmem_limit_bytes=60 << 20,
            **({"collective_id": 1, "has_side_effects": True} if places else {}),
        ),
    )(wbuf, gain_attn, gain_ffn, first_sums, *saved)


def finish_kernel(
    unit,
    sums, late, grad_in, result_in,
    grad, result, query, value, out, inner, outer, attn, ffn,
    grad_hold, result_hold, load_sem, store_sem,
):
    count, width = grad.shape
    part = count // 4
    moves = []
    for c in range(4):
        for n, (source, hold, target) in enumerate(
            ((result_in, result_hold, result), (grad_in, grad_hold, grad))
        ):
            rows_ = pl.ds(c * part, part)
            load = pltpu.make_async_copy(source.at[rows_], hold.at[rows_], load_sem.at[n, c])
            store = pltpu.make_async_copy(hold.at[rows_], target.at[rows_], store_sem.at[n, c])
            load.start()
            moves.append((load, store))
    devices = width // unit
    for l in range(LAYERS):
        here = slice(l, l + 1)
        for row, ref in ((D_OUT, out), (D_OUTER, outer), (D_ATTN, attn), (D_FFN, ffn)):
            ref[here, :] = sums[l, row : row + 1, :]
        query[here, :] = late[2 * l : 2 * l + 1, :]
        value[here, :] = late[2 * l + 1 : 2 * l + 2, :]
        for b in range(inner.shape[1] // 128):
            block = None
            for piece in range(128 // unit):
                device, quarter = divmod(b * (128 // unit) + piece, inner.shape[1] // width)
                source = device * unit
                row = D_INNER + quarter
                first = source // 128 * 128
                x = sums[l, row : row + 1, first : first + 128]
                shift = (piece * unit - source) % 128
                if shift:
                    x = pltpu.roll(x, shift, axis=1)
                if block is None:
                    block = x
                else:
                    lane = lax.broadcasted_iota(jnp.int32, x.shape, 1)
                    block = jnp.where(lane >= piece * unit, x, block)
            inner[here, b * 128 : (b + 1) * 128] = block
    for load, store in moves:
        load.wait()
        store.start()
    for _, store in moves:
        store.wait()


def finish(unit, hidden, sums, late, grad, result):
    width = sums.shape[2]
    vm = pl.BlockSpec(memory_space=VMEM)
    any_ = pl.BlockSpec(memory_space=HBM)
    sizes = (width, width, width, hidden, width, width, width)
    large = tuple(jax.ShapeDtypeStruct(x.shape, x.dtype) for x in (grad, result))
    return pl.pallas_call(
        functools.partial(finish_kernel, unit),
        out_shape=large + tuple(jax.ShapeDtypeStruct((LAYERS, n), jnp.float32) for n in sizes),
        in_specs=[vm, vm, any_, any_],
        out_specs=(any_, any_) + (vm,) * 7,
        scratch_shapes=[
            VMEM(grad.shape, grad.dtype),
            VMEM(result.shape, result.dtype),
            DMA((2, 4)),
            DMA((2, 4)),
        ],
    )(sums, late, grad, result)


def per_device(
    devices,
    tokens,
    lengths,
    w_query,
    w_key,
    w_value,
    w_out,
    w_inner,
    w_outer,
    bias_query,
    bias_value,
    bias_out,
    bias_inner,
    bias_outer,
    shift_attn,
    shift_ffn,
    gain_attn,
    gain_ffn,
    cotangent,
):
    rows, slots, width = tokens.shape
    hidden = bias_inner.shape[1]
    unit = w_query.shape[1]
    count = rows * slots
    vectors = (
        bias_query, bias_value, bias_out, bias_outer, shift_attn, shift_ffn, gain_attn, gain_ffn,
    )
    matrices = (w_query, w_key, w_value, w_out, w_inner, w_outer)
    wbuf, out, first_sums, *saved = forward(
        devices, lengths, matrices, tokens.reshape(count, width), cotangent.reshape(count, width),
        vectors, bias_inner, rows, slots,
    )
    wbuf = wbuf.reshape(LAYERS * GROUPS, width, WIDTH)
    grad, sums, late = backward(
        devices, wbuf, gain_attn, gain_ffn, first_sums, saved, rows, slots
    )
    grad, out, *small = finish(unit, hidden, sums, late, grad, out)
    return (out.reshape(rows, slots, width), grad.reshape(rows, slots, width), *small)


def solution(mesh):
    rows, whole = P("dp", None, None), P()
    weight = P(None, "dp", None)
    placed = (rows, P("dp", None)) + (weight,) * 6 + (whole,) * 9 + (rows,)
    return jax.shard_map(
        functools.partial(per_device, mesh.shape["dp"]),
        mesh=mesh,
        in_specs=placed,
        out_specs=(rows, rows) + (whole,) * 7,
        check_vma=False,
    )
```

```python
import functools

import jax
import jax.numpy as jnp
from jax import lax
from jax.experimental import pallas as pl
from jax.experimental.pallas import tpu as pltpu
from jax.sharding import PartitionSpec as P

HEADS = 16
LAYERS = 2
EPSILON = 1e-12
NEGATIVE = -1e9
PADDING_ID = 1000
MESH = pl.DeviceIdType.MESH
HBM = pltpu.MemorySpace.HBM
VMEM = pltpu.VMEM
DMA = pltpu.SemaphoreType.DMA

WIDTH = 512
GROUPS = 24
AT_OUT, AT_INNER, AT_OUTER = 6, 8, 16
BLOCK = 128
WINDOW = 256
ROW_TILE = 128
ROOT_HALF = 0.7071067811865476
DENSITY = 0.3989422804014327
B_Q, B_V, B_OUT, B_OUTER, S_ATTN, S_FFN, G_ATTN, G_FFN = range(8)
D_OUT, D_OUTER, D_ATTN, D_FFN, D_INNER = range(5)
EARLY = 8


def chip_dims(devices):
    bits = (devices // 2).bit_length() - 1
    first = -(-bits // 3)
    second = -(-(bits - first) // 2)
    return (1 << first, 1 << second, 1 << (bits - first - second))


RELAY = 4
ORDERS = ((0, 4, 2, 1, 3), (0, 4, 1, 2, 3), (1, 0, 4, 2, 3), (2, 0, 4, 1, 3))
STARTS = (0, 2, 4, 6, 8, 9)
DEPTH = STARTS[-1]
SLOTS = 4


class Gather:
    def __init__(self, dims, own, buf, ssem, rsem, total):
        self.dims, self.own, self.buf = dims, own, buf
        self.ssem, self.rsem, self.total = ssem, rsem, total
        self.me = lax.axis_index("dp")
        _, n1, n2 = dims
        self.core = lax.rem(self.me, 2)
        chip = self.me // 2
        self.at = (chip // (n1 * n2), lax.rem(chip // n2, n1), lax.rem(chip, n2))
        self.step = (n1 * n2 * 2, n2 * 2, 2)
        self.relay = dims[0] == 4
        self.orders = ORDERS
        if not self.relay:
            self.orders = tuple(tuple(d for d in order if d != RELAY) for order in ORDERS)
        self.phases = len(self.orders[0])
        rows, cols = own.shape[-2:]
        q, c = rows // 4, cols // 4
        if rows % 32 == 0:
            self.parts = (
                ((pl.ds(0, q), pl.ds(0, 3 * c)),),
                ((pl.ds(q, q), pl.ds(0, 3 * c)),),
                ((pl.ds(2 * q, q), pl.ds(0, cols)), (pl.ds(0, q), pl.ds(3 * c, c))),
                ((pl.ds(3 * q, q), pl.ds(0, cols)), (pl.ds(q, q), pl.ds(3 * c, c))),
            )
        else:
            self.parts = tuple(((pl.ds(0, rows), pl.ds(n * c, c)),) for n in range(4))

    def peers(self, dim):
        if dim == 3:
            return [self.me + 1 - 2 * self.core]
        out = []
        for d in range(1, self.dims[dim]):
            to = lax.rem(self.at[dim] + d, self.dims[dim])
            out.append(self.me + (to - self.at[dim]) * self.step[dim])
        return out

    def moves(self, g, s, p):
        order = self.orders[s]
        dim, full = order[p], order[:p]
        n0, n1, n2 = self.dims
        first = (0, n0, n0 + n1 - 1, n0 + n1 + n2 - 2, n0 - 1)[dim]
        where = [pl.ds(0, self.dims[d]) if d in full else self.at[d] for d in range(3)]
        slot = lax.rem(g, SLOTS)
        z = self.at[0]
        if dim == RELAY:
            middle = (z == 1) | (z == 2)
            where[0] = jnp.where(z < 2, 3, 0)
            targets = [self.me + (3 - where[0] - z) * self.step[0]]
            guards = [(middle, jnp.logical_not(middle))]
        else:
            targets = self.peers(dim)
            guards = [(None, None)] * len(targets)
            if dim == 0 and self.relay:
                guards = [
                    (jnp.abs(lax.rem(z + d, 4) - z) != 3, jnp.abs(lax.rem(z + 4 - d, 4) - z) != 3)
                    if d != 2
                    else (None, None)
                    for d in (1, 2, 3)
                ]
        out = []
        for n, sub in enumerate(self.parts[s], sum(len(part) for part in self.parts[:s])):
            dst = self.buf.at[(g,) + tuple(where) + (self.core,) + sub]
            src = self.own.at[(g,) + sub] if p == 0 else dst
            for i, (to, guard) in enumerate(zip(targets, guards)):
                copy = pltpu.make_async_remote_copy(
                    src_ref=src,
                    dst_ref=dst,
                    send_sem=self.ssem.at[slot, n, first + i],
                    recv_sem=self.rsem.at[slot, n, first + i],
                    device_id=(to,),
                    device_id_type=MESH,
                )
                out.append((copy, *guard))
        return out

    def greet(self):
        bar = pltpu.get_barrier_semaphore()
        for d in range(4):
            for to in self.peers(d):
                pl.semaphore_signal(bar, inc=1, device_id=(to,), device_id_type=MESH)

    def meet(self):
        pl.semaphore_wait(pltpu.get_barrier_semaphore(), sum(self.dims) - 3 + 1)

    def pump(self, step):
        for p in range(self.phases, -1, -1):
            g = step - (DEPTH if p == self.phases else STARTS[p])

            @pl.when((g >= 0) & (g < self.total))
            def _():
                for s in range(len(self.orders)):
                    if p > 0:
                        for copy, sends, receives in self.moves(g, s, p - 1):
                            if sends is None:
                                copy.wait()
                            else:
                                pl.when(sends)(copy.wait_send)
                                pl.when(receives)(copy.wait_recv)
                    if p < self.phases:
                        for copy, sends, _ in self.moves(g, s, p):
                            if sends is None:
                                copy.start()
                            else:
                                pl.when(sends)(copy.start)


def matmul(left, right):
    return jnp.dot(left, right, preferred_element_type=jnp.float32)


def matmul_nt(left, right):
    return lax.dot_general(
        left, right, (((1,), (1,)), ((), ())), preferred_element_type=jnp.float32
    )


def matmul_tn(left, right):
    return lax.dot_general(
        left, right, (((0,), (0,)), ((), ())), preferred_element_type=jnp.float32
    )


def loop(count, body):
    lax.fori_loop(0, count, lambda i, c: (body(i), c)[1], 0)


def tile(i, size):
    return pl.ds(pl.multiple_of(i * size, size), size)


def window_starts(slots):
    return [
        min(max(b * BLOCK - (WINDOW - BLOCK) // 2, 0), slots - WINDOW)
        for b in range(slots // BLOCK)
    ]


def pair_stack(rows):
    lane = lax.broadcasted_iota(jnp.int32, rows.shape, 1)
    zero = jnp.zeros_like(rows)
    half = rows.shape[1] // 2
    return jnp.concatenate(
        [jnp.where(lane < half, rows, zero), jnp.where(lane < half, zero, rows)], axis=0
    )


def pair_join(stacked):
    rows = stacked.shape[0] // 2
    lane = lax.broadcasted_iota(jnp.int32, (rows, stacked.shape[1]), 1)
    return jnp.where(lane < stacked.shape[1] // 2, stacked[:rows], stacked[rows:])


def permute_hidden(load, store, unit, hidden):
    devices = hidden // (4 * unit)
    for b in range(hidden // 128):
        block = None
        for piece in range(128 // unit):
            quarter, device = divmod(b * (128 // unit) + piece, devices)
            source = (4 * device + quarter) * unit
            x = load(source // 128)
            shift = (piece * unit - source) % 128
            if shift:
                x = pltpu.roll(x, shift, axis=1)
            if block is None:
                block = x
            else:
                lane = lax.broadcasted_iota(jnp.int32, x.shape, 1)
                block = jnp.where(lane >= piece * unit, x, block)
        store(b, block)


def store_block(own, first, b, x):
    per = WIDTH // 128
    own[first + b // per, :, b % per * 128 : (b % per + 1) * 128] = x.astype(own.dtype)


def slot_ids(lengths, r, position):
    segments = lengths.shape[1]
    number = jnp.zeros_like(position)
    end = jnp.int32(0)
    for j in range(segments):
        end = end + lengths[r, j]
        number = number + (position >= end).astype(jnp.int32)
    return jnp.where(number < segments - 1, number, PADDING_ID + position)


def fold(x):
    rows, width = x.shape
    return jnp.sum(x.reshape(rows // 8, 8, width), axis=0)


def norm_back(up, xhat, scale, gain_row):
    scaled = up * gain_row
    m1 = jnp.mean(scaled, axis=1, keepdims=True)
    m2 = jnp.mean(scaled * xhat, axis=1, keepdims=True)
    return scale * (scaled - m1 - xhat * m2)


def forward_kernel(
    dims, devices_dims,
    lengths, w_query, w_key, w_value, w_out, w_inner, w_outer, tokens, cotangent, *rest,
):
    vectors, rest = rest[:8], rest[8:]
    (
        inner_raw, wbuf, out, first_sums, saved_f, saved_qkv, saved_p, saved_x, saved_s, saved_d,
        h, a, qkv, o, z, u, w, p_stage, d_stage, x_stage, s_stage, own, id_row, id_col, inner_bias, cot,
        wsem, psem, dsem, xsem, ssem, qsem, tsem, hsem, csem, send_sem, recv_sem,
    ) = rest
    rows, slots = dims
    count = h.shape[0]
    pairs = HEADS // 2
    total = LAYERS * GROUPS
    gather = Gather(devices_dims, own, wbuf, send_sem, recv_sem, total)

    def wload(g):
        slot = lax.rem(g, 2)
        return pltpu.make_async_copy(wbuf.at[g], w.at[slot], wsem.at[slot])

    def weights(g):
        @pl.when(g + 1 < total)
        def _():
            wload(g + 1).start()

        wload(g).wait()
        return w[lax.rem(g, 2)].reshape(h.shape[1], WIDTH)

    def pump(half):
        gather.pump(half + DEPTH)

    gather.greet()
    load = pltpu.make_async_copy(tokens, a, tsem)
    load.start()
    load_cot = pltpu.make_async_copy(cotangent, cot, csem)
    load_cot.start()
    unit = own.shape[1]

    def cast(l, m):
        matrix = (w_query, w_key, w_value, w_out)[m]
        for c in range(2):
            own[l * GROUPS + 2 * m + c] = matrix[l, :, tile(c, WIDTH)].astype(jnp.bfloat16)

    def here(first, count):
        blocks = pl.ds(first, count)
        return pltpu.make_async_copy(
            own.at[blocks], wbuf.at[(blocks,) + gather.at + (gather.core,)], hsem
        )

    def start(i):
        gather.pump(i)

    for m in range(4):
        cast(0, m)
    here(0, AT_INNER).start()
    gather.meet()
    start(0)
    here(0, AT_INNER).wait()
    start(1)
    for l in range(LAYERS):
        at = l * GROUPS
        for m in range(4):
            if l > 0:
                cast(l, m)
        for c in range(2):
            for kc in range(4):
                piece = w_outer[l, kc * unit : (kc + 1) * unit, c * WIDTH : (c + 1) * WIDTH]
                own[at + AT_OUTER + 4 * c + kc] = piece.astype(jnp.bfloat16)
        permute_hidden(
            lambda b: w_inner[l, :, b * 128 : (b + 1) * 128],
            lambda b, x: store_block(own, at + AT_INNER, b, x),
            unit,
            w_inner.shape[2],
        )
        if l == 0:
            start(2)
    here(AT_INNER, total - AT_INNER).start()
    start(3)
    here(AT_INNER, total - AT_INNER).wait()

    def keep_bias(b, x):
        inner_bias[:, b * 128 : (b + 1) * 128] = x

    permute_hidden(
        lambda b: inner_raw[:, b * 128 : (b + 1) * 128], keep_bias, unit, w_inner.shape[2]
    )
    for r in range(rows):
        id_row[r] = slot_ids(lengths, r, lax.broadcasted_iota(jnp.int32, (8, slots), 1))
        id_col[r] = slot_ids(lengths, r, lax.broadcasted_iota(jnp.int32, (slots, 128), 0))
    first_sums[...] = jnp.zeros_like(first_sums)
    load_cot.wait()
    load.wait()

    def widen(i):
        h[tile(i, ROW_TILE), :] = a[tile(i, ROW_TILE), :].astype(jnp.float32)

    loop(count // ROW_TILE, widen)

    for i in range(4, DEPTH):
        start(i)
    pump(0)
    wload(0).start()

    def normalize(l, which):
        bias, gain, shift = ((B_OUT, G_ATTN, S_ATTN), (B_OUTER, G_FFN, S_FFN))[which]
        store_x = pltpu.make_async_copy(x_stage, saved_x.at[l, which], xsem)
        store_s = pltpu.make_async_copy(s_stage, saved_s.at[l, which], ssem)
        if which == 1:
            store_x.wait()
            store_s.wait()
        else:

            @pl.when(l > 0)
            def _():
                store_x.wait()
                store_s.wait()

        def body(i):
            t = tile(i, ROW_TILE)
            r = h[t, :] + vectors[bias][pl.ds(l, 1), :]
            centered = r - jnp.mean(r, axis=1, keepdims=True)
            var = jnp.mean(centered * centered, axis=1, keepdims=True)
            scale = lax.rsqrt(var + EPSILON)
            xhat = centered * scale
            x_stage[t, :] = xhat
            s_stage[t, :] = jnp.broadcast_to(scale, (ROW_TILE, 128))
            y = xhat * vectors[gain][pl.ds(l, 1), :] + vectors[shift][pl.ds(l, 1), :]
            h[t, :] = y
            a[t, :] = y.astype(jnp.bfloat16)
            if which == 1:

                @pl.when(l == LAYERS - 1)
                def _():
                    r = i // (slots // ROW_TILE)
                    real = slots - lengths[r, lengths.shape[1] - 1]
                    slot = lax.rem(i * ROW_TILE, slots) + lax.broadcasted_iota(
                        jnp.int32, (ROW_TILE, h.shape[1]), 0
                    )
                    up = jnp.where(slot < real, cot[t, :].astype(jnp.float32), 0.0)
                    down = norm_back(up, xhat, scale, vectors[gain][pl.ds(l, 1), :])
                    x_stage[t, :] = down
                    low = down.astype(jnp.bfloat16)
                    cot[t, :] = low
                    first_sums[0] += fold(up)
                    first_sums[1] += fold(low.astype(jnp.float32))

        loop(count // ROW_TILE, body)
        store_x.start()
        store_s.start()

    def layer(l):
        base = l * GROUPS

        @pl.when(l > 0)
        def _():
            for m in range(3):
                pltpu.make_async_copy(qkv.at[m], saved_qkv.at[l, m], qsem.at[m]).wait()

        def project(i):
            pump(base + i + 1)
            m = i // 2
            cols = tile(i % 2, WIDTH)
            bias_q = vectors[B_Q][pl.ds(l, 1), cols]
            bias_v = vectors[B_V][pl.ds(l, 1), cols]
            bias = jnp.where(m == 0, bias_q, jnp.where(m == 1, jnp.zeros_like(bias_v), bias_v))
            y = matmul(a[...], weights(base + i)) + bias
            y = y * jnp.where(m == 0, jnp.float32((h.shape[1] // HEADS) ** -0.5), jnp.float32(1))
            qkv[m, :, cols] = y.astype(jnp.bfloat16)

        loop(6, project)
        for m in range(3):
            pltpu.make_async_copy(qkv.at[m], saved_qkv.at[l, m], qsem.at[m]).start()

        def attend(i):
            @pl.when(lax.rem(i, 4) == 2)
            def _():
                pump(base + 7 + i // 4)


            r = i // pairs
            lanes = tile(lax.rem(i, pairs), 128)
            slot = lax.rem(i, 2)
            store_p = pltpu.make_async_copy(p_stage.at[slot], saved_p.at[l, i], psem.at[slot])

            @pl.when((i >= 2) | (l > 0))
            def _():
                store_p.wait()

            top = pl.multiple_of(r * slots, slots)
            starts = window_starts(slots)
            scores = [
                matmul_nt(
                    qkv[1, pl.ds(top + start, WINDOW), lanes],
                    pair_stack(qkv[0, pl.ds(top + b * BLOCK, BLOCK), lanes]),
                )
                for b, start in enumerate(starts)
            ]
            for b, start in enumerate(starts):
                vm = qkv[2, pl.ds(top + start, WINDOW), lanes]
                same = id_col[r, start : start + WINDOW, :] == id_row[r, :1, b * BLOCK : (b + 1) * BLOCK]
                s = jnp.where(jnp.concatenate([same, same], axis=1), scores[b], NEGATIVE)
                e = jnp.exp(s - jnp.max(s, axis=0, keepdims=True))
                p = e * (1.0 / jnp.sum(e, axis=0, keepdims=True))
                p = p.astype(jnp.bfloat16)
                p_stage[slot, b] = p
                o[pl.ds(top + b * BLOCK, BLOCK), lanes] = pair_join(matmul_tn(p, vm)).astype(jnp.bfloat16)
            store_p.start()

        loop(rows * pairs, attend)

        def attn_out(i):
            @pl.when(i == 1)
            def _():
                pump(base + 11)

            cols = tile(i, WIDTH)
            h[:, cols] += matmul(o[...], weights(base + AT_OUT + i))

        loop(2, attn_out)
        normalize(l, 0)

        def inner(i):
            pump(base + 12 + i)


            cols = tile(i, WIDTH)
            u[...] = matmul(a[...], weights(base + AT_INNER + i)) + inner_bias[pl.ds(l, 1), cols]
            slot = lax.rem(i, 2)
            store_d = pltpu.make_async_copy(d_stage.at[slot], saved_d.at[l, i], dsem.at[slot])

            @pl.when((i >= 2) | (l > 0))
            def _():
                store_d.wait()

            def activate(t):
                part = tile(t, ROW_TILE)
                x = u[part, :]
                cdf = 0.5 + 0.5 * lax.erf(x * ROOT_HALF)
                z[i // 2, part, tile(i % 2, WIDTH)] = (x * cdf).astype(jnp.bfloat16)
                slope = cdf + x * (DENSITY * jnp.exp(-0.5 * x * x))
                d_stage[slot, part, :] = slope.astype(jnp.bfloat16)

            loop(count // ROW_TILE, activate)
            store_d.start()

        loop(8, inner)

        def outer(i):
            @pl.when(i == 0)
            def _():
                pump(base + 20)

            @pl.when(i == 1)
            def _():
                pump(base + 21)

            @pl.when(i == 3)
            def _():
                pump(base + 22)

            @pl.when(i == 5)
            def _():
                pump(base + 23)

            @pl.when(i == 7)
            def _():
                pump(base + 24)


            cols = tile(i // 4, WIDTH)
            h[:, cols] += matmul(z[lax.rem(i, 4)], weights(base + AT_OUTER + i))

        loop(8, outer)
        normalize(l, 1)

    loop(LAYERS, layer)
    store = pltpu.make_async_copy(a, out, tsem)
    store.start()
    store_f = pltpu.make_async_copy(cot, saved_f, csem)
    store_f.start()
    last = LAYERS - 1
    for m in range(3):
        pltpu.make_async_copy(qkv.at[m], saved_qkv.at[last, m], qsem.at[m]).wait()
    for i in range(2):
        pltpu.make_async_copy(p_stage.at[i], saved_p.at[last, i], psem.at[i]).wait()
        pltpu.make_async_copy(d_stage.at[i], saved_d.at[last, i], dsem.at[i]).wait()
    pltpu.make_async_copy(x_stage, saved_x.at[last, 1], xsem).wait()
    pltpu.make_async_copy(s_stage, saved_s.at[last, 1], ssem).wait()
    store.wait()
    store_f.wait()


def forward(devices, lengths, matrices, tokens, cotangent, vectors, inner_bias, rows, slots):
    count, width = tokens.shape
    hidden = inner_bias.shape[-1]
    unit = matrices[0].shape[1]
    bf, f32 = jnp.bfloat16, jnp.float32
    blocks = slots // BLOCK
    devices_dims = chip_dims(devices)
    held = devices_dims + (2, unit, WIDTH)
    sems = sum(devices_dims) - 1
    any_ = pl.BlockSpec(memory_space=HBM)
    vm = pl.BlockSpec(memory_space=VMEM)
    return pl.pallas_call(
        functools.partial(forward_kernel, (rows, slots), devices_dims),
        out_shape=(
            jax.ShapeDtypeStruct((LAYERS * GROUPS,) + held, bf),
            jax.ShapeDtypeStruct((count, width), bf),
            jax.ShapeDtypeStruct((2, 8, width), f32),
            jax.ShapeDtypeStruct((count, width), bf),
            jax.ShapeDtypeStruct((LAYERS, 3, count, width), bf),
            jax.ShapeDtypeStruct((LAYERS, rows * HEADS // 2, blocks, WINDOW, 2 * BLOCK), bf),
            jax.ShapeDtypeStruct((LAYERS, 2, count, width), f32),
            jax.ShapeDtypeStruct((LAYERS, 2, count, 128), f32),
            jax.ShapeDtypeStruct((LAYERS, hidden // WIDTH, count, WIDTH), bf),
        ),
        in_specs=[pl.BlockSpec(memory_space=pltpu.SMEM)] + [vm] * 6 + [any_] * 2 + [vm] * 9,
        out_specs=(any_, any_, vm) + (any_,) * 6,
        scratch_shapes=[
            VMEM((count, width), f32),
            VMEM((count, width), bf),
            VMEM((3, count, width), bf),
            VMEM((count, width), bf),
            VMEM((hidden // width, count, width), bf),
            VMEM((count, WIDTH), f32),
            VMEM((2,) + held, bf),
            VMEM((2, blocks, WINDOW, 2 * BLOCK), bf),
            VMEM((2, count, WIDTH), bf),
            VMEM((count, width), f32),
            VMEM((count, 128), f32),
            VMEM((LAYERS * GROUPS, unit, WIDTH), bf),
            VMEM((rows, 8, slots), jnp.int32),
            VMEM((rows, slots, 128), jnp.int32),
            VMEM((LAYERS, hidden), f32),
            VMEM((count, width), bf),
            DMA((2,)), DMA((2,)), DMA((2,)), DMA, DMA, DMA((3,)), DMA, DMA, DMA,
            DMA((SLOTS, 6, sems)), DMA((SLOTS, 6, sems)),
        ],
        compiler_params=pltpu.CompilerParams(
            vmem_limit_bytes=58 << 20, collective_id=0, has_side_effects=True
        ),
    )(lengths, *matrices, tokens, cotangent, *vectors, inner_bias)


def digits(devices):
    out, stride = [], 1
    while stride < devices:
        size = 2 if stride == 1 else min(4, devices // stride)
        out.append((stride, size))
        stride *= size
    return out


class Exchange:
    def __init__(self, me, places, held, got, ssem, rsem):
        self.me, self.places = me, places
        self.held, self.got, self.ssem, self.rsem = held, got, ssem, rsem

    def copies(self, k):
        stride, size = self.places[k]
        digit = lax.rem(self.me // stride, size)
        out = []
        for d in range(1, size):
            to = self.me + (lax.rem(digit + d, size) - digit) * stride
            out.append(
                pltpu.make_async_remote_copy(
                    src_ref=self.held.at[k],
                    dst_ref=self.got.at[k, digit],
                    send_sem=self.ssem.at[k, d],
                    recv_sem=self.rsem.at[k, d],
                    device_id=(to,),
                    device_id_type=MESH,
                )
            )
        return out, digit, size

    def step(self, k):
        if k > 0:
            copies, digit, size = self.copies(k - 1)
            for c in copies:
                c.wait()
            self.got[k - 1, digit] = self.held[k - 1]
            total = self.got[k - 1, 0]
            for j in range(1, size):
                total = total + self.got[k - 1, j]
            self.held[k] = total
        if k < len(self.places):
            for c in self.copies(k)[0]:
                c.start()


def backward_kernel(
    dims, places,
    wbuf, gain_attn, gain_ffn, first_sums, saved_f, saved_qkv, saved_p, saved_x, saved_s, saved_d,
    grad, sums, late_sums,
    g, db, du, qkv, dqkv, x, sc, d, w, p, dk, dv, part, late,
    held, got, late_held, late_got,
    wsem, psem, dsem, xsem, ssem, qsem, csem, gsem, send_sem, recv_sem, late_send, late_recv,
):
    rows, slots = dims
    count, width = g.shape
    pairs = HEADS // 2
    per_layer = GROUPS // 2
    total = LAYERS * per_layer
    items = rows * pairs
    steps = len(places)
    chunk = 256
    chunks = [slice(c * chunk, (c + 1) * chunk) for c in range(width // chunk)]

    def wload(i):
        l = LAYERS - 1 - i // per_layer
        j = lax.rem(i, per_layer)
        outer = (j < 8) & (lax.rem(j, 2) == 0)
        ffn = jnp.where(outer, AT_OUTER + j // 2, AT_INNER + j // 2 * 2)
        block = l * GROUPS + jnp.where(j < 8, ffn, jnp.where(j == 8, AT_OUT, 2 * (j - 9)))
        slot = lax.rem(i, 3)
        apart = jnp.where(outer, 4, 1)
        return [
            pltpu.make_async_copy(wbuf.at[block + c * apart], w.at[slot, c], wsem.at[slot, c])
            for c in range(2)
        ]

    def weights(i):
        @pl.when(i + 2 < total)
        def _():
            for c in wload(i + 2):
                c.start()

        for c in wload(i):
            c.wait()
        return lax.rem(i, 3)

    def product(left, slot, n):
        return matmul_nt(left[:, :WIDTH], w[slot, 0, n, :]) + matmul_nt(left[:, WIDTH:], w[slot, 1, n, :])

    def xload(l, which):
        return (
            pltpu.make_async_copy(saved_x.at[l, which], x.at[which], xsem.at[which]),
            pltpu.make_async_copy(saved_s.at[l, which], sc.at[which], ssem.at[which]),
        )

    def dload(l, quarter):
        slot = lax.rem(quarter, 2)
        return pltpu.make_async_copy(saved_d.at[l, pl.ds(2 * quarter, 2)], d.at[slot], dsem.at[slot])

    def pload(l, i):
        slot = lax.rem(i, 3)
        return pltpu.make_async_copy(saved_p.at[l, i], p.at[slot], psem.at[slot])

    def qload(l):
        return [pltpu.make_async_copy(saved_qkv.at[l, m], qkv.at[m], qsem.at[m]) for m in range(3)]

    top_layer = LAYERS - 1
    opening = [
        pltpu.make_async_copy(saved_f, db, csem.at[0]),
        pltpu.make_async_copy(saved_x.at[top_layer, 1], g, csem.at[1]),
    ]
    opening[0].start()
    for c in wload(0):
        c.start()
    dload(top_layer, 0).start()
    for c in wload(1):
        c.start()
    opening[1].start()
    for c in xload(top_layer, 0):
        c.start()
    if top_layer:
        for c in xload(top_layer - 1, 1):
            c.start()
    me = lax.axis_index("dp")
    if steps:
        barrier = pltpu.get_barrier_semaphore()
        for stride, size in places:
            digit = lax.rem(me // stride, size)
            for k in range(1, size):
                to = me + (lax.rem(digit + k, size) - digit) * stride
                pl.semaphore_signal(barrier, inc=1, device_id=(to,), device_id_type=MESH)
    for c in opening:
        c.wait()
    part[D_FFN] = first_sums[0]
    part[D_OUTER] = first_sums[1]
    if steps:
        pl.semaphore_wait(barrier, sum(size - 1 for _, size in places))

    def normalize_back(l, which):
        gain = (gain_attn, gain_ffn)[which]
        row_shift = (D_ATTN, D_FFN)[which]
        row_bias = (D_OUT, D_OUTER)[which]
        for c in xload(l, which):
            c.wait()

        def body(i, carry):
            t = tile(i, ROW_TILE)
            up = g[t, :]
            xh = x[which, t, :]
            down = norm_back(up, xh, sc[which, t, :1], gain[pl.ds(l, 1), :])
            g[t, :] = down
            low = down.astype(jnp.bfloat16)
            db[t, :] = low
            return carry[0] + fold(up), carry[1] + fold(low.astype(jnp.float32))

        zero = jnp.zeros((8, width), jnp.float32)
        shift_sum, bias_sum = lax.fori_loop(0, count // ROW_TILE, body, (zero, zero))
        part[row_shift] = shift_sum
        part[row_bias] = bias_sum

        @pl.when(l > 0)
        def _():
            for c in xload(l - 1, which):
                c.start()

    last_sums = Exchange(me, places, late_held, late_got, late_send, late_recv)

    def layer(step):
        l = top_layer - step
        base = step * per_layer

        @pl.when(step > 0)
        def _():
            normalize_back(l, 1)

        def quarter(kc):
            @pl.when(kc + 1 < 4)
            def _():
                dload(l, kc + 1).start()

            @pl.when(kc == 1)
            def _():
                for c in qload(l):
                    c.start()

            slot = weights(base + 2 * kc)
            dload(l, kc).wait()
            for c, n in enumerate(chunks):
                within = slice(c * chunk % WIDTH, c * chunk % WIDTH + chunk)
                slope = d[lax.rem(kc, 2), c * chunk // WIDTH, :, within].astype(jnp.float32)
                low = (product(db, slot, n) * slope).astype(jnp.bfloat16)
                du[:, n] = low
                part[D_INNER + kc, :, n] = fold(low.astype(jnp.float32))
            slot = weights(base + 2 * kc + 1)
            for n in chunks:
                g[:, n] += product(du, slot, n)

        loop(4, quarter)

        @pl.when(l > 0)
        def _():
            dload(l - 1, 0).start()

        pload(l, 0).start()
        pload(l, 1).start()
        normalize_back(l, 0)
        slot = weights(base + 8)
        for n in chunks:
            du[:, n] = product(db, slot, n).astype(jnp.bfloat16)
        for c in qload(l):
            c.wait()
        early = Exchange(me, places, held.at[l], got.at[l], send_sem.at[l], recv_sem.at[l])
        held[l, 0] = jnp.sum(part[...], axis=1)
        early.step(0)

        def attend(i):
            for k in range(1, steps + 1):

                @pl.when(i == (items - 1) // steps * k)
                def _():
                    early.step(k)

            r = i // pairs
            lanes = tile(lax.rem(i, pairs), 128)
            slot = lax.rem(i, 3)

            @pl.when(i + 2 < items)
            def _():
                pload(l, i + 2).start()

            pload(l, i).wait()
            dk[...] = jnp.zeros_like(dk)
            dv[...] = jnp.zeros_like(dv)
            top = pl.multiple_of(r * slots, slots)
            starts = window_starts(slots)
            mine = [pl.ds(top + b * BLOCK, BLOCK) for b in range(len(starts))]
            reach = [pl.ds(top + start, WINDOW) for start in starts]
            stacked = [pair_stack(du[rows_, lanes]) for rows_ in mine]
            dps = [matmul_nt(qkv[2, keys, lanes], om) for keys, om in zip(reach, stacked)]
            for b, start in enumerate(starts):
                qm = pair_stack(qkv[0, mine[b], lanes])
                pb = p[slot, b]
                pf = pb.astype(jnp.float32)
                weighted = pf * dps[b]
                ds = weighted - pf * jnp.sum(weighted, axis=0, keepdims=True)
                ds = ds.astype(jnp.bfloat16)
                dk[start : start + WINDOW, :] += matmul(ds, qm)
                dv[start : start + WINDOW, :] += matmul(pb, stacked[b])
                dq = pair_join(matmul_tn(ds, qkv[1, reach[b], lanes]))
                dqkv[0, mine[b], lanes] = (dq * (width // HEADS) ** -0.5).astype(jnp.bfloat16)
            every = pl.ds(top, slots)
            dqkv[1, every, lanes] = dk[...].astype(jnp.bfloat16)
            dqkv[2, every, lanes] = dv[...].astype(jnp.bfloat16)

        loop(items, attend)
        sums[l] = held[l, steps]
        for m, row in ((0, 0), (2, 1)):

            def add(t, carry):
                return carry + fold(dqkv[m, tile(t, ROW_TILE), :].astype(jnp.float32))

            late[2 * l + row] = lax.fori_loop(
                0, count // ROW_TILE, add, jnp.zeros((8, width), jnp.float32)
            )

        @pl.when(l == 0)
        def _():
            late_held[0] = jnp.sum(late[...], axis=1)
            last_sums.step(0)

        for m in range(3):
            slot = weights(base + 9 + m)
            for c, n in enumerate(chunks):
                g[:, n] += product(dqkv.at[m], slot, n)
                if m == 2:

                    @pl.when(l == 0)
                    def _():
                        pltpu.make_async_copy(g.at[:, n], grad.at[:, n], gsem.at[c]).start()

            if m + 1 < steps:

                @pl.when(l == 0)
                def _():
                    last_sums.step(m + 1)

    late[...] = jnp.zeros_like(late)
    loop(LAYERS, layer)
    for k in range(min(steps, 3), steps + 1):
        if k > 0:
            last_sums.step(k)
    late_sums[...] = late_held[steps]
    for c, n in enumerate(chunks):
        pltpu.make_async_copy(g.at[:, n], grad.at[:, n], gsem.at[c]).wait()


def backward(devices, wbuf, gain_attn, gain_ffn, first_sums, saved, rows, slots):
    count, width = saved[0].shape
    bf, f32 = jnp.bfloat16, jnp.float32
    blocks = slots // BLOCK
    places = digits(devices)
    steps = max(len(places), 1)
    any_ = pl.BlockSpec(memory_space=HBM)
    vm = pl.BlockSpec(memory_space=VMEM)
    return pl.pallas_call(
        functools.partial(backward_kernel, (rows, slots), places),
        out_shape=(
            jax.ShapeDtypeStruct((count, width), f32),
            jax.ShapeDtypeStruct((LAYERS, EARLY, width), f32),
            jax.ShapeDtypeStruct((8, width), f32),
        ),
        in_specs=[any_, vm, vm, vm] + [any_] * 6,
        out_specs=(any_, vm, vm),
        scratch_shapes=[
            VMEM((count, width), f32),
            VMEM((count, width), bf),
            VMEM((count, width), bf),
            VMEM((3, count, width), bf),
            VMEM((3, count, width), bf),
            VMEM((2, count, width), f32),
            VMEM((2, count, 128), f32),
            VMEM((2, 2, count, WIDTH), bf),
            VMEM((3, 2, width, WIDTH), bf),
            VMEM((3, blocks, WINDOW, 2 * BLOCK), bf),
            VMEM((slots, 128), f32),
            VMEM((slots, 128), f32),
            VMEM((EARLY, 8, width), f32),
            VMEM((8, 8, width), f32),
            VMEM((LAYERS, steps + 1, EARLY, width), f32),
            VMEM((LAYERS, steps, 4, EARLY, width), f32),
            VMEM((steps + 1, 8, width), f32),
            VMEM((steps, 4, 8, width), f32),
            DMA((3, 2)), DMA((3,)), DMA((2,)), DMA((2,)), DMA((2,)), DMA((3,)), DMA((2,)), DMA((4,)),
            DMA((LAYERS, steps, 4)), DMA((LAYERS, steps, 4)), DMA((steps, 4)), DMA((steps, 4)),
        ],
        compiler_params=pltpu.CompilerParams(
            vmem_limit_bytes=60 << 20,
            **({"collective_id": 1, "has_side_effects": True} if places else {}),
        ),
    )(wbuf, gain_attn, gain_ffn, first_sums, *saved)


def finish_kernel(
    unit,
    sums, late, grad_in, result_in,
    grad, result, query, value, out, inner, outer, attn, ffn,
    grad_hold, result_hold, load_sem, store_sem,
):
    count, width = grad.shape
    part = count // 4
    moves = []
    for c in range(4):
        for n, (source, hold, target) in enumerate(
            ((result_in, result_hold, result), (grad_in, grad_hold, grad))
        ):
            rows_ = pl.ds(c * part, part)
            load = pltpu.make_async_copy(source.at[rows_], hold.at[rows_], load_sem.at[n, c])
            store = pltpu.make_async_copy(hold.at[rows_], target.at[rows_], store_sem.at[n, c])
            load.start()
            moves.append((load, store))
    for load, store in moves:
        load.wait()
        store.start()
    devices = width // unit
    for l in range(LAYERS):
        here = slice(l, l + 1)
        for row, ref in ((D_OUT, out), (D_OUTER, outer), (D_ATTN, attn), (D_FFN, ffn)):
            ref[here, :] = sums[l, row : row + 1, :]
        query[here, :] = late[2 * l : 2 * l + 1, :]
        value[here, :] = late[2 * l + 1 : 2 * l + 2, :]
        for b in range(inner.shape[1] // 128):
            block = None
            for piece in range(128 // unit):
                device, quarter = divmod(b * (128 // unit) + piece, inner.shape[1] // width)
                source = device * unit
                row = D_INNER + quarter
                first = source // 128 * 128
                x = sums[l, row : row + 1, first : first + 128]
                shift = (piece * unit - source) % 128
                if shift:
                    x = pltpu.roll(x, shift, axis=1)
                if block is None:
                    block = x
                else:
                    lane = lax.broadcasted_iota(jnp.int32, x.shape, 1)
                    block = jnp.where(lane >= piece * unit, x, block)
            inner[here, b * 128 : (b + 1) * 128] = block
    for _, store in moves:
        store.wait()


def finish(unit, hidden, sums, late, grad, result):
    width = sums.shape[2]
    vm = pl.BlockSpec(memory_space=VMEM)
    any_ = pl.BlockSpec(memory_space=HBM)
    sizes = (width, width, width, hidden, width, width, width)
    large = tuple(jax.ShapeDtypeStruct(x.shape, x.dtype) for x in (grad, result))
    return pl.pallas_call(
        functools.partial(finish_kernel, unit),
        out_shape=large + tuple(jax.ShapeDtypeStruct((LAYERS, n), jnp.float32) for n in sizes),
        in_specs=[vm, vm, any_, any_],
        out_specs=(any_, any_) + (vm,) * 7,
        scratch_shapes=[
            VMEM(grad.shape, grad.dtype),
            VMEM(result.shape, result.dtype),
            DMA((2, 4)),
            DMA((2, 4)),
        ],
    )(sums, late, grad, result)


def per_device(
    devices,
    tokens,
    lengths,
    w_query,
    w_key,
    w_value,
    w_out,
    w_inner,
    w_outer,
    bias_query,
    bias_value,
    bias_out,
    bias_inner,
    bias_outer,
    shift_attn,
    shift_ffn,
    gain_attn,
    gain_ffn,
    cotangent,
):
    rows, slots, width = tokens.shape
    hidden = bias_inner.shape[1]
    unit = w_query.shape[1]
    count = rows * slots
    vectors = (
        bias_query, bias_value, bias_out, bias_outer, shift_attn, shift_ffn, gain_attn, gain_ffn,
    )
    matrices = (w_query, w_key, w_value, w_out, w_inner, w_outer)
    wbuf, out, first_sums, *saved = forward(
        devices, lengths, matrices, tokens.reshape(count, width), cotangent.reshape(count, width),
        vectors, bias_inner, rows, slots,
    )
    wbuf = wbuf.reshape(LAYERS * GROUPS, width, WIDTH)
    grad, sums, late = backward(
        devices, wbuf, gain_attn, gain_ffn, first_sums, saved, rows, slots
    )
    grad, out, *small = finish(unit, hidden, sums, late, grad, out)
    return (out.reshape(rows, slots, width), grad.reshape(rows, slots, width), *small)


def solution(mesh):
    rows, whole = P("dp", None, None), P()
    weight = P(None, "dp", None)
    placed = (rows, P("dp", None)) + (weight,) * 6 + (whole,) * 9 + (rows,)
    return jax.shard_map(
        functools.partial(per_device, mesh.shape["dp"]),
        mesh=mesh,
        in_specs=placed,
        out_specs=(rows, rows) + (whole,) * 7,
        check_vma=False,
    )
```

```python
import functools

import jax
import jax.numpy as jnp
from jax import lax
from jax.experimental import pallas as pl
from jax.experimental.pallas import tpu as pltpu
from jax.sharding import PartitionSpec as P

HEADS = 16
LAYERS = 2
EPSILON = 1e-12
NEGATIVE = -1e9
PADDING_ID = 1000
MESH = pl.DeviceIdType.MESH
HBM = pltpu.MemorySpace.HBM
VMEM = pltpu.VMEM
DMA = pltpu.SemaphoreType.DMA

WIDTH = 512
GROUPS = 24
AT_OUT, AT_INNER, AT_OUTER = 6, 8, 16
BLOCK = 128
WINDOW = 256
ROW_TILE = 128
ROOT_HALF = 0.7071067811865476
DENSITY = 0.3989422804014327
B_Q, B_V, B_OUT, B_OUTER, S_ATTN, S_FFN, G_ATTN, G_FFN = range(8)
D_OUT, D_OUTER, D_ATTN, D_FFN, D_INNER = range(5)
EARLY = 8


def chip_dims(devices):
    bits = (devices // 2).bit_length() - 1
    first = -(-bits // 3)
    second = -(-(bits - first) // 2)
    return (1 << first, 1 << second, 1 << (bits - first - second))


RELAY = 4
ORDERS = ((0, 4, 2, 1, 3), (0, 4, 1, 2, 3), (1, 0, 4, 2, 3), (2, 0, 4, 1, 3))
STARTS = (0, 2, 4, 6, 8, 9)
DEPTH = STARTS[-1]
SLOTS = 4


class Gather:
    def __init__(self, dims, own, buf, ssem, rsem, total):
        self.dims, self.own, self.buf = dims, own, buf
        self.ssem, self.rsem, self.total = ssem, rsem, total
        self.me = lax.axis_index("dp")
        _, n1, n2 = dims
        self.core = lax.rem(self.me, 2)
        chip = self.me // 2
        self.at = (chip // (n1 * n2), lax.rem(chip // n2, n1), lax.rem(chip, n2))
        self.step = (n1 * n2 * 2, n2 * 2, 2)
        self.relay = dims[0] == 4
        self.orders = ORDERS
        if not self.relay:
            self.orders = tuple(tuple(d for d in order if d != RELAY) for order in ORDERS)
        self.phases = len(self.orders[0])
        rows, cols = own.shape[-2:]
        q, c = rows // 4, cols // 4
        if rows % 32 == 0:
            self.parts = (
                ((pl.ds(0, q), pl.ds(0, 3 * c)),),
                ((pl.ds(q, q), pl.ds(0, 3 * c)),),
                ((pl.ds(2 * q, q), pl.ds(0, cols)), (pl.ds(0, q), pl.ds(3 * c, c))),
                ((pl.ds(3 * q, q), pl.ds(0, cols)), (pl.ds(q, q), pl.ds(3 * c, c))),
            )
        else:
            self.parts = tuple(((pl.ds(0, rows), pl.ds(n * c, c)),) for n in range(4))

    def peers(self, dim):
        if dim == 3:
            return [self.me + 1 - 2 * self.core]
        out = []
        for d in range(1, self.dims[dim]):
            to = lax.rem(self.at[dim] + d, self.dims[dim])
            out.append(self.me + (to - self.at[dim]) * self.step[dim])
        return out

    def moves(self, g, s, p):
        order = self.orders[s]
        dim, full = order[p], order[:p]
        n0, n1, n2 = self.dims
        first = (0, n0, n0 + n1 - 1, n0 + n1 + n2 - 2, n0 - 1)[dim]
        where = [pl.ds(0, self.dims[d]) if d in full else self.at[d] for d in range(3)]
        slot = lax.rem(g, SLOTS)
        z = self.at[0]
        if dim == RELAY:
            middle = (z == 1) | (z == 2)
            where[0] = jnp.where(z < 2, 3, 0)
            targets = [self.me + (3 - where[0] - z) * self.step[0]]
            guards = [(middle, jnp.logical_not(middle))]
        else:
            targets = self.peers(dim)
            guards = [(None, None)] * len(targets)
            if dim == 0 and self.relay:
                guards = [
                    (jnp.abs(lax.rem(z + d, 4) - z) != 3, jnp.abs(lax.rem(z + 4 - d, 4) - z) != 3)
                    if d != 2
                    else (None, None)
                    for d in (1, 2, 3)
                ]
        out = []
        for n, sub in enumerate(self.parts[s], sum(len(part) for part in self.parts[:s])):
            dst = self.buf.at[(g,) + tuple(where) + (self.core,) + sub]
            src = self.own.at[(g,) + sub] if p == 0 else dst
            for i, (to, guard) in enumerate(zip(targets, guards)):
                copy = pltpu.make_async_remote_copy(
                    src_ref=src,
                    dst_ref=dst,
                    send_sem=self.ssem.at[slot, n, first + i],
                    recv_sem=self.rsem.at[slot, n, first + i],
                    device_id=(to,),
                    device_id_type=MESH,
                )
                out.append((copy, *guard))
        return out

    def greet(self):
        bar = pltpu.get_barrier_semaphore()
        for d in range(4):
            for to in self.peers(d):
                pl.semaphore_signal(bar, inc=1, device_id=(to,), device_id_type=MESH)

    def meet(self):
        pl.semaphore_wait(pltpu.get_barrier_semaphore(), sum(self.dims) - 3 + 1)

    def pump(self, step):
        for p in range(self.phases, -1, -1):
            g = step - (DEPTH if p == self.phases else STARTS[p])

            @pl.when((g >= 0) & (g < self.total))
            def _():
                for s in range(len(self.orders)):
                    if p > 0:
                        for copy, sends, receives in self.moves(g, s, p - 1):
                            if sends is None:
                                copy.wait()
                            else:
                                pl.when(sends)(copy.wait_send)
                                pl.when(receives)(copy.wait_recv)
                    if p < self.phases:
                        for copy, sends, _ in self.moves(g, s, p):
                            if sends is None:
                                copy.start()
                            else:
                                pl.when(sends)(copy.start)


def matmul(left, right):
    return jnp.dot(left, right, preferred_element_type=jnp.float32)


def matmul_nt(left, right):
    return lax.dot_general(
        left, right, (((1,), (1,)), ((), ())), preferred_element_type=jnp.float32
    )


def matmul_tn(left, right):
    return lax.dot_general(
        left, right, (((0,), (0,)), ((), ())), preferred_element_type=jnp.float32
    )


def loop(count, body):
    lax.fori_loop(0, count, lambda i, c: (body(i), c)[1], 0)


def tile(i, size):
    return pl.ds(pl.multiple_of(i * size, size), size)


def window_starts(slots):
    return [
        min(max(b * BLOCK - (WINDOW - BLOCK) // 2, 0), slots - WINDOW)
        for b in range(slots // BLOCK)
    ]


def pair_stack(rows):
    lane = lax.broadcasted_iota(jnp.int32, rows.shape, 1)
    zero = jnp.zeros_like(rows)
    half = rows.shape[1] // 2
    return jnp.concatenate(
        [jnp.where(lane < half, rows, zero), jnp.where(lane < half, zero, rows)], axis=0
    )


def pair_join(stacked):
    rows = stacked.shape[0] // 2
    lane = lax.broadcasted_iota(jnp.int32, (rows, stacked.shape[1]), 1)
    return jnp.where(lane < stacked.shape[1] // 2, stacked[:rows], stacked[rows:])


def permute_hidden(load, store, unit, hidden):
    devices = hidden // (4 * unit)
    for b in range(hidden // 128):
        block = None
        for piece in range(128 // unit):
            quarter, device = divmod(b * (128 // unit) + piece, devices)
            source = (4 * device + quarter) * unit
            x = load(source // 128)
            shift = (piece * unit - source) % 128
            if shift:
                x = pltpu.roll(x, shift, axis=1)
            if block is None:
                block = x
            else:
                lane = lax.broadcasted_iota(jnp.int32, x.shape, 1)
                block = jnp.where(lane >= piece * unit, x, block)
        store(b, block)


def store_block(own, first, b, x):
    per = WIDTH // 128
    own[first + b // per, :, b % per * 128 : (b % per + 1) * 128] = x.astype(own.dtype)


def slot_ids(lengths, r, position):
    segments = lengths.shape[1]
    number = jnp.zeros_like(position)
    end = jnp.int32(0)
    for j in range(segments):
        end = end + lengths[r, j]
        number = number + (position >= end).astype(jnp.int32)
    return jnp.where(number < segments - 1, number, PADDING_ID + position)


def fold(x):
    rows, width = x.shape
    return jnp.sum(x.reshape(rows // 8, 8, width), axis=0)


def norm_back(up, xhat, scale, gain_row):
    scaled = up * gain_row
    m1 = jnp.mean(scaled, axis=1, keepdims=True)
    m2 = jnp.mean(scaled * xhat, axis=1, keepdims=True)
    return scale * (scaled - m1 - xhat * m2)


def forward_kernel(
    dims, devices_dims,
    lengths, *rest,
):
    matrices, rest = rest[:6], rest[6:]
    (tokens, cotangent), rest = rest[:2], rest[2:]
    vectors, rest = rest[:8], rest[8:]
    (
        inner_raw, wbuf, out, first_sums, saved_f, saved_qkv, saved_p, saved_x, saved_s, saved_d,
        h, a, qkv, o, z, u, w, p_stage, d_stage, x_stage, s_stage, own, id_row, id_col, inner_bias, cot,
        w_query, w_key, w_value, w_out, w_inner, w_outer, msem,
        wsem, psem, dsem, xsem, ssem, qsem, tsem, hsem, csem, send_sem, recv_sem,
    ) = rest
    rows, slots = dims
    count = h.shape[0]
    pairs = HEADS // 2
    total = LAYERS * GROUPS
    gather = Gather(devices_dims, own, wbuf, send_sem, recv_sem, total)

    def wload(g):
        slot = lax.rem(g, 2)
        return pltpu.make_async_copy(wbuf.at[g], w.at[slot], wsem.at[slot])

    def weights(g):
        @pl.when(g + 1 < total)
        def _():
            wload(g + 1).start()

        wload(g).wait()
        return w[lax.rem(g, 2)].reshape(h.shape[1], WIDTH)

    def pump(half):
        gather.pump(half + DEPTH)

    gather.greet()
    fetches = [
        pltpu.make_async_copy(source, target, msem.at[n])
        for n, (source, target) in enumerate(
            zip(matrices, (w_query, w_key, w_value, w_out, w_inner, w_outer))
        )
    ]
    for fetch in fetches:
        fetch.start()
    load = pltpu.make_async_copy(tokens, a, tsem)
    load.start()
    load_cot = pltpu.make_async_copy(cotangent, cot, csem)
    load_cot.start()
    unit = own.shape[1]

    def cast(l, m):
        matrix = (w_query, w_key, w_value, w_out)[m]
        for c in range(2):
            own[l * GROUPS + 2 * m + c] = matrix[l, :, tile(c, WIDTH)].astype(jnp.bfloat16)

    def here(first, count):
        blocks = pl.ds(first, count)
        return pltpu.make_async_copy(
            own.at[blocks], wbuf.at[(blocks,) + gather.at + (gather.core,)], hsem
        )

    def start(i):
        gather.pump(i)

    for m in range(4):
        fetches[m].wait()
        cast(0, m)
    here(0, AT_INNER).start()
    gather.meet()
    start(0)
    here(0, AT_INNER).wait()
    start(1)
    fetches[4].wait()
    fetches[5].wait()
    for l in range(LAYERS):
        at = l * GROUPS
        for m in range(4):
            if l > 0:
                cast(l, m)
        for c in range(2):
            for kc in range(4):
                piece = w_outer[l, kc * unit : (kc + 1) * unit, c * WIDTH : (c + 1) * WIDTH]
                own[at + AT_OUTER + 4 * c + kc] = piece.astype(jnp.bfloat16)
        permute_hidden(
            lambda b: w_inner[l, :, b * 128 : (b + 1) * 128],
            lambda b, x: store_block(own, at + AT_INNER, b, x),
            unit,
            w_inner.shape[2],
        )
        if l == 0:
            start(2)
    here(AT_INNER, total - AT_INNER).start()
    start(3)
    here(AT_INNER, total - AT_INNER).wait()

    def keep_bias(b, x):
        inner_bias[:, b * 128 : (b + 1) * 128] = x

    permute_hidden(
        lambda b: inner_raw[:, b * 128 : (b + 1) * 128], keep_bias, unit, w_inner.shape[2]
    )
    for r in range(rows):
        id_row[r] = slot_ids(lengths, r, lax.broadcasted_iota(jnp.int32, (8, slots), 1))
        id_col[r] = slot_ids(lengths, r, lax.broadcasted_iota(jnp.int32, (slots, 128), 0))
    first_sums[...] = jnp.zeros_like(first_sums)
    load_cot.wait()
    load.wait()

    def widen(i):
        h[tile(i, ROW_TILE), :] = a[tile(i, ROW_TILE), :].astype(jnp.float32)

    loop(count // ROW_TILE, widen)

    for i in range(4, DEPTH):
        start(i)
    pump(0)
    wload(0).start()

    def normalize(l, which):
        bias, gain, shift = ((B_OUT, G_ATTN, S_ATTN), (B_OUTER, G_FFN, S_FFN))[which]
        store_x = pltpu.make_async_copy(x_stage, saved_x.at[l, which], xsem)
        store_s = pltpu.make_async_copy(s_stage, saved_s.at[l, which], ssem)
        if which == 1:
            store_x.wait()
            store_s.wait()
        else:

            @pl.when(l > 0)
            def _():
                store_x.wait()
                store_s.wait()

        def body(i):
            t = tile(i, ROW_TILE)
            r = h[t, :] + vectors[bias][pl.ds(l, 1), :]
            centered = r - jnp.mean(r, axis=1, keepdims=True)
            var = jnp.mean(centered * centered, axis=1, keepdims=True)
            scale = lax.rsqrt(var + EPSILON)
            xhat = centered * scale
            x_stage[t, :] = xhat
            s_stage[t, :] = jnp.broadcast_to(scale, (ROW_TILE, 128))
            y = xhat * vectors[gain][pl.ds(l, 1), :] + vectors[shift][pl.ds(l, 1), :]
            h[t, :] = y
            a[t, :] = y.astype(jnp.bfloat16)
            if which == 1:

                @pl.when(l == LAYERS - 1)
                def _():
                    r = i // (slots // ROW_TILE)
                    real = slots - lengths[r, lengths.shape[1] - 1]
                    slot = lax.rem(i * ROW_TILE, slots) + lax.broadcasted_iota(
                        jnp.int32, (ROW_TILE, h.shape[1]), 0
                    )
                    up = jnp.where(slot < real, cot[t, :].astype(jnp.float32), 0.0)
                    down = norm_back(up, xhat, scale, vectors[gain][pl.ds(l, 1), :])
                    x_stage[t, :] = down
                    low = down.astype(jnp.bfloat16)
                    cot[t, :] = low
                    first_sums[0] += fold(up)
                    first_sums[1] += fold(low.astype(jnp.float32))

        loop(count // ROW_TILE, body)
        store_x.start()
        store_s.start()

    def layer(l):
        base = l * GROUPS

        @pl.when(l > 0)
        def _():
            for m in range(3):
                pltpu.make_async_copy(qkv.at[m], saved_qkv.at[l, m], qsem.at[m]).wait()

        def project(i):
            pump(base + i + 1)
            m = i // 2
            cols = tile(i % 2, WIDTH)
            bias_q = vectors[B_Q][pl.ds(l, 1), cols]
            bias_v = vectors[B_V][pl.ds(l, 1), cols]
            bias = jnp.where(m == 0, bias_q, jnp.where(m == 1, jnp.zeros_like(bias_v), bias_v))
            y = matmul(a[...], weights(base + i)) + bias
            y = y * jnp.where(m == 0, jnp.float32((h.shape[1] // HEADS) ** -0.5), jnp.float32(1))
            qkv[m, :, cols] = y.astype(jnp.bfloat16)

        loop(6, project)
        for m in range(3):
            pltpu.make_async_copy(qkv.at[m], saved_qkv.at[l, m], qsem.at[m]).start()

        def attend(i):
            @pl.when(lax.rem(i, 4) == 2)
            def _():
                pump(base + 7 + i // 4)


            r = i // pairs
            lanes = tile(lax.rem(i, pairs), 128)
            slot = lax.rem(i, 2)
            store_p = pltpu.make_async_copy(p_stage.at[slot], saved_p.at[l, i], psem.at[slot])

            @pl.when((i >= 2) | (l > 0))
            def _():
                store_p.wait()

            top = pl.multiple_of(r * slots, slots)
            starts = window_starts(slots)
            scores = [
                matmul_nt(
                    qkv[1, pl.ds(top + start, WINDOW), lanes],
                    pair_stack(qkv[0, pl.ds(top + b * BLOCK, BLOCK), lanes]),
                )
                for b, start in enumerate(starts)
            ]
            for b, start in enumerate(starts):
                vm = qkv[2, pl.ds(top + start, WINDOW), lanes]
                same = id_col[r, start : start + WINDOW, :] == id_row[r, :1, b * BLOCK : (b + 1) * BLOCK]
                s = jnp.where(jnp.concatenate([same, same], axis=1), scores[b], NEGATIVE)
                e = jnp.exp(s - jnp.max(s, axis=0, keepdims=True))
                p = e * (1.0 / jnp.sum(e, axis=0, keepdims=True))
                p = p.astype(jnp.bfloat16)
                p_stage[slot, b] = p
                o[pl.ds(top + b * BLOCK, BLOCK), lanes] = pair_join(matmul_tn(p, vm)).astype(jnp.bfloat16)
            store_p.start()

        loop(rows * pairs, attend)

        def attn_out(i):
            @pl.when(i == 1)
            def _():
                pump(base + 11)

            cols = tile(i, WIDTH)
            h[:, cols] += matmul(o[...], weights(base + AT_OUT + i))

        loop(2, attn_out)
        normalize(l, 0)

        def inner(i):
            pump(base + 12 + i)


            cols = tile(i, WIDTH)
            u[...] = matmul(a[...], weights(base + AT_INNER + i)) + inner_bias[pl.ds(l, 1), cols]
            slot = lax.rem(i, 2)
            store_d = pltpu.make_async_copy(d_stage.at[slot], saved_d.at[l, i], dsem.at[slot])

            @pl.when((i >= 2) | (l > 0))
            def _():
                store_d.wait()

            def activate(t):
                part = tile(t, ROW_TILE)
                x = u[part, :]
                cdf = 0.5 + 0.5 * lax.erf(x * ROOT_HALF)
                z[i // 2, part, tile(i % 2, WIDTH)] = (x * cdf).astype(jnp.bfloat16)
                slope = cdf + x * (DENSITY * jnp.exp(-0.5 * x * x))
                d_stage[slot, part, :] = slope.astype(jnp.bfloat16)

            loop(count // ROW_TILE, activate)
            store_d.start()

        loop(8, inner)

        def outer(i):
            @pl.when(i == 0)
            def _():
                pump(base + 20)

            @pl.when(i == 1)
            def _():
                pump(base + 21)

            @pl.when(i == 3)
            def _():
                pump(base + 22)

            @pl.when(i == 5)
            def _():
                pump(base + 23)

            @pl.when(i == 7)
            def _():
                pump(base + 24)


            cols = tile(i // 4, WIDTH)
            h[:, cols] += matmul(z[lax.rem(i, 4)], weights(base + AT_OUTER + i))

        loop(8, outer)
        normalize(l, 1)

    loop(LAYERS, layer)
    store = pltpu.make_async_copy(a, out, tsem)
    store.start()
    store_f = pltpu.make_async_copy(cot, saved_f, csem)
    store_f.start()
    last = LAYERS - 1
    for m in range(3):
        pltpu.make_async_copy(qkv.at[m], saved_qkv.at[last, m], qsem.at[m]).wait()
    for i in range(2):
        pltpu.make_async_copy(p_stage.at[i], saved_p.at[last, i], psem.at[i]).wait()
        pltpu.make_async_copy(d_stage.at[i], saved_d.at[last, i], dsem.at[i]).wait()
    pltpu.make_async_copy(x_stage, saved_x.at[last, 1], xsem).wait()
    pltpu.make_async_copy(s_stage, saved_s.at[last, 1], ssem).wait()
    store.wait()
    store_f.wait()


def forward(devices, lengths, matrices, tokens, cotangent, vectors, inner_bias, rows, slots):
    count, width = tokens.shape
    hidden = inner_bias.shape[-1]
    unit = matrices[0].shape[1]
    bf, f32 = jnp.bfloat16, jnp.float32
    blocks = slots // BLOCK
    devices_dims = chip_dims(devices)
    held = devices_dims + (2, unit, WIDTH)
    sems = sum(devices_dims) - 1
    any_ = pl.BlockSpec(memory_space=HBM)
    vm = pl.BlockSpec(memory_space=VMEM)
    return pl.pallas_call(
        functools.partial(forward_kernel, (rows, slots), devices_dims),
        out_shape=(
            jax.ShapeDtypeStruct((LAYERS * GROUPS,) + held, bf),
            jax.ShapeDtypeStruct((count, width), bf),
            jax.ShapeDtypeStruct((2, 8, width), f32),
            jax.ShapeDtypeStruct((count, width), bf),
            jax.ShapeDtypeStruct((LAYERS, 3, count, width), bf),
            jax.ShapeDtypeStruct((LAYERS, rows * HEADS // 2, blocks, WINDOW, 2 * BLOCK), bf),
            jax.ShapeDtypeStruct((LAYERS, 2, count, width), f32),
            jax.ShapeDtypeStruct((LAYERS, 2, count, 128), f32),
            jax.ShapeDtypeStruct((LAYERS, hidden // WIDTH, count, WIDTH), bf),
        ),
        in_specs=[pl.BlockSpec(memory_space=pltpu.SMEM)] + [any_] * 8 + [vm] * 9,
        out_specs=(any_, any_, vm) + (any_,) * 6,
        scratch_shapes=[
            VMEM((count, width), f32),
            VMEM((count, width), bf),
            VMEM((3, count, width), bf),
            VMEM((count, width), bf),
            VMEM((hidden // width, count, width), bf),
            VMEM((count, WIDTH), f32),
            VMEM((2,) + held, bf),
            VMEM((2, blocks, WINDOW, 2 * BLOCK), bf),
            VMEM((2, count, WIDTH), bf),
            VMEM((count, width), f32),
            VMEM((count, 128), f32),
            VMEM((LAYERS * GROUPS, unit, WIDTH), bf),
            VMEM((rows, 8, slots), jnp.int32),
            VMEM((rows, slots, 128), jnp.int32),
            VMEM((LAYERS, hidden), f32),
            VMEM((count, width), bf),
            *(VMEM(m.shape, f32) for m in matrices),
            DMA((6,)),
            DMA((2,)), DMA((2,)), DMA((2,)), DMA, DMA, DMA((3,)), DMA, DMA, DMA,
            DMA((SLOTS, 6, sems)), DMA((SLOTS, 6, sems)),
        ],
        compiler_params=pltpu.CompilerParams(
            vmem_limit_bytes=58 << 20, collective_id=0, has_side_effects=True
        ),
    )(lengths, *matrices, tokens, cotangent, *vectors, inner_bias)


def digits(devices):
    out, stride = [], 1
    while stride < devices:
        size = 2 if stride == 1 else min(4, devices // stride)
        out.append((stride, size))
        stride *= size
    return out


class Exchange:
    def __init__(self, me, places, held, got, ssem, rsem):
        self.me, self.places = me, places
        self.held, self.got, self.ssem, self.rsem = held, got, ssem, rsem

    def copies(self, k):
        stride, size = self.places[k]
        digit = lax.rem(self.me // stride, size)
        out = []
        for d in range(1, size):
            to = self.me + (lax.rem(digit + d, size) - digit) * stride
            out.append(
                pltpu.make_async_remote_copy(
                    src_ref=self.held.at[k],
                    dst_ref=self.got.at[k, digit],
                    send_sem=self.ssem.at[k, d],
                    recv_sem=self.rsem.at[k, d],
                    device_id=(to,),
                    device_id_type=MESH,
                )
            )
        return out, digit, size

    def step(self, k):
        if k > 0:
            copies, digit, size = self.copies(k - 1)
            for c in copies:
                c.wait()
            self.got[k - 1, digit] = self.held[k - 1]
            total = self.got[k - 1, 0]
            for j in range(1, size):
                total = total + self.got[k - 1, j]
            self.held[k] = total
        if k < len(self.places):
            for c in self.copies(k)[0]:
                c.start()


def backward_kernel(
    dims, places,
    wbuf, gain_attn, gain_ffn, first_sums, saved_f, saved_qkv, saved_p, saved_x, saved_s, saved_d,
    grad, sums, late_sums,
    g, db, du, qkv, dqkv, x, sc, d, w, p, dk, dv, part, late,
    held, got, late_held, late_got,
    wsem, psem, dsem, xsem, ssem, qsem, csem, gsem, send_sem, recv_sem, late_send, late_recv,
):
    rows, slots = dims
    count, width = g.shape
    pairs = HEADS // 2
    per_layer = GROUPS // 2
    total = LAYERS * per_layer
    items = rows * pairs
    steps = len(places)
    chunk = 256
    chunks = [slice(c * chunk, (c + 1) * chunk) for c in range(width // chunk)]

    def wload(i):
        l = LAYERS - 1 - i // per_layer
        j = lax.rem(i, per_layer)
        outer = (j < 8) & (lax.rem(j, 2) == 0)
        ffn = jnp.where(outer, AT_OUTER + j // 2, AT_INNER + j // 2 * 2)
        block = l * GROUPS + jnp.where(j < 8, ffn, jnp.where(j == 8, AT_OUT, 2 * (j - 9)))
        slot = lax.rem(i, 3)
        apart = jnp.where(outer, 4, 1)
        return [
            pltpu.make_async_copy(wbuf.at[block + c * apart], w.at[slot, c], wsem.at[slot, c])
            for c in range(2)
        ]

    def weights(i):
        @pl.when(i + 2 < total)
        def _():
            for c in wload(i + 2):
                c.start()

        for c in wload(i):
            c.wait()
        return lax.rem(i, 3)

    def product(left, slot, n):
        return matmul_nt(left[:, :WIDTH], w[slot, 0, n, :]) + matmul_nt(left[:, WIDTH:], w[slot, 1, n, :])

    def xload(l, which):
        return (
            pltpu.make_async_copy(saved_x.at[l, which], x.at[which], xsem.at[which]),
            pltpu.make_async_copy(saved_s.at[l, which], sc.at[which], ssem.at[which]),
        )

    def dload(l, quarter):
        slot = lax.rem(quarter, 2)
        return pltpu.make_async_copy(saved_d.at[l, pl.ds(2 * quarter, 2)], d.at[slot], dsem.at[slot])

    def pload(l, i):
        slot = lax.rem(i, 3)
        return pltpu.make_async_copy(saved_p.at[l, i], p.at[slot], psem.at[slot])

    def qload(l):
        return [pltpu.make_async_copy(saved_qkv.at[l, m], qkv.at[m], qsem.at[m]) for m in range(3)]

    top_layer = LAYERS - 1
    opening = [
        pltpu.make_async_copy(saved_f, db, csem.at[0]),
        pltpu.make_async_copy(saved_x.at[top_layer, 1], g, csem.at[1]),
    ]
    opening[0].start()
    for c in wload(0):
        c.start()
    dload(top_layer, 0).start()
    for c in wload(1):
        c.start()
    opening[1].start()
    for c in xload(top_layer, 0):
        c.start()
    if top_layer:
        for c in xload(top_layer - 1, 1):
            c.start()
    me = lax.axis_index("dp")
    if steps:
        barrier = pltpu.get_barrier_semaphore()
        for stride, size in places:
            digit = lax.rem(me // stride, size)
            for k in range(1, size):
                to = me + (lax.rem(digit + k, size) - digit) * stride
                pl.semaphore_signal(barrier, inc=1, device_id=(to,), device_id_type=MESH)
    for c in opening:
        c.wait()
    part[D_FFN] = first_sums[0]
    part[D_OUTER] = first_sums[1]
    if steps:
        pl.semaphore_wait(barrier, sum(size - 1 for _, size in places))

    def normalize_back(l, which):
        gain = (gain_attn, gain_ffn)[which]
        row_shift = (D_ATTN, D_FFN)[which]
        row_bias = (D_OUT, D_OUTER)[which]
        for c in xload(l, which):
            c.wait()

        def body(i, carry):
            t = tile(i, ROW_TILE)
            up = g[t, :]
            xh = x[which, t, :]
            down = norm_back(up, xh, sc[which, t, :1], gain[pl.ds(l, 1), :])
            g[t, :] = down
            low = down.astype(jnp.bfloat16)
            db[t, :] = low
            return carry[0] + fold(up), carry[1] + fold(low.astype(jnp.float32))

        zero = jnp.zeros((8, width), jnp.float32)
        shift_sum, bias_sum = lax.fori_loop(0, count // ROW_TILE, body, (zero, zero))
        part[row_shift] = shift_sum
        part[row_bias] = bias_sum

        @pl.when(l > 0)
        def _():
            for c in xload(l - 1, which):
                c.start()

    last_sums = Exchange(me, places, late_held, late_got, late_send, late_recv)

    def layer(step):
        l = top_layer - step
        base = step * per_layer

        @pl.when(step > 0)
        def _():
            normalize_back(l, 1)

        def quarter(kc):
            @pl.when(kc + 1 < 4)
            def _():
                dload(l, kc + 1).start()

            @pl.when(kc == 1)
            def _():
                for c in qload(l):
                    c.start()

            slot = weights(base + 2 * kc)
            dload(l, kc).wait()
            for c, n in enumerate(chunks):
                within = slice(c * chunk % WIDTH, c * chunk % WIDTH + chunk)
                slope = d[lax.rem(kc, 2), c * chunk // WIDTH, :, within].astype(jnp.float32)
                low = (product(db, slot, n) * slope).astype(jnp.bfloat16)
                du[:, n] = low
                part[D_INNER + kc, :, n] = fold(low.astype(jnp.float32))
            slot = weights(base + 2 * kc + 1)
            for n in chunks:
                g[:, n] += product(du, slot, n)

        loop(4, quarter)

        @pl.when(l > 0)
        def _():
            dload(l - 1, 0).start()

        pload(l, 0).start()
        pload(l, 1).start()
        normalize_back(l, 0)
        slot = weights(base + 8)
        for n in chunks:
            du[:, n] = product(db, slot, n).astype(jnp.bfloat16)
        for c in qload(l):
            c.wait()
        early = Exchange(me, places, held.at[l], got.at[l], send_sem.at[l], recv_sem.at[l])
        held[l, 0] = jnp.sum(part[...], axis=1)
        early.step(0)

        def attend(i):
            for k in range(1, steps + 1):

                @pl.when(i == (items - 1) // steps * k)
                def _():
                    early.step(k)

            r = i // pairs
            lanes = tile(lax.rem(i, pairs), 128)
            slot = lax.rem(i, 3)

            @pl.when(i + 2 < items)
            def _():
                pload(l, i + 2).start()

            pload(l, i).wait()
            dk[...] = jnp.zeros_like(dk)
            dv[...] = jnp.zeros_like(dv)
            top = pl.multiple_of(r * slots, slots)
            starts = window_starts(slots)
            mine = [pl.ds(top + b * BLOCK, BLOCK) for b in range(len(starts))]
            reach = [pl.ds(top + start, WINDOW) for start in starts]
            stacked = [pair_stack(du[rows_, lanes]) for rows_ in mine]
            dps = [matmul_nt(qkv[2, keys, lanes], om) for keys, om in zip(reach, stacked)]
            for b, start in enumerate(starts):
                qm = pair_stack(qkv[0, mine[b], lanes])
                pb = p[slot, b]
                pf = pb.astype(jnp.float32)
                weighted = pf * dps[b]
                ds = weighted - pf * jnp.sum(weighted, axis=0, keepdims=True)
                ds = ds.astype(jnp.bfloat16)
                dk[start : start + WINDOW, :] += matmul(ds, qm)
                dv[start : start + WINDOW, :] += matmul(pb, stacked[b])
                dq = pair_join(matmul_tn(ds, qkv[1, reach[b], lanes]))
                dqkv[0, mine[b], lanes] = (dq * (width // HEADS) ** -0.5).astype(jnp.bfloat16)
            every = pl.ds(top, slots)
            dqkv[1, every, lanes] = dk[...].astype(jnp.bfloat16)
            dqkv[2, every, lanes] = dv[...].astype(jnp.bfloat16)

        loop(items, attend)
        sums[l] = held[l, steps]
        for m, row in ((0, 0), (2, 1)):

            def add(t, carry):
                return carry + fold(dqkv[m, tile(t, ROW_TILE), :].astype(jnp.float32))

            late[2 * l + row] = lax.fori_loop(
                0, count // ROW_TILE, add, jnp.zeros((8, width), jnp.float32)
            )

        @pl.when(l == 0)
        def _():
            late_held[0] = jnp.sum(late[...], axis=1)
            last_sums.step(0)

        for m in range(3):
            slot = weights(base + 9 + m)
            for c, n in enumerate(chunks):
                g[:, n] += product(dqkv.at[m], slot, n)
                if m == 2:

                    @pl.when(l == 0)
                    def _():
                        pltpu.make_async_copy(g.at[:, n], grad.at[:, n], gsem.at[c]).start()

            if m + 1 < steps:

                @pl.when(l == 0)
                def _():
                    last_sums.step(m + 1)

    late[...] = jnp.zeros_like(late)
    loop(LAYERS, layer)
    for k in range(min(steps, 3), steps + 1):
        if k > 0:
            last_sums.step(k)
    late_sums[...] = late_held[steps]
    for c, n in enumerate(chunks):
        pltpu.make_async_copy(g.at[:, n], grad.at[:, n], gsem.at[c]).wait()


def backward(devices, wbuf, gain_attn, gain_ffn, first_sums, saved, rows, slots):
    count, width = saved[0].shape
    bf, f32 = jnp.bfloat16, jnp.float32
    blocks = slots // BLOCK
    places = digits(devices)
    steps = max(len(places), 1)
    any_ = pl.BlockSpec(memory_space=HBM)
    vm = pl.BlockSpec(memory_space=VMEM)
    return pl.pallas_call(
        functools.partial(backward_kernel, (rows, slots), places),
        out_shape=(
            jax.ShapeDtypeStruct((count, width), f32),
            jax.ShapeDtypeStruct((LAYERS, EARLY, width), f32),
            jax.ShapeDtypeStruct((8, width), f32),
        ),
        in_specs=[any_, vm, vm, vm] + [any_] * 6,
        out_specs=(any_, vm, vm),
        scratch_shapes=[
            VMEM((count, width), f32),
            VMEM((count, width), bf),
            VMEM((count, width), bf),
            VMEM((3, count, width), bf),
            VMEM((3, count, width), bf),
            VMEM((2, count, width), f32),
            VMEM((2, count, 128), f32),
            VMEM((2, 2, count, WIDTH), bf),
            VMEM((3, 2, width, WIDTH), bf),
            VMEM((3, blocks, WINDOW, 2 * BLOCK), bf),
            VMEM((slots, 128), f32),
            VMEM((slots, 128), f32),
            VMEM((EARLY, 8, width), f32),
            VMEM((8, 8, width), f32),
            VMEM((LAYERS, steps + 1, EARLY, width), f32),
            VMEM((LAYERS, steps, 4, EARLY, width), f32),
            VMEM((steps + 1, 8, width), f32),
            VMEM((steps, 4, 8, width), f32),
            DMA((3, 2)), DMA((3,)), DMA((2,)), DMA((2,)), DMA((2,)), DMA((3,)), DMA((2,)), DMA((4,)),
            DMA((LAYERS, steps, 4)), DMA((LAYERS, steps, 4)), DMA((steps, 4)), DMA((steps, 4)),
        ],
        compiler_params=pltpu.CompilerParams(
            vmem_limit_bytes=60 << 20,
            **({"collective_id": 1, "has_side_effects": True} if places else {}),
        ),
    )(wbuf, gain_attn, gain_ffn, first_sums, *saved)


def finish_kernel(
    unit,
    sums, late, grad_in, result_in,
    grad, result, query, value, out, inner, outer, attn, ffn,
    grad_hold, result_hold, load_sem, store_sem,
):
    count, width = grad.shape
    part = count // 4
    moves = []
    for c in range(4):
        for n, (source, hold, target) in enumerate(
            ((result_in, result_hold, result), (grad_in, grad_hold, grad))
        ):
            rows_ = pl.ds(c * part, part)
            load = pltpu.make_async_copy(source.at[rows_], hold.at[rows_], load_sem.at[n, c])
            store = pltpu.make_async_copy(hold.at[rows_], target.at[rows_], store_sem.at[n, c])
            load.start()
            moves.append((load, store))
    for load, store in moves:
        load.wait()
        store.start()
    devices = width // unit
    for l in range(LAYERS):
        here = slice(l, l + 1)
        for row, ref in ((D_OUT, out), (D_OUTER, outer), (D_ATTN, attn), (D_FFN, ffn)):
            ref[here, :] = sums[l, row : row + 1, :]
        query[here, :] = late[2 * l : 2 * l + 1, :]
        value[here, :] = late[2 * l + 1 : 2 * l + 2, :]
        for b in range(inner.shape[1] // 128):
            block = None
            for piece in range(128 // unit):
                device, quarter = divmod(b * (128 // unit) + piece, inner.shape[1] // width)
                source = device * unit
                row = D_INNER + quarter
                first = source // 128 * 128
                x = sums[l, row : row + 1, first : first + 128]
                shift = (piece * unit - source) % 128
                if shift:
                    x = pltpu.roll(x, shift, axis=1)
                if block is None:
                    block = x
                else:
                    lane = lax.broadcasted_iota(jnp.int32, x.shape, 1)
                    block = jnp.where(lane >= piece * unit, x, block)
            inner[here, b * 128 : (b + 1) * 128] = block
    for _, store in moves:
        store.wait()


def finish(unit, hidden, sums, late, grad, result):
    width = sums.shape[2]
    vm = pl.BlockSpec(memory_space=VMEM)
    any_ = pl.BlockSpec(memory_space=HBM)
    sizes = (width, width, width, hidden, width, width, width)
    large = tuple(jax.ShapeDtypeStruct(x.shape, x.dtype) for x in (grad, result))
    return pl.pallas_call(
        functools.partial(finish_kernel, unit),
        out_shape=large + tuple(jax.ShapeDtypeStruct((LAYERS, n), jnp.float32) for n in sizes),
        in_specs=[vm, vm, any_, any_],
        out_specs=(any_, any_) + (vm,) * 7,
        scratch_shapes=[
            VMEM(grad.shape, grad.dtype),
            VMEM(result.shape, result.dtype),
            DMA((2, 4)),
            DMA((2, 4)),
        ],
    )(sums, late, grad, result)


def per_device(
    devices,
    tokens,
    lengths,
    w_query,
    w_key,
    w_value,
    w_out,
    w_inner,
    w_outer,
    bias_query,
    bias_value,
    bias_out,
    bias_inner,
    bias_outer,
    shift_attn,
    shift_ffn,
    gain_attn,
    gain_ffn,
    cotangent,
):
    rows, slots, width = tokens.shape
    hidden = bias_inner.shape[1]
    unit = w_query.shape[1]
    count = rows * slots
    vectors = (
        bias_query, bias_value, bias_out, bias_outer, shift_attn, shift_ffn, gain_attn, gain_ffn,
    )
    matrices = (w_query, w_key, w_value, w_out, w_inner, w_outer)
    wbuf, out, first_sums, *saved = forward(
        devices, lengths, matrices, tokens.reshape(count, width), cotangent.reshape(count, width),
        vectors, bias_inner, rows, slots,
    )
    wbuf = wbuf.reshape(LAYERS * GROUPS, width, WIDTH)
    grad, sums, late = backward(
        devices, wbuf, gain_attn, gain_ffn, first_sums, saved, rows, slots
    )
    grad, out, *small = finish(unit, hidden, sums, late, grad, out)
    return (out.reshape(rows, slots, width), grad.reshape(rows, slots, width), *small)


def solution(mesh):
    rows, whole = P("dp", None, None), P()
    weight = P(None, "dp", None)
    placed = (rows, P("dp", None)) + (weight,) * 6 + (whole,) * 9 + (rows,)
    return jax.shard_map(
        functools.partial(per_device, mesh.shape["dp"]),
        mesh=mesh,
        in_specs=placed,
        out_specs=(rows, rows) + (whole,) * 7,
        check_vma=False,
    )
```

```python
import functools

import jax
import jax.numpy as jnp
from jax import lax
from jax.experimental import pallas as pl
from jax.experimental.pallas import tpu as pltpu
from jax.sharding import PartitionSpec as P

HEADS = 16
LAYERS = 2
EPSILON = 1e-12
NEGATIVE = -1e9
PADDING_ID = 1000
MESH = pl.DeviceIdType.MESH
HBM = pltpu.MemorySpace.HBM
VMEM = pltpu.VMEM
DMA = pltpu.SemaphoreType.DMA

WIDTH = 512
GROUPS = 24
AT_OUT, AT_INNER, AT_OUTER = 6, 8, 16
BLOCK = 128
WINDOW = 256
ROW_TILE = 128
ROOT_HALF = 0.7071067811865476
DENSITY = 0.3989422804014327
B_Q, B_V, B_OUT, B_OUTER, S_ATTN, S_FFN, G_ATTN, G_FFN = range(8)
D_OUT, D_OUTER, D_ATTN, D_FFN, D_INNER = range(5)
EARLY = 8


def chip_dims(devices):
    bits = (devices // 2).bit_length() - 1
    first = -(-bits // 3)
    second = -(-(bits - first) // 2)
    return (1 << first, 1 << second, 1 << (bits - first - second))


RELAY = 4
ORDERS = ((0, 4, 2, 1, 3), (0, 4, 1, 2, 3), (1, 0, 4, 2, 3), (2, 0, 4, 1, 3))
STARTS = (0, 2, 4, 6, 8, 9)
DEPTH = STARTS[-1]
SLOTS = 4


class Gather:
    def __init__(self, dims, own, buf, ssem, rsem, total):
        self.dims, self.own, self.buf = dims, own, buf
        self.ssem, self.rsem, self.total = ssem, rsem, total
        self.me = lax.axis_index("dp")
        _, n1, n2 = dims
        self.core = lax.rem(self.me, 2)
        chip = self.me // 2
        self.at = (chip // (n1 * n2), lax.rem(chip // n2, n1), lax.rem(chip, n2))
        self.step = (n1 * n2 * 2, n2 * 2, 2)
        self.relay = dims[0] == 4
        self.orders = ORDERS
        if not self.relay:
            self.orders = tuple(tuple(d for d in order if d != RELAY) for order in ORDERS)
        self.phases = len(self.orders[0])
        rows, cols = own.shape[-2:]
        q, c = rows // 4, cols // 4
        if rows % 32 == 0:
            self.parts = (
                ((pl.ds(0, q), pl.ds(0, 3 * c)),),
                ((pl.ds(q, q), pl.ds(0, 3 * c)),),
                ((pl.ds(2 * q, q), pl.ds(0, cols)), (pl.ds(0, q), pl.ds(3 * c, c))),
                ((pl.ds(3 * q, q), pl.ds(0, cols)), (pl.ds(q, q), pl.ds(3 * c, c))),
            )
        else:
            self.parts = tuple(((pl.ds(0, rows), pl.ds(n * c, c)),) for n in range(4))

    def peers(self, dim):
        if dim == 3:
            return [self.me + 1 - 2 * self.core]
        out = []
        for d in range(1, self.dims[dim]):
            to = lax.rem(self.at[dim] + d, self.dims[dim])
            out.append(self.me + (to - self.at[dim]) * self.step[dim])
        return out

    def moves(self, g, s, p):
        order = self.orders[s]
        dim, full = order[p], order[:p]
        n0, n1, n2 = self.dims
        first = (0, n0, n0 + n1 - 1, n0 + n1 + n2 - 2, n0 - 1)[dim]
        where = [pl.ds(0, self.dims[d]) if d in full else self.at[d] for d in range(3)]
        slot = lax.rem(g, SLOTS)
        z = self.at[0]
        if dim == RELAY:
            middle = (z == 1) | (z == 2)
            where[0] = jnp.where(z < 2, 3, 0)
            targets = [self.me + (3 - where[0] - z) * self.step[0]]
            guards = [(middle, jnp.logical_not(middle))]
        else:
            targets = self.peers(dim)
            guards = [(None, None)] * len(targets)
            if dim == 0 and self.relay:
                guards = [
                    (jnp.abs(lax.rem(z + d, 4) - z) != 3, jnp.abs(lax.rem(z + 4 - d, 4) - z) != 3)
                    if d != 2
                    else (None, None)
                    for d in (1, 2, 3)
                ]
        out = []
        for n, sub in enumerate(self.parts[s], sum(len(part) for part in self.parts[:s])):
            dst = self.buf.at[(g,) + tuple(where) + (self.core,) + sub]
            src = self.own.at[(g,) + sub] if p == 0 else dst
            for i, (to, guard) in enumerate(zip(targets, guards)):
                copy = pltpu.make_async_remote_copy(
                    src_ref=src,
                    dst_ref=dst,
                    send_sem=self.ssem.at[slot, n, first + i],
                    recv_sem=self.rsem.at[slot, n, first + i],
                    device_id=(to,),
                    device_id_type=MESH,
                )
                out.append((copy, *guard))
        return out

    def greet(self):
        bar = pltpu.get_barrier_semaphore()
        for d in range(4):
            for to in self.peers(d):
                pl.semaphore_signal(bar, inc=1, device_id=(to,), device_id_type=MESH)

    def meet(self):
        pl.semaphore_wait(pltpu.get_barrier_semaphore(), sum(self.dims) - 3 + 1)

    def pump(self, step):
        for p in range(self.phases, -1, -1):
            g = step - (DEPTH if p == self.phases else STARTS[p])

            @pl.when((g >= 0) & (g < self.total))
            def _():
                for s in range(len(self.orders)):
                    if p > 0:
                        for copy, sends, receives in self.moves(g, s, p - 1):
                            if sends is None:
                                copy.wait()
                            else:
                                pl.when(sends)(copy.wait_send)
                                pl.when(receives)(copy.wait_recv)
                    if p < self.phases:
                        for copy, sends, _ in self.moves(g, s, p):
                            if sends is None:
                                copy.start()
                            else:
                                pl.when(sends)(copy.start)


def matmul(left, right):
    return jnp.dot(left, right, preferred_element_type=jnp.float32)


def matmul_nt(left, right):
    return lax.dot_general(
        left, right, (((1,), (1,)), ((), ())), preferred_element_type=jnp.float32
    )


def matmul_tn(left, right):
    return lax.dot_general(
        left, right, (((0,), (0,)), ((), ())), preferred_element_type=jnp.float32
    )


def loop(count, body):
    lax.fori_loop(0, count, lambda i, c: (body(i), c)[1], 0)


def tile(i, size):
    return pl.ds(pl.multiple_of(i * size, size), size)


def window_starts(slots):
    return [
        min(max(b * BLOCK - (WINDOW - BLOCK) // 2, 0), slots - WINDOW)
        for b in range(slots // BLOCK)
    ]


def pair_stack(rows):
    lane = lax.broadcasted_iota(jnp.int32, rows.shape, 1)
    zero = jnp.zeros_like(rows)
    half = rows.shape[1] // 2
    return jnp.concatenate(
        [jnp.where(lane < half, rows, zero), jnp.where(lane < half, zero, rows)], axis=0
    )


def pair_join(stacked):
    rows = stacked.shape[0] // 2
    lane = lax.broadcasted_iota(jnp.int32, (rows, stacked.shape[1]), 1)
    return jnp.where(lane < stacked.shape[1] // 2, stacked[:rows], stacked[rows:])


def permute_hidden(load, store, unit, hidden):
    devices = hidden // (4 * unit)
    for b in range(hidden // 128):
        block = None
        for piece in range(128 // unit):
            quarter, device = divmod(b * (128 // unit) + piece, devices)
            source = (4 * device + quarter) * unit
            x = load(source // 128)
            shift = (piece * unit - source) % 128
            if shift:
                x = pltpu.roll(x, shift, axis=1)
            if block is None:
                block = x
            else:
                lane = lax.broadcasted_iota(jnp.int32, x.shape, 1)
                block = jnp.where(lane >= piece * unit, x, block)
        store(b, block)


def store_block(own, first, b, x):
    per = WIDTH // 128
    own[first + b // per, :, b % per * 128 : (b % per + 1) * 128] = x.astype(own.dtype)


def slot_ids(lengths, r, position):
    segments = lengths.shape[1]
    number = jnp.zeros_like(position)
    end = jnp.int32(0)
    for j in range(segments):
        end = end + lengths[r, j]
        number = number + (position >= end).astype(jnp.int32)
    return jnp.where(number < segments - 1, number, PADDING_ID + position)


def fold(x):
    rows, width = x.shape
    return jnp.sum(x.reshape(rows // 8, 8, width), axis=0)


def norm_back(up, xhat, scale, gain_row):
    scaled = up * gain_row
    m1 = jnp.mean(scaled, axis=1, keepdims=True)
    m2 = jnp.mean(scaled * xhat, axis=1, keepdims=True)
    return scale * (scaled - m1 - xhat * m2)


def forward_kernel(
    dims, devices_dims,
    lengths, *rest,
):
    matrices, rest = rest[:6], rest[6:]
    (tokens, cotangent), rest = rest[:2], rest[2:]
    vectors, rest = rest[:8], rest[8:]
    (
        inner_raw, wbuf, out, first_sums, saved_f, saved_qkv, saved_p, saved_x, saved_s, saved_d,
        h, a, qkv, o, z, u, w, p_stage, d_stage, x_stage, s_stage, own, id_row, id_col, inner_bias, cot,
        w_query, w_key, w_value, w_out, w_inner, w_outer, msem,
        wsem, psem, dsem, xsem, ssem, qsem, tsem, hsem, csem, send_sem, recv_sem,
    ) = rest
    rows, slots = dims
    count = h.shape[0]
    pairs = HEADS // 2
    total = LAYERS * GROUPS
    gather = Gather(devices_dims, own, wbuf, send_sem, recv_sem, total)

    def wload(g):
        slot = lax.rem(g, 2)
        return pltpu.make_async_copy(wbuf.at[g], w.at[slot], wsem.at[slot])

    def weights(g):
        @pl.when(g + 1 < total)
        def _():
            wload(g + 1).start()

        wload(g).wait()
        return w[lax.rem(g, 2)].reshape(h.shape[1], WIDTH)

    def pump(half):
        gather.pump(half + DEPTH)

    gather.greet()
    fetches = [
        pltpu.make_async_copy(source, target, msem.at[n])
        for n, (source, target) in enumerate(
            zip(matrices, (w_query, w_key, w_value, w_out, w_inner, w_outer))
        )
    ]
    for fetch in fetches:
        fetch.start()
    load = pltpu.make_async_copy(tokens, a, tsem)
    load.start()
    load_cot = pltpu.make_async_copy(cotangent, cot, csem)
    load_cot.start()
    unit = own.shape[1]

    def cast(l, m):
        matrix = (w_query, w_key, w_value, w_out)[m]
        for c in range(2):
            own[l * GROUPS + 2 * m + c] = matrix[l, :, tile(c, WIDTH)].astype(jnp.bfloat16)

    def here(first, count):
        blocks = pl.ds(first, count)
        return pltpu.make_async_copy(
            own.at[blocks], wbuf.at[(blocks,) + gather.at + (gather.core,)], hsem
        )

    def start(i):
        gather.pump(i)

    for m in range(4):
        fetches[m].wait()
        cast(0, m)
    here(0, AT_INNER).start()
    gather.meet()
    start(0)
    here(0, AT_INNER).wait()
    start(1)
    fetches[4].wait()
    fetches[5].wait()
    for l in range(LAYERS):
        at = l * GROUPS
        for m in range(4):
            if l > 0:
                cast(l, m)
        for c in range(2):
            for kc in range(4):
                piece = w_outer[l, kc * unit : (kc + 1) * unit, c * WIDTH : (c + 1) * WIDTH]
                own[at + AT_OUTER + 4 * c + kc] = piece.astype(jnp.bfloat16)
        permute_hidden(
            lambda b: w_inner[l, :, b * 128 : (b + 1) * 128],
            lambda b, x: store_block(own, at + AT_INNER, b, x),
            unit,
            w_inner.shape[2],
        )
        if l == 0:
            start(2)
    here(AT_INNER, total - AT_INNER).start()
    start(3)
    here(AT_INNER, total - AT_INNER).wait()

    def keep_bias(b, x):
        inner_bias[:, b * 128 : (b + 1) * 128] = x

    permute_hidden(
        lambda b: inner_raw[:, b * 128 : (b + 1) * 128], keep_bias, unit, w_inner.shape[2]
    )
    for r in range(rows):
        id_row[r] = slot_ids(lengths, r, lax.broadcasted_iota(jnp.int32, (8, slots), 1))
        id_col[r] = slot_ids(lengths, r, lax.broadcasted_iota(jnp.int32, (slots, 128), 0))
    first_sums[...] = jnp.zeros_like(first_sums)
    load_cot.wait()
    load.wait()

    def widen(i):
        h[tile(i, ROW_TILE), :] = a[tile(i, ROW_TILE), :].astype(jnp.float32)

    loop(count // ROW_TILE, widen)

    for i in range(4, DEPTH):
        start(i)
    pump(0)
    wload(0).start()

    def normalize(l, which):
        bias, gain, shift = ((B_OUT, G_ATTN, S_ATTN), (B_OUTER, G_FFN, S_FFN))[which]
        store_x = pltpu.make_async_copy(x_stage, saved_x.at[l, which], xsem)
        store_s = pltpu.make_async_copy(s_stage, saved_s.at[l, which], ssem)
        if which == 1:
            store_x.wait()
            store_s.wait()
        else:

            @pl.when(l > 0)
            def _():
                store_x.wait()
                store_s.wait()

        def body(i):
            t = tile(i, ROW_TILE)
            r = h[t, :] + vectors[bias][pl.ds(l, 1), :]
            centered = r - jnp.mean(r, axis=1, keepdims=True)
            var = jnp.mean(centered * centered, axis=1, keepdims=True)
            scale = lax.rsqrt(var + EPSILON)
            xhat = centered * scale
            x_stage[t, :] = xhat
            s_stage[t, :] = jnp.broadcast_to(scale, (ROW_TILE, 128))
            y = xhat * vectors[gain][pl.ds(l, 1), :] + vectors[shift][pl.ds(l, 1), :]
            h[t, :] = y
            a[t, :] = y.astype(jnp.bfloat16)
            if which == 1:

                @pl.when(l == LAYERS - 1)
                def _():
                    r = i // (slots // ROW_TILE)
                    real = slots - lengths[r, lengths.shape[1] - 1]
                    slot = lax.rem(i * ROW_TILE, slots) + lax.broadcasted_iota(
                        jnp.int32, (ROW_TILE, h.shape[1]), 0
                    )
                    up = jnp.where(slot < real, cot[t, :].astype(jnp.float32), 0.0)
                    down = norm_back(up, xhat, scale, vectors[gain][pl.ds(l, 1), :])
                    x_stage[t, :] = down
                    low = down.astype(jnp.bfloat16)
                    cot[t, :] = low
                    first_sums[0] += fold(up)
                    first_sums[1] += fold(low.astype(jnp.float32))

        loop(count // ROW_TILE, body)
        store_x.start()
        store_s.start()

    def layer(l):
        base = l * GROUPS

        @pl.when(l > 0)
        def _():
            for m in range(3):
                pltpu.make_async_copy(qkv.at[m], saved_qkv.at[l, m], qsem.at[m]).wait()

        def project(i):
            pump(base + i + 1)
            m = i // 2
            cols = tile(i % 2, WIDTH)
            bias_q = vectors[B_Q][pl.ds(l, 1), cols]
            bias_v = vectors[B_V][pl.ds(l, 1), cols]
            bias = jnp.where(m == 0, bias_q, jnp.where(m == 1, jnp.zeros_like(bias_v), bias_v))
            y = matmul(a[...], weights(base + i)) + bias
            y = y * jnp.where(m == 0, jnp.float32((h.shape[1] // HEADS) ** -0.5), jnp.float32(1))
            qkv[m, :, cols] = y.astype(jnp.bfloat16)

        loop(6, project)
        for m in range(3):
            pltpu.make_async_copy(qkv.at[m], saved_qkv.at[l, m], qsem.at[m]).start()

        def attend(i):
            @pl.when((lax.rem(i, 3) == 1) & (i < 15))
            def _():
                pump(base + 7 + i // 3)


            r = i // pairs
            lanes = tile(lax.rem(i, pairs), 128)
            slot = lax.rem(i, 2)
            store_p = pltpu.make_async_copy(p_stage.at[slot], saved_p.at[l, i], psem.at[slot])

            @pl.when((i >= 2) | (l > 0))
            def _():
                store_p.wait()

            top = pl.multiple_of(r * slots, slots)
            starts = window_starts(slots)
            scores = [
                matmul_nt(
                    qkv[1, pl.ds(top + start, WINDOW), lanes],
                    pair_stack(qkv[0, pl.ds(top + b * BLOCK, BLOCK), lanes]),
                )
                for b, start in enumerate(starts)
            ]
            for b, start in enumerate(starts):
                vm = qkv[2, pl.ds(top + start, WINDOW), lanes]
                same = id_col[r, start : start + WINDOW, :] == id_row[r, :1, b * BLOCK : (b + 1) * BLOCK]
                s = jnp.where(jnp.concatenate([same, same], axis=1), scores[b], NEGATIVE)
                e = jnp.exp(s - jnp.max(s, axis=0, keepdims=True))
                p = e * (1.0 / jnp.sum(e, axis=0, keepdims=True))
                p = p.astype(jnp.bfloat16)
                p_stage[slot, b] = p
                o[pl.ds(top + b * BLOCK, BLOCK), lanes] = pair_join(matmul_tn(p, vm)).astype(jnp.bfloat16)
            store_p.start()

        loop(rows * pairs, attend)

        def attn_out(i):
            @pl.when(i == 1)
            def _():
                pump(base + 12)

            cols = tile(i, WIDTH)
            h[:, cols] += matmul(o[...], weights(base + AT_OUT + i))

        loop(2, attn_out)
        normalize(l, 0)

        def inner(i):
            @pl.when(i != 3)
            def _():
                pump(base + 13 + i - i // 4)


            cols = tile(i, WIDTH)
            u[...] = matmul(a[...], weights(base + AT_INNER + i)) + inner_bias[pl.ds(l, 1), cols]
            slot = lax.rem(i, 2)
            store_d = pltpu.make_async_copy(d_stage.at[slot], saved_d.at[l, i], dsem.at[slot])

            @pl.when((i >= 2) | (l > 0))
            def _():
                store_d.wait()

            def activate(t):
                part = tile(t, ROW_TILE)
                x = u[part, :]
                cdf = 0.5 + 0.5 * lax.erf(x * ROOT_HALF)
                z[i // 2, part, tile(i % 2, WIDTH)] = (x * cdf).astype(jnp.bfloat16)
                slope = cdf + x * (DENSITY * jnp.exp(-0.5 * x * x))
                d_stage[slot, part, :] = slope.astype(jnp.bfloat16)

            loop(count // ROW_TILE, activate)
            store_d.start()

        loop(8, inner)

        def outer(i):
            @pl.when(i == 0)
            def _():
                pump(base + 20)

            @pl.when(i == 1)
            def _():
                pump(base + 21)

            @pl.when(i == 3)
            def _():
                pump(base + 22)

            @pl.when(i == 5)
            def _():
                pump(base + 23)

            @pl.when(i == 7)
            def _():
                pump(base + 24)


            cols = tile(i // 4, WIDTH)
            h[:, cols] += matmul(z[lax.rem(i, 4)], weights(base + AT_OUTER + i))

        loop(8, outer)
        normalize(l, 1)

    loop(LAYERS, layer)
    store = pltpu.make_async_copy(a, out, tsem)
    store.start()
    store_f = pltpu.make_async_copy(cot, saved_f, csem)
    store_f.start()
    last = LAYERS - 1
    for m in range(3):
        pltpu.make_async_copy(qkv.at[m], saved_qkv.at[last, m], qsem.at[m]).wait()
    for i in range(2):
        pltpu.make_async_copy(p_stage.at[i], saved_p.at[last, i], psem.at[i]).wait()
        pltpu.make_async_copy(d_stage.at[i], saved_d.at[last, i], dsem.at[i]).wait()
    pltpu.make_async_copy(x_stage, saved_x.at[last, 1], xsem).wait()
    pltpu.make_async_copy(s_stage, saved_s.at[last, 1], ssem).wait()
    store.wait()
    store_f.wait()


def forward(devices, lengths, matrices, tokens, cotangent, vectors, inner_bias, rows, slots):
    count, width = tokens.shape
    hidden = inner_bias.shape[-1]
    unit = matrices[0].shape[1]
    bf, f32 = jnp.bfloat16, jnp.float32
    blocks = slots // BLOCK
    devices_dims = chip_dims(devices)
    held = devices_dims + (2, unit, WIDTH)
    sems = sum(devices_dims) - 1
    any_ = pl.BlockSpec(memory_space=HBM)
    vm = pl.BlockSpec(memory_space=VMEM)
    return pl.pallas_call(
        functools.partial(forward_kernel, (rows, slots), devices_dims),
        out_shape=(
            jax.ShapeDtypeStruct((LAYERS * GROUPS,) + held, bf),
            jax.ShapeDtypeStruct((count, width), bf),
            jax.ShapeDtypeStruct((2, 8, width), f32),
            jax.ShapeDtypeStruct((count, width), bf),
            jax.ShapeDtypeStruct((LAYERS, 3, count, width), bf),
            jax.ShapeDtypeStruct((LAYERS, rows * HEADS // 2, blocks, WINDOW, 2 * BLOCK), bf),
            jax.ShapeDtypeStruct((LAYERS, 2, count, width), f32),
            jax.ShapeDtypeStruct((LAYERS, 2, count, 128), f32),
            jax.ShapeDtypeStruct((LAYERS, hidden // WIDTH, count, WIDTH), bf),
        ),
        in_specs=[pl.BlockSpec(memory_space=pltpu.SMEM)] + [any_] * 8 + [vm] * 9,
        out_specs=(any_, any_, vm) + (any_,) * 6,
        scratch_shapes=[
            VMEM((count, width), f32),
            VMEM((count, width), bf),
            VMEM((3, count, width), bf),
            VMEM((count, width), bf),
            VMEM((hidden // width, count, width), bf),
            VMEM((count, WIDTH), f32),
            VMEM((2,) + held, bf),
            VMEM((2, blocks, WINDOW, 2 * BLOCK), bf),
            VMEM((2, count, WIDTH), bf),
            VMEM((count, width), f32),
            VMEM((count, 128), f32),
            VMEM((LAYERS * GROUPS, unit, WIDTH), bf),
            VMEM((rows, 8, slots), jnp.int32),
            VMEM((rows, slots, 128), jnp.int32),
            VMEM((LAYERS, hidden), f32),
            VMEM((count, width), bf),
            *(VMEM(m.shape, f32) for m in matrices),
            DMA((6,)),
            DMA((2,)), DMA((2,)), DMA((2,)), DMA, DMA, DMA((3,)), DMA, DMA, DMA,
            DMA((SLOTS, 6, sems)), DMA((SLOTS, 6, sems)),
        ],
        compiler_params=pltpu.CompilerParams(
            vmem_limit_bytes=58 << 20, collective_id=0, has_side_effects=True
        ),
    )(lengths, *matrices, tokens, cotangent, *vectors, inner_bias)


def digits(devices):
    out, stride = [], 1
    while stride < devices:
        size = 2 if stride == 1 else min(4, devices // stride)
        out.append((stride, size))
        stride *= size
    return out


class Exchange:
    def __init__(self, me, places, held, got, ssem, rsem):
        self.me, self.places = me, places
        self.held, self.got, self.ssem, self.rsem = held, got, ssem, rsem

    def copies(self, k):
        stride, size = self.places[k]
        digit = lax.rem(self.me // stride, size)
        out = []
        for d in range(1, size):
            to = self.me + (lax.rem(digit + d, size) - digit) * stride
            out.append(
                pltpu.make_async_remote_copy(
                    src_ref=self.held.at[k],
                    dst_ref=self.got.at[k, digit],
                    send_sem=self.ssem.at[k, d],
                    recv_sem=self.rsem.at[k, d],
                    device_id=(to,),
                    device_id_type=MESH,
                )
            )
        return out, digit, size

    def step(self, k):
        if k > 0:
            copies, digit, size = self.copies(k - 1)
            for c in copies:
                c.wait()
            self.got[k - 1, digit] = self.held[k - 1]
            total = self.got[k - 1, 0]
            for j in range(1, size):
                total = total + self.got[k - 1, j]
            self.held[k] = total
        if k < len(self.places):
            for c in self.copies(k)[0]:
                c.start()


def backward_kernel(
    dims, places,
    wbuf, gain_attn, gain_ffn, first_sums, saved_f, saved_qkv, saved_p, saved_x, saved_s, saved_d,
    grad, sums, late_sums,
    g, db, du, qkv, dqkv, x, sc, d, w, p, dk, dv, part, late,
    held, got, late_held, late_got,
    wsem, psem, dsem, xsem, ssem, qsem, csem, gsem, send_sem, recv_sem, late_send, late_recv,
):
    rows, slots = dims
    count, width = g.shape
    pairs = HEADS // 2
    per_layer = GROUPS // 2
    total = LAYERS * per_layer
    items = rows * pairs
    steps = len(places)
    chunk = 256
    chunks = [slice(c * chunk, (c + 1) * chunk) for c in range(width // chunk)]

    def wload(i):
        l = LAYERS - 1 - i // per_layer
        j = lax.rem(i, per_layer)
        outer = (j < 8) & (lax.rem(j, 2) == 0)
        ffn = jnp.where(outer, AT_OUTER + j // 2, AT_INNER + j // 2 * 2)
        block = l * GROUPS + jnp.where(j < 8, ffn, jnp.where(j == 8, AT_OUT, 2 * (j - 9)))
        slot = lax.rem(i, 3)
        apart = jnp.where(outer, 4, 1)
        return [
            pltpu.make_async_copy(wbuf.at[block + c * apart], w.at[slot, c], wsem.at[slot, c])
            for c in range(2)
        ]

    def weights(i):
        @pl.when(i + 2 < total)
        def _():
            for c in wload(i + 2):
                c.start()

        for c in wload(i):
            c.wait()
        return lax.rem(i, 3)

    def product(left, slot, n):
        return matmul_nt(left[:, :WIDTH], w[slot, 0, n, :]) + matmul_nt(left[:, WIDTH:], w[slot, 1, n, :])

    def xload(l, which):
        return (
            pltpu.make_async_copy(saved_x.at[l, which], x.at[which], xsem.at[which]),
            pltpu.make_async_copy(saved_s.at[l, which], sc.at[which], ssem.at[which]),
        )

    def dload(l, quarter):
        slot = lax.rem(quarter, 2)
        return pltpu.make_async_copy(saved_d.at[l, pl.ds(2 * quarter, 2)], d.at[slot], dsem.at[slot])

    def pload(l, i):
        slot = lax.rem(i, 3)
        return pltpu.make_async_copy(saved_p.at[l, i], p.at[slot], psem.at[slot])

    def qload(l):
        return [pltpu.make_async_copy(saved_qkv.at[l, m], qkv.at[m], qsem.at[m]) for m in range(3)]

    top_layer = LAYERS - 1
    opening = [
        pltpu.make_async_copy(saved_f, db, csem.at[0]),
        pltpu.make_async_copy(saved_x.at[top_layer, 1], g, csem.at[1]),
    ]
    opening[0].start()
    for c in wload(0):
        c.start()
    dload(top_layer, 0).start()
    for c in wload(1):
        c.start()
    opening[1].start()
    for c in xload(top_layer, 0):
        c.start()
    if top_layer:
        for c in xload(top_layer - 1, 1):
            c.start()
    me = lax.axis_index("dp")
    if steps:
        barrier = pltpu.get_barrier_semaphore()
        for stride, size in places:
            digit = lax.rem(me // stride, size)
            for k in range(1, size):
                to = me + (lax.rem(digit + k, size) - digit) * stride
                pl.semaphore_signal(barrier, inc=1, device_id=(to,), device_id_type=MESH)
    for c in opening:
        c.wait()
    part[D_FFN] = first_sums[0]
    part[D_OUTER] = first_sums[1]
    if steps:
        pl.semaphore_wait(barrier, sum(size - 1 for _, size in places))

    def normalize_back(l, which):
        gain = (gain_attn, gain_ffn)[which]
        row_shift = (D_ATTN, D_FFN)[which]
        row_bias = (D_OUT, D_OUTER)[which]
        for c in xload(l, which):
            c.wait()

        def body(i, carry):
            t = tile(i, ROW_TILE)
            up = g[t, :]
            xh = x[which, t, :]
            down = norm_back(up, xh, sc[which, t, :1], gain[pl.ds(l, 1), :])
            g[t, :] = down
            low = down.astype(jnp.bfloat16)
            db[t, :] = low
            return carry[0] + fold(up), carry[1] + fold(low.astype(jnp.float32))

        zero = jnp.zeros((8, width), jnp.float32)
        shift_sum, bias_sum = lax.fori_loop(0, count // ROW_TILE, body, (zero, zero))
        part[row_shift] = shift_sum
        part[row_bias] = bias_sum

        @pl.when(l > 0)
        def _():
            for c in xload(l - 1, which):
                c.start()

    last_sums = Exchange(me, places, late_held, late_got, late_send, late_recv)

    def layer(step):
        l = top_layer - step
        base = step * per_layer

        @pl.when(step > 0)
        def _():
            normalize_back(l, 1)

        def quarter(kc):
            @pl.when(kc + 1 < 4)
            def _():
                dload(l, kc + 1).start()

            @pl.when(kc == 1)
            def _():
                for c in qload(l):
                    c.start()

            slot = weights(base + 2 * kc)
            dload(l, kc).wait()
            for c, n in enumerate(chunks):
                within = slice(c * chunk % WIDTH, c * chunk % WIDTH + chunk)
                slope = d[lax.rem(kc, 2), c * chunk // WIDTH, :, within].astype(jnp.float32)
                low = (product(db, slot, n) * slope).astype(jnp.bfloat16)
                du[:, n] = low
                part[D_INNER + kc, :, n] = fold(low.astype(jnp.float32))
            slot = weights(base + 2 * kc + 1)
            for n in chunks:
                g[:, n] += product(du, slot, n)

        loop(4, quarter)

        @pl.when(l > 0)
        def _():
            dload(l - 1, 0).start()

        pload(l, 0).start()
        pload(l, 1).start()
        normalize_back(l, 0)
        slot = weights(base + 8)
        for n in chunks:
            du[:, n] = product(db, slot, n).astype(jnp.bfloat16)
        for c in qload(l):
            c.wait()
        early = Exchange(me, places, held.at[l], got.at[l], send_sem.at[l], recv_sem.at[l])
        held[l, 0] = jnp.sum(part[...], axis=1)
        early.step(0)

        def attend(i):
            for k in range(1, steps + 1):

                @pl.when(i == (items - 1) // steps * k)
                def _():
                    early.step(k)

            r = i // pairs
            lanes = tile(lax.rem(i, pairs), 128)
            slot = lax.rem(i, 3)

            @pl.when(i + 2 < items)
            def _():
                pload(l, i + 2).start()

            pload(l, i).wait()
            dk[...] = jnp.zeros_like(dk)
            dv[...] = jnp.zeros_like(dv)
            top = pl.multiple_of(r * slots, slots)
            starts = window_starts(slots)
            mine = [pl.ds(top + b * BLOCK, BLOCK) for b in range(len(starts))]
            reach = [pl.ds(top + start, WINDOW) for start in starts]
            stacked = [pair_stack(du[rows_, lanes]) for rows_ in mine]
            dps = [matmul_nt(qkv[2, keys, lanes], om) for keys, om in zip(reach, stacked)]
            for b, start in enumerate(starts):
                qm = pair_stack(qkv[0, mine[b], lanes])
                pb = p[slot, b]
                pf = pb.astype(jnp.float32)
                weighted = pf * dps[b]
                ds = weighted - pf * jnp.sum(weighted, axis=0, keepdims=True)
                ds = ds.astype(jnp.bfloat16)
                dk[start : start + WINDOW, :] += matmul(ds, qm)
                dv[start : start + WINDOW, :] += matmul(pb, stacked[b])
                dq = pair_join(matmul_tn(ds, qkv[1, reach[b], lanes]))
                dqkv[0, mine[b], lanes] = (dq * (width // HEADS) ** -0.5).astype(jnp.bfloat16)
            every = pl.ds(top, slots)
            dqkv[1, every, lanes] = dk[...].astype(jnp.bfloat16)
            dqkv[2, every, lanes] = dv[...].astype(jnp.bfloat16)

        loop(items, attend)
        sums[l] = held[l, steps]
        for m, row in ((0, 0), (2, 1)):

            def add(t, carry):
                return carry + fold(dqkv[m, tile(t, ROW_TILE), :].astype(jnp.float32))

            late[2 * l + row] = lax.fori_loop(
                0, count // ROW_TILE, add, jnp.zeros((8, width), jnp.float32)
            )

        @pl.when(l == 0)
        def _():
            late_held[0] = jnp.sum(late[...], axis=1)
            last_sums.step(0)

        for m in range(3):
            slot = weights(base + 9 + m)
            for c, n in enumerate(chunks):
                g[:, n] += product(dqkv.at[m], slot, n)
                if m == 2:

                    @pl.when(l == 0)
                    def _():
                        pltpu.make_async_copy(g.at[:, n], grad.at[:, n], gsem.at[c]).start()

            if m + 1 < steps:

                @pl.when(l == 0)
                def _():
                    last_sums.step(m + 1)

    late[...] = jnp.zeros_like(late)
    loop(LAYERS, layer)
    for k in range(min(steps, 3), steps + 1):
        if k > 0:
            last_sums.step(k)
    late_sums[...] = late_held[steps]
    for c, n in enumerate(chunks):
        pltpu.make_async_copy(g.at[:, n], grad.at[:, n], gsem.at[c]).wait()


def backward(devices, wbuf, gain_attn, gain_ffn, first_sums, saved, rows, slots):
    count, width = saved[0].shape
    bf, f32 = jnp.bfloat16, jnp.float32
    blocks = slots // BLOCK
    places = digits(devices)
    steps = max(len(places), 1)
    any_ = pl.BlockSpec(memory_space=HBM)
    vm = pl.BlockSpec(memory_space=VMEM)
    return pl.pallas_call(
        functools.partial(backward_kernel, (rows, slots), places),
        out_shape=(
            jax.ShapeDtypeStruct((count, width), f32),
            jax.ShapeDtypeStruct((LAYERS, EARLY, width), f32),
            jax.ShapeDtypeStruct((8, width), f32),
        ),
        in_specs=[any_, vm, vm, vm] + [any_] * 6,
        out_specs=(any_, vm, vm),
        scratch_shapes=[
            VMEM((count, width), f32),
            VMEM((count, width), bf),
            VMEM((count, width), bf),
            VMEM((3, count, width), bf),
            VMEM((3, count, width), bf),
            VMEM((2, count, width), f32),
            VMEM((2, count, 128), f32),
            VMEM((2, 2, count, WIDTH), bf),
            VMEM((3, 2, width, WIDTH), bf),
            VMEM((3, blocks, WINDOW, 2 * BLOCK), bf),
            VMEM((slots, 128), f32),
            VMEM((slots, 128), f32),
            VMEM((EARLY, 8, width), f32),
            VMEM((8, 8, width), f32),
            VMEM((LAYERS, steps + 1, EARLY, width), f32),
            VMEM((LAYERS, steps, 4, EARLY, width), f32),
            VMEM((steps + 1, 8, width), f32),
            VMEM((steps, 4, 8, width), f32),
            DMA((3, 2)), DMA((3,)), DMA((2,)), DMA((2,)), DMA((2,)), DMA((3,)), DMA((2,)), DMA((4,)),
            DMA((LAYERS, steps, 4)), DMA((LAYERS, steps, 4)), DMA((steps, 4)), DMA((steps, 4)),
        ],
        compiler_params=pltpu.CompilerParams(
            vmem_limit_bytes=60 << 20,
            **({"collective_id": 1, "has_side_effects": True} if places else {}),
        ),
    )(wbuf, gain_attn, gain_ffn, first_sums, *saved)


def finish_kernel(
    unit,
    sums, late, grad_in, result_in,
    grad, result, query, value, out, inner, outer, attn, ffn,
    grad_hold, result_hold, load_sem, store_sem,
):
    count, width = grad.shape
    part = count // 4
    moves = []
    for c in range(4):
        for n, (source, hold, target) in enumerate(
            ((result_in, result_hold, result), (grad_in, grad_hold, grad))
        ):
            rows_ = pl.ds(c * part, part)
            load = pltpu.make_async_copy(source.at[rows_], hold.at[rows_], load_sem.at[n, c])
            store = pltpu.make_async_copy(hold.at[rows_], target.at[rows_], store_sem.at[n, c])
            load.start()
            moves.append((load, store))
    for load, store in moves:
        load.wait()
        store.start()
    devices = width // unit
    for l in range(LAYERS):
        here = slice(l, l + 1)
        for row, ref in ((D_OUT, out), (D_OUTER, outer), (D_ATTN, attn), (D_FFN, ffn)):
            ref[here, :] = sums[l, row : row + 1, :]
        query[here, :] = late[2 * l : 2 * l + 1, :]
        value[here, :] = late[2 * l + 1 : 2 * l + 2, :]
        for b in range(inner.shape[1] // 128):
            block = None
            for piece in range(128 // unit):
                device, quarter = divmod(b * (128 // unit) + piece, inner.shape[1] // width)
                source = device * unit
                row = D_INNER + quarter
                first = source // 128 * 128
                x = sums[l, row : row + 1, first : first + 128]
                shift = (piece * unit - source) % 128
                if shift:
                    x = pltpu.roll(x, shift, axis=1)
                if block is None:
                    block = x
                else:
                    lane = lax.broadcasted_iota(jnp.int32, x.shape, 1)
                    block = jnp.where(lane >= piece * unit, x, block)
            inner[here, b * 128 : (b + 1) * 128] = block
    for _, store in moves:
        store.wait()


def finish(unit, hidden, sums, late, grad, result):
    width = sums.shape[2]
    vm = pl.BlockSpec(memory_space=VMEM)
    any_ = pl.BlockSpec(memory_space=HBM)
    sizes = (width, width, width, hidden, width, width, width)
    large = tuple(jax.ShapeDtypeStruct(x.shape, x.dtype) for x in (grad, result))
    return pl.pallas_call(
        functools.partial(finish_kernel, unit),
        out_shape=large + tuple(jax.ShapeDtypeStruct((LAYERS, n), jnp.float32) for n in sizes),
        in_specs=[vm, vm, any_, any_],
        out_specs=(any_, any_) + (vm,) * 7,
        scratch_shapes=[
            VMEM(grad.shape, grad.dtype),
            VMEM(result.shape, result.dtype),
            DMA((2, 4)),
            DMA((2, 4)),
        ],
    )(sums, late, grad, result)


def per_device(
    devices,
    tokens,
    lengths,
    w_query,
    w_key,
    w_value,
    w_out,
    w_inner,
    w_outer,
    bias_query,
    bias_value,
    bias_out,
    bias_inner,
    bias_outer,
    shift_attn,
    shift_ffn,
    gain_attn,
    gain_ffn,
    cotangent,
):
    rows, slots, width = tokens.shape
    hidden = bias_inner.shape[1]
    unit = w_query.shape[1]
    count = rows * slots
    vectors = (
        bias_query, bias_value, bias_out, bias_outer, shift_attn, shift_ffn, gain_attn, gain_ffn,
    )
    matrices = (w_query, w_key, w_value, w_out, w_inner, w_outer)
    wbuf, out, first_sums, *saved = forward(
        devices, lengths, matrices, tokens.reshape(count, width), cotangent.reshape(count, width),
        vectors, bias_inner, rows, slots,
    )
    wbuf = wbuf.reshape(LAYERS * GROUPS, width, WIDTH)
    grad, sums, late = backward(
        devices, wbuf, gain_attn, gain_ffn, first_sums, saved, rows, slots
    )
    grad, out, *small = finish(unit, hidden, sums, late, grad, out)
    return (out.reshape(rows, slots, width), grad.reshape(rows, slots, width), *small)


def solution(mesh):
    rows, whole = P("dp", None, None), P()
    weight = P(None, "dp", None)
    placed = (rows, P("dp", None)) + (weight,) * 6 + (whole,) * 9 + (rows,)
    return jax.shard_map(
        functools.partial(per_device, mesh.shape["dp"]),
        mesh=mesh,
        in_specs=placed,
        out_specs=(rows, rows) + (whole,) * 7,
        check_vma=False,
    )
```
